256 devices in a mesh: mem: 32 (over x, z_hi, core), gx: 4 (over y), gy: 2 (over z_lo).
Axes of the slice: x: 4, y: 4, z: 8 (z_hi: 4, z_lo: 2; z = z_hi * 2 + z_lo), core: 2. Of those that a mesh axis runs over, the one named last changes fastest.
Arguments:
- perturbations: float32 [32, 32, 128, 512], P('mem', None, 'gx', 'gy'), may hold values from -9 to 9
- control: float32 [32, 128, 512], P(None, 'gx', 'gy'), may hold values from -6 to 6
Outputs:
- increment: float32 [32, 128, 512], P('mem', 'gx', 'gy')
The draws below stay inside these ranges and needn't reach their ends.
All inputs are finite; a program needn't handle non-finite values.
Results may differ from the reference program's by a relative error of at most 0.0001.
Values sent between devices are 32-bit elements; how exact they have to be, the bound alone decides.
No kernel may reach another device: no remote copies, remote signals or barrier semaphores. Data moves between devices by JAX's collectives and lax.ppermute only.
A program may use at most 64 MiB of HBM per device.

```python
import jax
import jax.numpy as jnp
from jax import lax

FIELDS = 32
MEMBERS = 32
NX = 128
NY = 512


def spiked(array, stream_key, source, target, blocks, factor):
    def block_of(position):
        return (jnp.arange(array.shape[position]) // (array.shape[position] // blocks)).reshape((-1,) + (1,) * (array.ndim - 1 - position))

    first = jax.random.permutation(stream_key, blocks)[block_of(target)]
    far = (block_of(target) + blocks // 2) % blocks
    return jnp.where((block_of(source) == first) | (block_of(source) == far), factor * array, array)


def levels(key, shape, pieces, low, top_value):
    loudness, own = 1.0, jax.random.fold_in(key, 6)
    for axis_at, blocks in pieces:
        heights = jnp.exp(jax.random.uniform(jax.random.fold_in(own, axis_at), (blocks,), jnp.float32, low / len(pieces), top_value / len(pieces)))
        loudness = loudness * jnp.repeat(heights, shape[axis_at] // blocks).reshape([-1 if axis == axis_at else 1 for axis in range(len(shape))])
    return loudness


def gaussian(key, shape, deviation, reach, pieces=(), dtype=jnp.bfloat16):
    drawn = jax.random.normal(key, shape, jnp.float32) * deviation
    if len(pieces) > 0:
        drawn = levels(key, shape, pieces, -0.22, 0.18) * drawn
    return jnp.clip(drawn, min=-reach, max=reach).astype(dtype)


def heavy_noise(key, dims, deviation, limit, pieces, heavy, kind=jnp.bfloat16):
    array = deviation * jax.random.normal(key, dims, jnp.float32)
    if pieces:
        array = array * levels(key, dims, pieces, -0.22, 0.18)
    return jnp.clip(spiked(array, jax.random.fold_in(key, 3), *heavy), -limit, limit).astype(kind)


def setup_inputs(seed: int = 0) -> dict:
    splits = jax.random.split(jax.random.key(seed), 3)
    return {
        "perturbations": heavy_noise(splits[0], (MEMBERS, FIELDS, NX, NY), 1.5, 9.0, ((0, 32), (2, 4), (3, 2)), (0, 1, 32, 2.75), jnp.float32),
        "control": gaussian(splits[1], (FIELDS, NX, NY), 1.0, 6.0, ((1, 4), (2, 2)), jnp.float32),
    }


def tap_weights():
    offsets = jnp.arange(-4, 5).astype(jnp.float32)
    raw_taps = jnp.exp(-offsets * offsets / 18.0)
    return raw_taps / jnp.sqrt(jnp.sum(raw_taps * raw_taps))

def smooth(values):
    weights = tap_weights()
    count_x, count_y = (values.shape[-2], values.shape[-1])
    widths = [(0, 0)] * (values.ndim - 2) + [(4, 4), (4, 4)]
    padded = jnp.pad(values, widths)
    along_x = sum((weights[offset] * padded[..., offset:offset + count_x, :] for offset in range(9)))
    return sum((weights[offset] * along_x[..., offset:offset + count_y] for offset in range(9)))

def restrict(values):
    shape_now = values.shape
    blocks = values.reshape(shape_now[:-2] + (shape_now[-2] // 2, 2, shape_now[-1] // 2, 2))
    return 0.5 * lax.optimization_barrier(jnp.sum(blocks, axis=(-3, -1)))

def prolong(coarse):
    return 0.5 * jnp.repeat(jnp.repeat(coarse, 2, axis=-2), 2, axis=-1)

def localize(values):
    return smooth(values) + prolong(smooth(restrict(values)))

def reference(perturbations, control):

    def add_member(running, member_field):
        alpha = localize(localize(member_field * control))
        return (running + member_field * alpha, None)
    running, unused = lax.scan(add_member, jnp.zeros(control.shape, jnp.float32), perturbations)
    return running / (MEMBERS - 1)
```

```python
import jax
import jax.numpy as jnp
import numpy as np
from jax import lax
from jax.experimental import pallas as pl
from jax.experimental.pallas import tpu as pltpu
from jax.sharding import PartitionSpec as P

F32, BF16 = jnp.float32, jnp.bfloat16
HALO = 16
VMEM = pl.BlockSpec(memory_space=pltpu.VMEM)


def line_terms(size):
    offsets = np.arange(-4, 5)
    taps = np.exp(-offsets * offsets / 18.0)
    taps = taps / np.sqrt(np.sum(taps * taps))

    def banded(count):
        return sum(t * np.eye(count, k=o) for t, o in zip(taps, offsets))

    pairs = np.repeat(np.eye(size // 2), 2, axis=1) * np.sqrt(0.5)
    return banded(size), pairs.T @ banded(size // 2) @ pairs


def split(values):
    high = values.astype(BF16)
    return high, (values - high.astype(values.dtype)).astype(BF16)


def left_table(size, parts):
    fine, pair = line_terms(size)
    rows = size // parts
    tables = []
    for part in range(parts):
        terms = []
        for term in (fine @ fine, fine @ pair, pair @ fine, pair @ pair):
            wide = np.zeros((rows, rows + 2 * HALO))
            for e in range(rows + 2 * HALO):
                source = part * rows - HALO + e
                if 0 <= source < size:
                    wide[:, e] = term[part * rows : (part + 1) * rows, source]
            segments = wide.reshape(rows, 4, 1, HALO)
            terms.append(np.broadcast_to(segments, (rows, 4, 4, HALO)).reshape(rows, 256))
        tables.append(np.concatenate(terms))
    return np.stack(tables)


def right_table(size, parts):
    fine, pair = line_terms(size)
    columns = size // parts
    tables = []
    for part in range(parts):
        own = slice(part * columns, (part + 1) * columns)
        edge = slice(columns, columns + HALO) if part == 0 else slice(columns - HALO, columns)
        terms = (fine @ fine, pair @ fine, fine @ pair, pair @ pair)
        rows = [term[own, own] for term in terms] + [term[edge, own] for term in terms]
        rows.append(np.zeros((64, columns)))
        tables.append(np.concatenate(rows))
    return np.stack(tables)


def halves(table):
    high = table.astype(np.float32).astype(BF16)
    low = (table - high.astype(np.float64)).astype(np.float32).astype(BF16)
    return np.stack([high, low], axis=1)


def dot3(left, right):
    (lh, ll), (rh, rl) = left, right
    dot = lambda a, b: jnp.dot(a, b, preferred_element_type=F32)
    return dot(lh, rh) + (dot(lh, rl) + dot(ll, rh))


def product_kernel(where, p_ref, c_ref, top_ref, bottom_ref, edge_top_ref, edge_bottom_ref):
    gy = where[4]
    lane = lax.broadcasted_iota(jnp.int32, (1, 1, 128), 2)
    edges = jnp.zeros((4, 32, 128), F32)
    for g in range(8):
        v = p_ref[0, 4 * g : 4 * g + 4] * c_ref[4 * g : 4 * g + 4]
        top_ref[4 * g : 4 * g + 4] = v[:, :HALO]
        bottom_ref[4 * g : 4 * g + 4] = v[:, HALO:]
        last = v[:, :, 128:].reshape(128, 128)
        first = v[:, :, :128].reshape(128, 128)
        edge = jnp.where(gy == 0, pltpu.roll(last, 16, 1), first)
        if g:
            edge = pltpu.roll(edge, 16 * g, 1)
        edges = jnp.where(lane // 16 == g, edge.reshape(4, 32, 128), edges)
    edge_top_ref[...] = edges[:, :HALO]
    edge_bottom_ref[...] = edges[:, HALO:]


def filter_kernel(
    where, p_ref, above_ref, top_ref, bottom_ref, below_ref,
    side_above_ref, side_top_ref, side_bottom_ref, side_below_ref,
    left_ref, right_ref, keep_ref, send_ref, xh_ref, xl_ref, sh_ref, sl_ref,
):
    core, gx, gy = where[2], where[3], where[4]
    lane = lax.broadcasted_iota(jnp.int32, (1, 256), 1)
    for t in range(4):
        for f in range(4):
            mine = (lane // 16) % 4 == f
            rows = slice(32 * t, 32 * t + 32)
            at = slice(128 * t + 32 * f, 128 * t + 32 * f + 32)
            zero = jnp.zeros((32, 256), F32)
            xh_ref[at] = jnp.where(mine, left_ref[gx, 0, rows].astype(F32), zero).astype(BF16)
            xl_ref[at] = jnp.where(mine, left_ref[gx, 1, rows].astype(F32), zero).astype(BF16)
    left = (xh_ref[...], xl_ref[...])

    sides = [r[...].reshape(64, 128) for r in (side_above_ref, side_top_ref, side_bottom_ref, side_below_ref)]
    side = dot3(left, split(jnp.concatenate(sides)))
    narrow = lax.broadcasted_iota(jnp.int32, (1, 128), 1)
    for g in range(8):
        packed = jnp.zeros((128, 128), F32)
        for t in range(4):
            moved = side[128 * t : 128 * t + 128]
            if t != g:
                moved = pltpu.roll(moved, (16 * (t - g)) % 128, 1)
            packed = jnp.where(narrow // 16 == t, moved, packed)
        sh_ref[g], sl_ref[g] = split(packed)

    def group(g, carry):
        fields = pl.ds(4 * g, 4)
        v = [r[fields].reshape(64, 256) for r in (above_ref, top_ref, bottom_ref, below_ref)]
        u = dot3((xh_ref[...], xl_ref[...]), split(jnp.concatenate(v)))
        parts = [split(u[128 * t : 128 * t + 128]) for t in range(4)]
        uh = jnp.concatenate([h for h, _ in parts] + [sh_ref[g]], axis=1)
        ul = jnp.concatenate([l for _, l in parts] + [sl_ref[g]], axis=1)
        alpha = dot3((uh, ul), (right_ref[gy, 0], right_ref[gy, 1]))
        q = p_ref[0, fields] * alpha.reshape(4, 32, 256)
        for j in range(2):
            keep_ref[2 * g + j] = jnp.where(core == 0, q[2 * j], q[2 * j + 1])
            send_ref[2 * g + j] = jnp.where(core == 0, q[2 * j + 1], q[2 * j])
        return carry

    lax.fori_loop(0, 8, group, 0)


def core_sum_kernel(where, keep_ref, got_ref, *out_refs):
    for d, out_ref in enumerate(out_refs):
        at = pl.ds(4 * lax.rem(where[0] + d, 4), 4)
        out_ref[...] = keep_ref[at] + got_ref[at]


def row_sum_kernel(where, a_ref, b_ref, c_ref, d_ref, *out_refs):
    for e, out_ref in enumerate(out_refs):
        at = lax.rem(where[1] + e, 4)
        out_ref[0] = (a_ref[at] + b_ref[at]) + (c_ref[at] + d_ref[at])


def last_sum_kernel(a_ref, b_ref, c_ref, d_ref, out_ref):
    out_ref[...] = ((a_ref[...] + b_ref[...]) + (c_ref[...] + d_ref[...])) * (1.0 / 31.0)


def call(kernel, outs, *args, scalars=True, scratch=(), cost=0):
    specs = ([pl.BlockSpec(memory_space=pltpu.SMEM)] if scalars else []) + [VMEM] * (len(args) - scalars)
    return pl.pallas_call(
        kernel,
        out_shape=[jax.ShapeDtypeStruct(s, F32) for s in outs],
        in_specs=specs,
        out_specs=[VMEM] * len(outs),
        scratch_shapes=scratch,
        cost_estimate=pl.CostEstimate(flops=cost, bytes_accessed=1 << 20, transcendentals=0),
    )(*args)


def body(perturbations, control):
    mem, gx, gy = lax.axis_index("mem"), lax.axis_index("gx"), lax.axis_index("gy")
    where = jnp.stack([mem // 8, (mem // 2) % 4, mem % 2, gx, gy]).astype(jnp.int32)
    left = jnp.asarray(halves(left_table(128, 4)))
    right = jnp.asarray(halves(right_table(512, 2)))

    top, bottom, edge_top, edge_bottom = call(
        product_kernel, [(32, 16, 256)] * 2 + [(4, 16, 128)] * 2, where, perturbations, control
    )
    down = [(i, i + 1) for i in range(3)]
    up = [(i + 1, i) for i in range(3)]
    cross = lambda pairs: [(2 * a + s, 2 * b + 1 - s) for a, b in pairs for s in range(2)]
    above = lax.ppermute(bottom, "gx", down)
    below = lax.ppermute(top, "gx", up)
    side_top = lax.ppermute(edge_top, "gy", [(0, 1), (1, 0)])
    side_bottom = lax.ppermute(edge_bottom, "gy", [(0, 1), (1, 0)])
    side_above = lax.ppermute(edge_bottom, ("gx", "gy"), cross(down))
    side_below = lax.ppermute(edge_top, ("gx", "gy"), cross(up))

    keep, send = call(
        filter_kernel, [(16, 32, 256)] * 2, where, perturbations, above, top, bottom, below,
        side_above, side_top, side_bottom, side_below, left, right,
        scratch=[pltpu.VMEM((512, 256), BF16)] * 2 + [pltpu.VMEM((8, 128, 128), BF16)] * 2,
        cost=4 * 10**9,
    )
    got = lax.ppermute(send, "mem", [(m, m ^ 1) for m in range(32)])
    pieces = call(core_sum_kernel, [(4, 32, 256)] * 4, where, keep, got)
    along_x = lambda d: [(m, (m + 8 * d) % 32) for m in range(32)]
    along_z = lambda e: [(m, m - m % 8 + (m % 8 + 2 * e) % 8) for m in range(32)]
    got_x = {d: lax.ppermute(pieces[d], "mem", along_x(d)) for d in (2, 1, 3)}
    cells = call(row_sum_kernel, [(1, 32, 256)] * 4, where, pieces[0], got_x[1], got_x[2], got_x[3])
    got_z = {e: lax.ppermute(cells[e], "mem", along_z(e)) for e in (2, 1, 3)}
    return call(last_sum_kernel, [(1, 32, 256)], cells[0], got_z[1], got_z[2], got_z[3], scalars=False)[0]


def solution(mesh):
    placed = (P("mem", None, "gx", "gy"), P(None, "gx", "gy"))
    return jax.shard_map(
        body, mesh=mesh, in_specs=placed, out_specs=P("mem", "gx", "gy"), check_vma=False
    )
```

```python
import jax
import jax.numpy as jnp
import numpy as np
from jax import lax
from jax.experimental import pallas as pl
from jax.experimental.pallas import tpu as pltpu
from jax.sharding import Mesh, PartitionSpec as P

F32, BF16 = jnp.float32, jnp.bfloat16
HALO = 16
VMEM = pl.BlockSpec(memory_space=pltpu.VMEM)


def line_terms(size):
    offsets = np.arange(-4, 5)
    taps = np.exp(-offsets * offsets / 18.0)
    taps = taps / np.sqrt(np.sum(taps * taps))

    def banded(count):
        return sum(t * np.eye(count, k=o) for t, o in zip(taps, offsets))

    pairs = np.repeat(np.eye(size // 2), 2, axis=1) * np.sqrt(0.5)
    coarse = np.sqrt(0.5) * banded(size // 2) @ pairs
    return banded(size), np.repeat(coarse, 2, axis=0), coarse


def split(values):
    high = values.astype(BF16)
    return high, (values - high.astype(values.dtype)).astype(BF16)


def left_table(size, parts):
    fine, pair, coarse = line_terms(size)
    rows = size // parts
    tables = []
    for part in range(parts):
        terms = []
        for term in (fine @ fine, fine @ pair, coarse @ fine, coarse @ pair):
            count = term.shape[0] // parts
            wide = np.zeros((count, rows + 2 * HALO))
            for e in range(rows + 2 * HALO):
                source = part * rows - HALO + e
                if 0 <= source < size:
                    wide[:, e] = term[part * count : (part + 1) * count, source]
            segments = wide.reshape(count, 4, 1, HALO)
            terms.append(np.broadcast_to(segments, (count, 4, 4, HALO)).reshape(count, 256))
        tables.append(np.concatenate(terms))
    return np.stack(tables)


def right_tables(size, parts):
    fine, pair, _ = line_terms(size)
    columns = size // parts
    owns, sides = [], []
    for part in range(parts):
        own = slice(part * columns, (part + 1) * columns)
        edge = slice(columns, columns + HALO) if part == 0 else slice(columns - HALO, columns)
        near = slice(columns - HALO, columns) if part == 0 else slice(columns, columns + HALO)
        terms = (fine @ fine, pair @ fine, fine @ pair, pair @ pair)
        owns.append(np.concatenate([term[own, own] for term in terms]))
        sides.append(np.concatenate([np.kron(np.eye(8), term[edge, near]) for term in terms]))
    return np.stack(owns), np.stack(sides)


def halves(table):
    high = table.astype(np.float32).astype(BF16)
    low = (table - high.astype(np.float64)).astype(np.float32).astype(BF16)
    return np.stack([high, low], axis=1)


def dot3(left, right):
    (lh, ll), (rh, rl) = left, right
    dot = lambda a, b: jnp.dot(a, b, preferred_element_type=F32)
    return dot(lh, rh) + (dot(lh, rl) + dot(ll, rh))


def product_kernel(where, p_ref, c_ref, top_ref, bottom_ref, edge_top_ref, edge_bottom_ref):
    gy = where[2]
    lane = lax.broadcasted_iota(jnp.int32, (1, 1, 128), 2)
    edges = jnp.zeros((4, 32, 128), F32)
    for g in range(8):
        v = p_ref[0, 4 * g : 4 * g + 4] * c_ref[4 * g : 4 * g + 4]
        top_ref[4 * g : 4 * g + 4] = v[:, :HALO]
        bottom_ref[4 * g : 4 * g + 4] = v[:, HALO:]
        last = v[:, :, 128:].reshape(128, 128)
        first = v[:, :, :128].reshape(128, 128)
        edge = jnp.where(gy == 0, pltpu.roll(last, 16, 1), first)
        if g:
            edge = pltpu.roll(edge, 16 * g, 1)
        edges = jnp.where(lane // 16 == g, edge.reshape(4, 32, 128), edges)
    edge_top_ref[...] = edges[:, :HALO]
    edge_bottom_ref[...] = edges[:, HALO:]


def filter_kernel(
    where, p_ref, above_ref, top_ref, bottom_ref, below_ref,
    side_above_ref, side_top_ref, side_bottom_ref, side_below_ref,
    left_ref, right_ref, edge_ref, keep_ref, send_ref,
    xh_ref, xl_ref, fh_ref, fl_ref, ch_ref, cl_ref, alpha_ref, pairs_ref, near_ref,
):
    core, gx, gy = where[0], where[1], where[2]
    lane = lax.broadcasted_iota(jnp.int32, (1, 256), 1)
    row, start = 0, 0
    for count in (32, 32, 16, 16):
        for f in range(4):
            mine = (lane // 16) % 4 == f
            rows, at = slice(start, start + count), slice(row, row + count)
            zero = jnp.zeros((count, 256), F32)
            xh_ref[at] = jnp.where(mine, left_ref[gx, 0, rows].astype(F32), zero).astype(BF16)
            xl_ref[at] = jnp.where(mine, left_ref[gx, 1, rows].astype(F32), zero).astype(BF16)
            row += count
        start += count

    def by_rows(refs, pick):
        return dot3((xh_ref[...], xl_ref[...]), split(jnp.concatenate([pick(r) for r in refs])))

    side = by_rows((side_above_ref, side_top_ref, side_bottom_ref, side_below_ref), lambda r: r[...].reshape(64, 128))
    fine = split(jnp.concatenate([side[:128], side[128:256]], axis=1))
    pair = split(jnp.concatenate([side[256:320], side[320:]], axis=1))
    near = dot3(fine, (edge_ref[gy, 0, :256], edge_ref[gy, 1, :256]))
    near_pairs = dot3(pair, (edge_ref[gy, 0, 256:], edge_ref[gy, 1, 256:]))
    near_ref[pl.ds(0, 64, stride=2), :] = near_pairs
    near_ref[pl.ds(1, 64, stride=2), :] = near_pairs
    near = near + near_ref[...]
    near = jnp.where(gy == 0, pltpu.roll(near, 112, 1), near)
    narrow = lax.broadcasted_iota(jnp.int32, (1, 128), 1)
    on_left = (narrow < HALO) & (gy == 1)
    on_right = (narrow >= 128 - HALO) & (gy == 0)

    for g in range(8):
        u = by_rows((above_ref, top_ref, bottom_ref, below_ref), lambda r: r[4 * g : 4 * g + 4].reshape(64, 256))
        for t in range(2):
            at, lanes = slice(128 * g, 128 * g + 128), slice(256 * t, 256 * t + 256)
            fh_ref[at, lanes], fl_ref[at, lanes] = split(u[128 * t : 128 * t + 128])
            at = slice(64 * g, 64 * g + 64)
            ch_ref[at, lanes], cl_ref[at, lanes] = split(u[256 + 64 * t : 320 + 64 * t])

    alpha_ref[...] = dot3((fh_ref[...], fl_ref[...]), (right_ref[gy, 0, :512], right_ref[gy, 1, :512]))
    pairs = dot3((ch_ref[...], cl_ref[...]), (right_ref[gy, 0, 512:], right_ref[gy, 1, 512:]))
    for h in range(2):
        for s in range(2):
            pairs_ref[h, pl.ds(s, 512, stride=2), :] = pairs[:, 128 * h : 128 * h + 128]

    for g in range(8):
        at = slice(128 * g, 128 * g + 128)
        moved = pltpu.roll(near, (128 - 16 * g) % 128, 1) if g else near
        zero = jnp.zeros_like(moved)
        low = pairs_ref[0, at] + jnp.where(on_left, moved, zero)
        high = pairs_ref[1, at] + jnp.where(on_right, moved, zero)
        alpha = alpha_ref[at] + jnp.concatenate([low, high], axis=1)
        q = p_ref[0, 4 * g : 4 * g + 4] * alpha.reshape(4, 32, 256)
        for j in range(2):
            keep_ref[2 * g + j] = jnp.where(core == 0, q[2 * j], q[2 * j + 1])
            send_ref[2 * g + j] = jnp.where(core == 0, q[2 * j + 1], q[2 * j])


def call(kernel, outs, *args, scratch=(), cost=0, grant=16):
    specs = [pl.BlockSpec(memory_space=pltpu.SMEM)] + [VMEM] * (len(args) - 1)
    return pl.pallas_call(
        kernel,
        out_shape=[jax.ShapeDtypeStruct(s, F32) for s in outs],
        in_specs=specs,
        out_specs=[VMEM] * len(outs),
        scratch_shapes=scratch,
        cost_estimate=pl.CostEstimate(flops=cost, bytes_accessed=1 << 20, transcendentals=0),
        compiler_params=pltpu.CompilerParams(vmem_limit_bytes=grant << 20),
    )(*args)


def body(perturbations, control):
    core, gx, gy = lax.axis_index("core"), lax.axis_index("gx"), lax.axis_index("gy")
    where = jnp.stack([core, gx, gy]).astype(jnp.int32)
    left = jnp.asarray(halves(left_table(128, 4)))
    right, edge = (jnp.asarray(halves(t)) for t in right_tables(512, 2))

    top, bottom, edge_top, edge_bottom = call(
        product_kernel, [(32, 16, 256)] * 2 + [(4, 16, 128)] * 2, where, perturbations, control
    )
    down = [(i, i + 1) for i in range(3)]
    up = [(i + 1, i) for i in range(3)]
    cross = lambda pairs: [(2 * a + s, 2 * b + 1 - s) for a, b in pairs for s in range(2)]
    above = lax.ppermute(bottom, "gx", down)
    below = lax.ppermute(top, "gx", up)
    side_top = lax.ppermute(edge_top, "gy", [(0, 1), (1, 0)])
    side_bottom = lax.ppermute(edge_bottom, "gy", [(0, 1), (1, 0)])
    side_above = lax.ppermute(edge_bottom, ("gx", "gy"), cross(down))
    side_below = lax.ppermute(edge_top, ("gx", "gy"), cross(up))

    vmem, f32 = pltpu.VMEM, F32
    keep, send = call(
        filter_kernel, [(16, 32, 256)] * 2, where, perturbations, above, top, bottom, below,
        side_above, side_top, side_bottom, side_below, left, right, edge,
        scratch=[vmem((384, 256), BF16)] * 2 + [vmem((1024, 512), BF16)] * 2 + [vmem((512, 512), BF16)] * 2
        + [vmem((1024, 256), f32), vmem((2, 1024, 128), f32), vmem((128, 128), f32)],
        cost=4 * 10**9, grant=24,
    )
    got = lax.ppermute(send, "core", [(0, 1), (1, 0)])
    pieces = lax.all_to_all(keep + got, ("x", "z"), 0, 0, tiled=True)
    return jnp.sum(pieces, axis=0, keepdims=True) * (1.0 / 31.0)


def solution(mesh):
    grid = Mesh(mesh.devices.reshape(4, 4, 2, 4, 2), ("x", "z", "core", "gx", "gy"))
    mem = ("x", "z", "core")
    placed = (P(mem, None, "gx", "gy"), P(None, "gx", "gy"))
    return jax.shard_map(
        body, mesh=grid, in_specs=placed, out_specs=P(mem, "gx", "gy"), check_vma=False
    )
```

```python
import jax
import jax.numpy as jnp
import numpy as np
from jax import lax
from jax.experimental import pallas as pl
from jax.experimental.pallas import tpu as pltpu
from jax.sharding import Mesh, PartitionSpec as P

F32, BF16 = jnp.float32, jnp.bfloat16
HALO = 16
VMEM = pl.BlockSpec(memory_space=pltpu.VMEM)


def line_terms(size):
    offsets = np.arange(-4, 5)
    taps = np.exp(-offsets * offsets / 18.0)
    taps = taps / np.sqrt(np.sum(taps * taps))

    def banded(count):
        return sum(t * np.eye(count, k=o) for t, o in zip(taps, offsets))

    pairs = np.repeat(np.eye(size // 2), 2, axis=1) * np.sqrt(0.5)
    coarse = np.sqrt(0.5) * banded(size // 2) @ pairs
    return banded(size), np.repeat(coarse, 2, axis=0), coarse


def split(values):
    high = values.astype(BF16)
    return high, (values - high.astype(values.dtype)).astype(BF16)


def left_table(size, parts):
    fine, pair, coarse = line_terms(size)
    rows = size // parts
    tables = []
    for part in range(parts):
        terms = []
        for term in (fine @ fine, fine @ pair, coarse @ fine, coarse @ pair):
            count = term.shape[0] // parts
            wide = np.zeros((count, rows + 2 * HALO))
            for e in range(rows + 2 * HALO):
                source = part * rows - HALO + e
                if 0 <= source < size:
                    wide[:, e] = term[part * count : (part + 1) * count, source]
            segments = wide.reshape(count, 4, 1, HALO)
            terms.append(np.broadcast_to(segments, (count, 4, 4, HALO)).reshape(count, 256))
        tables.append(np.concatenate(terms))
    return np.stack(tables)


def right_tables(size, parts):
    fine, pair, _ = line_terms(size)
    columns = size // parts
    owns, sides = [], []
    for part in range(parts):
        own = slice(part * columns, (part + 1) * columns)
        edge = slice(columns, columns + HALO) if part == 0 else slice(columns - HALO, columns)
        near = slice(columns - HALO, columns) if part == 0 else slice(columns, columns + HALO)
        terms = (fine @ fine, pair @ fine, fine @ pair, pair @ pair)
        owns.append(np.concatenate([term[own, own] for term in terms]))
        sides.append(np.concatenate([np.tile(term[edge, near], (1, 8)) for term in terms]))
    return np.stack(owns), np.stack(sides)


def halves(table):
    high = table.astype(np.float32).astype(BF16)
    low = (table - high.astype(np.float64)).astype(np.float32).astype(BF16)
    return np.stack([high, low], axis=1)


def dot3(left, right):
    (lh, ll), (rh, rl) = left, right
    dot = lambda a, b: jnp.dot(a, b, preferred_element_type=F32)
    return dot(lh, rh) + (dot(lh, rl) + dot(ll, rh))


def product_kernel(where, p_hbm, c_hbm, top_ref, bottom_ref, edge_ref, edge_top_ref, edge_bottom_ref, p_ref, c_ref, sems):
    gy = where[2]
    copies = []
    for g in range(8):
        at = pl.ds(4 * g, 4)
        copies.append(pltpu.make_async_copy(p_hbm.at[0, at], p_ref.at[at], sems.at[0, g]))
        copies.append(pltpu.make_async_copy(c_hbm.at[at], c_ref.at[at], sems.at[1, g]))
    for copy in copies:
        copy.start()
    lane = lax.broadcasted_iota(jnp.int32, (1, 1, 128), 2)
    edges = jnp.zeros((4, 32, 128), F32)
    for g in range(8):
        copies[2 * g].wait()
        copies[2 * g + 1].wait()
        v = p_ref[4 * g : 4 * g + 4] * c_ref[4 * g : 4 * g + 4]
        top_ref[4 * g : 4 * g + 4] = v[:, :HALO]
        bottom_ref[4 * g : 4 * g + 4] = v[:, HALO:]
        last = v[:, :, 128:].reshape(128, 128)
        first = v[:, :, :128].reshape(128, 128)
        edge = jnp.where(gy == 0, pltpu.roll(last, 16, 1), first)
        if g:
            edge = pltpu.roll(edge, 16 * g, 1)
        edges = jnp.where(lane // 16 == g, edge.reshape(4, 32, 128), edges)
    edge_ref[...] = edges
    edge_top_ref[...] = edges[:, :HALO]
    edge_bottom_ref[...] = edges[:, HALO:]


def filter_kernel(
    where, p_ref, above_ref, top_ref, bottom_ref, below_ref,
    side_above_ref, side_ref, side_below_ref, left_ref, edge_ref, right_hbm, keep_ref, send_ref,
    xh_ref, xl_ref, fh_ref, fl_ref, ch_ref, cl_ref, alpha_ref, pairs_ref, near_ref, right_ref, sems,
):
    core, gx, gy = where[0], where[1], where[2]
    copies = []
    for h in range(2):
        for k in range(4):
            at = pl.ds(256 * k, 256)
            copies.append(pltpu.make_async_copy(right_hbm.at[gy, h, at], right_ref.at[h, at], sems.at[h, k]))
    for copy in copies:
        copy.start()
    lane = lax.broadcasted_iota(jnp.int32, (1, 256), 1)
    row, start = 0, 0
    for count in (32, 32, 16, 16):
        for f in range(4):
            mine = (lane // 16) % 4 == f
            rows, at = slice(start, start + count), slice(row, row + count)
            zero = jnp.zeros((count, 256), F32)
            xh_ref[at] = jnp.where(mine, left_ref[gx, 0, rows].astype(F32), zero).astype(BF16)
            xl_ref[at] = jnp.where(mine, left_ref[gx, 1, rows].astype(F32), zero).astype(BF16)
            row += count
        start += count

    def by_rows(parts):
        return dot3((xh_ref[...], xl_ref[...]), split(jnp.concatenate(parts)))

    sides = (side_above_ref[...], side_ref[:, :HALO], side_ref[:, HALO:], side_below_ref[...])
    side = by_rows([s.reshape(64, 128) for s in sides])
    fine = split(jnp.concatenate([side[:128], side[128:256]], axis=1))
    pair = split(jnp.concatenate([side[256:320], side[320:]], axis=1))
    narrow = lax.broadcasted_iota(jnp.int32, (1, 128), 1)

    def edge(h, t):
        rows = edge_ref[gy, h, 16 * t : 16 * t + 16].astype(F32)
        return [jnp.where(narrow // 16 == g, rows, jnp.zeros_like(rows)).astype(BF16) for g in range(8)]

    near = dot3(fine, [jnp.concatenate(edge(h, 0) + edge(h, 1)) for h in range(2)])
    near_pairs = dot3(pair, [jnp.concatenate(edge(h, 2) + edge(h, 3)) for h in range(2)])
    near_ref[pl.ds(0, 64, stride=2), :] = near_pairs
    near_ref[pl.ds(1, 64, stride=2), :] = near_pairs
    near = near + near_ref[...]
    near = jnp.where(gy == 0, pltpu.roll(near, 112, 1), near)
    on_left = (narrow < HALO) & (gy == 1)
    on_right = (narrow >= 128 - HALO) & (gy == 0)

    for g in range(8):
        u = by_rows([r[4 * g : 4 * g + 4].reshape(64, 256) for r in (above_ref, top_ref, bottom_ref, below_ref)])
        for t in range(2):
            at, lanes = slice(128 * g, 128 * g + 128), slice(256 * t, 256 * t + 256)
            fh_ref[at, lanes], fl_ref[at, lanes] = split(u[128 * t : 128 * t + 128])
            at = slice(64 * g, 64 * g + 64)
            ch_ref[at, lanes], cl_ref[at, lanes] = split(u[256 + 64 * t : 320 + 64 * t])

    for copy in copies:
        copy.wait()
    alpha_ref[...] = dot3((fh_ref[...], fl_ref[...]), (right_ref[0, :512], right_ref[1, :512]))
    pairs = dot3((ch_ref[...], cl_ref[...]), (right_ref[0, 512:], right_ref[1, 512:]))
    for h in range(2):
        for s in range(2):
            pairs_ref[h, pl.ds(s, 512, stride=2), :] = pairs[:, 128 * h : 128 * h + 128]

    for g in range(8):
        at = slice(128 * g, 128 * g + 128)
        moved = pltpu.roll(near, (128 - 16 * g) % 128, 1) if g else near
        zero = jnp.zeros_like(moved)
        low = pairs_ref[0, at] + jnp.where(on_left, moved, zero)
        high = pairs_ref[1, at] + jnp.where(on_right, moved, zero)
        alpha = alpha_ref[at] + jnp.concatenate([low, high], axis=1)
        q = p_ref[4 * g : 4 * g + 4] * alpha.reshape(4, 32, 256)
        for j in range(2):
            at = 4 * lax.rem(g // 2 + 4 - where[3], 4) + lax.rem(2 * (g % 2) + j + 4 - where[4], 4)
            keep_ref[at] = jnp.where(core == 0, q[2 * j], q[2 * j + 1])
            send_ref[at] = jnp.where(core == 0, q[2 * j + 1], q[2 * j])


def call(kernel, outs, *args, hbm=(), scratch=(), cost=0, grant=16):
    args = [pltpu.with_memory_space_constraint(a, pltpu.HBM) if i in hbm else a for i, a in enumerate(args)]
    specs = [pl.BlockSpec(memory_space=pltpu.SMEM)] + [
        pl.BlockSpec(memory_space=pltpu.HBM) if i in hbm else VMEM for i in range(1, len(args))
    ]
    return pl.pallas_call(
        kernel,
        out_shape=[jax.ShapeDtypeStruct(s, F32) for s in outs],
        in_specs=specs,
        out_specs=[VMEM] * len(outs),
        scratch_shapes=scratch,
        cost_estimate=pl.CostEstimate(flops=cost, bytes_accessed=1 << 20, transcendentals=0),
        compiler_params=pltpu.CompilerParams(vmem_limit_bytes=grant << 20),
    )(*args)


def body(perturbations, control):
    x, z, core, gx, gy = (lax.axis_index(a) for a in ("x", "z", "core", "gx", "gy"))
    where = jnp.stack([core, gx, gy, x, z]).astype(jnp.int32)
    left = jnp.asarray(halves(left_table(128, 4)))
    right, edge = (jnp.asarray(halves(t)) for t in right_tables(512, 2))
    vmem, sems = pltpu.VMEM, pltpu.SemaphoreType.DMA

    top, bottom, edges, edge_top, edge_bottom, near_p = call(
        product_kernel, [(32, 16, 256)] * 2 + [(4, 32, 128)] + [(4, 16, 128)] * 2 + [(32, 32, 256)],
        where, perturbations, control, hbm=(1, 2), scratch=[vmem((32, 32, 256), F32), sems((2, 8))],
    )
    down = [(i, i + 1) for i in range(3)]
    up = [(i + 1, i) for i in range(3)]
    cross = lambda pairs: [(2 * a + s, 2 * b + 1 - s) for a, b in pairs for s in range(2)]

    side = lax.ppermute(edges, "gy", [(0, 1), (1, 0)])
    side_above = lax.ppermute(edge_bottom, ("gx", "gy"), cross(down))
    side_below = lax.ppermute(edge_top, ("gx", "gy"), cross(up))
    above = lax.ppermute(bottom, "gx", down)
    below = lax.ppermute(top, "gx", up)

    keep, give = call(
        filter_kernel, [(16, 32, 256)] * 2, where, near_p, above, top, bottom, below,
        side_above, side, side_below, left, edge, right, hbm=(11,),
        scratch=[vmem((384, 256), BF16)] * 2 + [vmem((1024, 512), BF16)] * 2 + [vmem((512, 512), BF16)] * 2
        + [vmem((1024, 256), F32), vmem((2, 1024, 128), F32), vmem((128, 128), F32)]
        + [vmem((2, 1024, 256), BF16), sems((2, 4))],
        cost=4 * 10**9, grant=24,
    )
    got = lax.ppermute(give, "core", [(0, 1), (1, 0)])
    ring = lambda d: [(i, (i + d) % 4) for i in range(4)]
    piece = [keep[4 * d : 4 * d + 4] + got[4 * d : 4 * d + 4] for d in range(4)]
    x2, x1, x3 = (lax.ppermute(piece[d], "x", ring(d)) for d in (2, 1, 3))
    cell = [(piece[0][e : e + 1] + x2[e : e + 1]) + (x1[e : e + 1] + x3[e : e + 1]) for e in range(4)]
    z2, z1, z3 = (lax.ppermute(cell[e], "z", ring(e)) for e in (2, 1, 3))
    return ((cell[0] + z2) + (z1 + z3)) * (1.0 / 31.0)


def solution(mesh):
    grid = Mesh(mesh.devices.reshape(4, 4, 2, 4, 2), ("x", "z", "core", "gx", "gy"))
    mem = ("x", "z", "core")
    placed = (P(mem, None, "gx", "gy"), P(None, "gx", "gy"))
    return jax.shard_map(body, mesh=grid, in_specs=placed, out_specs=P(mem, "gx", "gy"), check_vma=False)
```

```python
import jax
import jax.numpy as jnp
import numpy as np
from jax import lax
from jax.experimental import pallas as pl
from jax.experimental.pallas import tpu as pltpu
from jax.sharding import Mesh, PartitionSpec as P

F32, BF16 = jnp.float32, jnp.bfloat16
HALO = 16
VMEM = pl.BlockSpec(memory_space=pltpu.VMEM)


def line_terms(size):
    offsets = np.arange(-4, 5)
    taps = np.exp(-offsets * offsets / 18.0)
    taps = taps / np.sqrt(np.sum(taps * taps))

    def banded(count):
        return sum(t * np.eye(count, k=o) for t, o in zip(taps, offsets))

    pairs = np.repeat(np.eye(size // 2), 2, axis=1) * np.sqrt(0.5)
    coarse = np.sqrt(0.5) * banded(size // 2) @ pairs
    return banded(size), np.repeat(coarse, 2, axis=0), coarse


def split(values):
    high = values.astype(BF16)
    return high, (values - high.astype(values.dtype)).astype(BF16)


def left_table(size, parts):
    fine, pair, coarse = line_terms(size)
    rows = size // parts
    tables = []
    for part in range(parts):
        terms = []
        for term in (fine @ fine, fine @ pair, coarse @ fine, coarse @ pair):
            count = term.shape[0] // parts
            wide = np.zeros((count, rows + 2 * HALO))
            for e in range(rows + 2 * HALO):
                source = part * rows - HALO + e
                if 0 <= source < size:
                    wide[:, e] = term[part * count : (part + 1) * count, source]
            segments = wide.reshape(count, 4, 1, HALO)
            terms.append(np.broadcast_to(segments, (count, 4, 4, HALO)).reshape(count, 256))
        tables.append(np.concatenate(terms))
    return np.stack(tables)


def right_tables(size, parts):
    fine, pair, _ = line_terms(size)
    columns = size // parts
    owns, sides = [], []
    for part in range(parts):
        own = slice(part * columns, (part + 1) * columns)
        edge = slice(columns, columns + HALO) if part == 0 else slice(columns - HALO, columns)
        near = slice(columns - HALO, columns) if part == 0 else slice(columns, columns + HALO)
        terms = (fine @ fine, pair @ fine, fine @ pair, pair @ pair)
        owns.append(np.concatenate([term[own, own] for term in terms]))
        sides.append(np.concatenate([np.tile(term[edge, near], (1, 8)) for term in terms]))
    return np.stack(owns), np.stack(sides)


def halves(table):
    high = table.astype(np.float32).astype(BF16)
    low = (table - high.astype(np.float64)).astype(np.float32).astype(BF16)
    return np.stack([high, low], axis=1)


def dot3(left, right):
    (lh, ll), (rh, rl) = left, right
    dot = lambda a, b: jnp.dot(a, b, preferred_element_type=F32)
    return dot(lh, rh) + (dot(lh, rl) + dot(ll, rh))


def load_half(p_hbm, c_hbm, p_ref, c_ref, sems, half):
    copies = []
    lanes = pl.ds(pl.multiple_of(128 * half, 128), 128)
    for g in range(4):
        at = pl.ds(8 * g, 8)
        copies.append(pltpu.make_async_copy(p_hbm.at[0, at, :, lanes], p_ref.at[at], sems.at[0, g]))
        copies.append(pltpu.make_async_copy(c_hbm.at[at, :, lanes], c_ref.at[at], sems.at[1, g]))
    for copy in copies:
        copy.start()
    return copies


def edge_kernel(where, p_hbm, c_hbm, v_ref, edge_ref, p_ref, c_ref, sems):
    gy = where[2]
    copies = load_half(p_hbm, c_hbm, p_ref, c_ref, sems, 1 - gy)
    lane = lax.broadcasted_iota(jnp.int32, (1, 1, 128), 2)
    edges = jnp.zeros((4, 32, 128), F32)
    for g in range(8):
        if g % 2 == 0:
            copies[g].wait()
            copies[g + 1].wait()
        at = slice(4 * g, 4 * g + 4)
        v = p_ref[at] * c_ref[at]
        v_ref[at] = v
        v = v.reshape(128, 128)
        v = jnp.where(gy == 0, pltpu.roll(v, 16, 1), v)
        if g:
            v = pltpu.roll(v, 16 * g, 1)
        edges = jnp.where(lane // 16 == g, v.reshape(4, 32, 128), edges)
    for f in range(4):
        edge_ref[f // 2, :, 128 * (f % 2) : 128 * (f % 2) + 128] = edges[f]


def product_kernel(where, p_hbm, c_hbm, near_ref, top_ref, bottom_ref, p_ref, c_ref, sems):
    gy = where[2]
    copies = load_half(p_hbm, c_hbm, p_ref, c_ref, sems, gy)
    for g in range(8):
        if g % 2 == 0:
            copies[g].wait()
            copies[g + 1].wait()
        at = slice(4 * g, 4 * g + 4)
        far, near = p_ref[at] * c_ref[at], near_ref[at]
        v = jnp.concatenate([jnp.where(gy == 0, far, near), jnp.where(gy == 0, near, far)], axis=2)
        top_ref[at] = v[:, :HALO]
        bottom_ref[at] = v[:, HALO:]


def table_kernel(
    where, left_ref, edge_ref, right_hbm, p_hbm, xh_ref, xl_ref, eh_ref, el_ref, right_ref, p_ref, sems
):
    gx, gy = where[1], where[2]
    copies = []
    for h in range(2):
        for k in range(4):
            at = pl.ds(256 * k, 256)
            copies.append(pltpu.make_async_copy(right_hbm.at[gy, h, at], right_ref.at[h, at], sems.at[h, k]))
            at = pl.ds(16 * h + 4 * k, 4)
            copies.append(pltpu.make_async_copy(p_hbm.at[0, at], p_ref.at[at], sems.at[2 + h, k]))
    for copy in copies:
        copy.start()
    lane = lax.broadcasted_iota(jnp.int32, (1, 256), 1)
    narrow = lax.broadcasted_iota(jnp.int32, (1, 128), 1)
    for h, x_ref, e_ref in ((0, xh_ref, eh_ref), (1, xl_ref, el_ref)):
        row, start = 0, 0
        for count in (32, 32, 16, 16):
            rows = left_ref[gx, h, start : start + count].astype(F32)
            for f in range(4):
                mine = (lane // 16) % 4 == f
                x_ref[row : row + count] = jnp.where(mine, rows, jnp.zeros_like(rows)).astype(BF16)
                row += count
            start += count
        for t in range(4):
            rows = edge_ref[gy, h, 16 * t : 16 * t + 16].astype(F32)
            for g in range(8):
                at = 128 * t + 16 * g
                e_ref[at : at + 16] = jnp.where(narrow // 16 == g, rows, jnp.zeros_like(rows)).astype(BF16)
    for copy in copies:
        copy.wait()


def filter_kernel(
    where, p_ref, above_ref, top_ref, bottom_ref, below_ref, side_ref,
    xh_ref, xl_ref, eh_ref, el_ref, right_ref, keep_ref, send_ref,
    fh_ref, fl_ref, ch_ref, cl_ref, alpha_ref, pairs_ref, near_ref,
):
    core, gy = where[0], where[2]

    def by_rows(parts):
        return dot3((xh_ref[...], xl_ref[...]), split(jnp.concatenate(parts)))

    sides = (above_ref[32:], side_ref[:, :HALO], side_ref[:, HALO:], below_ref[32:])
    lanes = (slice(0, 128), slice(128, 256))
    side = by_rows([s[f // 2, :, lanes[f % 2]] for s in sides for f in range(4)])
    fine = split(jnp.concatenate([side[:128], side[128:256]], axis=1))
    pair = split(jnp.concatenate([side[256:320], side[320:]], axis=1))
    narrow = lax.broadcasted_iota(jnp.int32, (1, 128), 1)
    near = dot3(fine, (eh_ref[:256], el_ref[:256]))
    near_pairs = dot3(pair, (eh_ref[256:], el_ref[256:]))
    near_ref[pl.ds(0, 64, stride=2), :] = near_pairs
    near_ref[pl.ds(1, 64, stride=2), :] = near_pairs
    near = near + near_ref[...]
    near = jnp.where(gy == 0, pltpu.roll(near, 112, 1), near)
    on_left = (narrow < HALO) & (gy == 1)
    on_right = (narrow >= 128 - HALO) & (gy == 0)

    for g in range(8):
        u = by_rows([r[4 * g : 4 * g + 4].reshape(64, 256) for r in (above_ref, top_ref, bottom_ref, below_ref)])
        for t in range(2):
            at, lanes = slice(128 * g, 128 * g + 128), slice(256 * t, 256 * t + 256)
            fh_ref[at, lanes], fl_ref[at, lanes] = split(u[128 * t : 128 * t + 128])
            at = slice(64 * g, 64 * g + 64)
            ch_ref[at, lanes], cl_ref[at, lanes] = split(u[256 + 64 * t : 320 + 64 * t])

    alpha_ref[...] = dot3((fh_ref[...], fl_ref[...]), (right_ref[0, :512], right_ref[1, :512]))
    pairs = dot3((ch_ref[...], cl_ref[...]), (right_ref[0, 512:], right_ref[1, 512:]))
    for h in range(2):
        for s in range(2):
            pairs_ref[h, pl.ds(s, 512, stride=2), :] = pairs[:, 128 * h : 128 * h + 128]

    for g in range(8):
        at = slice(128 * g, 128 * g + 128)
        moved = pltpu.roll(near, (128 - 16 * g) % 128, 1) if g else near
        zero = jnp.zeros_like(moved)
        low = pairs_ref[0, at] + jnp.where(on_left, moved, zero)
        high = pairs_ref[1, at] + jnp.where(on_right, moved, zero)
        alpha = alpha_ref[at] + jnp.concatenate([low, high], axis=1)
        q = p_ref[4 * g : 4 * g + 4] * alpha.reshape(4, 32, 256)
        for j in range(2):
            at = 4 * lax.rem(g // 2 + 4 - where[3], 4) + lax.rem(2 * (g % 2) + j + 4 - where[4], 4)
            keep_ref[at] = jnp.where(core == 0, q[2 * j], q[2 * j + 1])
            send_ref[at] = jnp.where(core == 0, q[2 * j + 1], q[2 * j])


def call(kernel, outs, *args, hbm=(), scratch=(), cost=0, grant=16):
    args = [pltpu.with_memory_space_constraint(a, pltpu.HBM) if i in hbm else a for i, a in enumerate(args)]
    specs = [pl.BlockSpec(memory_space=pltpu.SMEM)] + [
        pl.BlockSpec(memory_space=pltpu.HBM) if i in hbm else VMEM for i in range(1, len(args))
    ]
    return pl.pallas_call(
        kernel,
        out_shape=[o if isinstance(o, jax.ShapeDtypeStruct) else jax.ShapeDtypeStruct(o, F32) for o in outs],
        in_specs=specs,
        out_specs=[VMEM] * len(outs),
        scratch_shapes=scratch,
        cost_estimate=pl.CostEstimate(flops=cost, bytes_accessed=1 << 20, transcendentals=0),
        compiler_params=pltpu.CompilerParams(vmem_limit_bytes=grant << 20),
    )(*args)


def body(perturbations, control):
    x, z, core, gx, gy = (lax.axis_index(a) for a in ("x", "z", "core", "gx", "gy"))
    where = jnp.stack([core, gx, gy, x, z]).astype(jnp.int32)
    left = jnp.asarray(halves(left_table(128, 4)))
    right, edge = (jnp.asarray(halves(t)) for t in right_tables(512, 2))
    vmem, sems = pltpu.VMEM, pltpu.SemaphoreType.DMA

    half = [vmem((32, 32, 128), F32)] * 2 + [sems((2, 4))]
    near, edges = call(
        edge_kernel, [(32, 32, 128), (2, 32, 256)], where, perturbations, control, hbm=(1, 2), scratch=half
    )

    ring = lambda d: [(i, (i + d) % 4) for i in range(4)]
    side = lax.ppermute(edges, "gy", [(0, 1), (1, 0)])
    top, bottom = call(
        product_kernel, [(34, 16, 256)] * 2, where, perturbations, control, near, hbm=(1, 2), scratch=half
    )
    top = top.at[32:].set(side[:, :HALO])
    bottom = bottom.at[32:].set(side[:, HALO:])
    above = lax.ppermute(bottom, "gx", ring(1))
    below = lax.ppermute(top, "gx", ring(3))
    *tables, near_p = call(
        table_kernel,
        [jax.ShapeDtypeStruct(s, BF16) for s in [(384, 256)] * 2 + [(512, 128)] * 2 + [(2, 1024, 256)]]
        + [(32, 32, 256)],
        where, left, edge, right, perturbations, hbm=(3, 4), scratch=[sems((4, 4))],
    )
    keep, give = call(
        filter_kernel, [(16, 32, 256)] * 2, where, near_p, above, top, bottom, below, side, *tables,
        scratch=[vmem((1024, 512), BF16)] * 2 + [vmem((512, 512), BF16)] * 2
        + [vmem((1024, 256), F32), vmem((2, 1024, 128), F32), vmem((128, 128), F32)],
        cost=4 * 10**9, grant=24,
    )
    got = lax.ppermute(give, "core", [(0, 1), (1, 0)])
    piece = [keep[4 * d : 4 * d + 4] + got[4 * d : 4 * d + 4] for d in range(4)]
    x2, x1, x3 = (lax.ppermute(piece[d], "x", ring(d)) for d in (2, 1, 3))
    cell = [(piece[0][e : e + 1] + x2[e : e + 1]) + (x1[e : e + 1] + x3[e : e + 1]) for e in range(4)]
    z2, z1, z3 = (lax.ppermute(cell[e], "z", ring(e)) for e in (2, 1, 3))
    return ((cell[0] + z2) + (z1 + z3)) * (1.0 / 31.0)


def solution(mesh):
    grid = Mesh(mesh.devices.reshape(4, 4, 2, 4, 2), ("x", "z", "core", "gx", "gy"))
    mem = ("x", "z", "core")
    placed = (P(mem, None, "gx", "gy"), P(None, "gx", "gy"))
    return jax.shard_map(body, mesh=grid, in_specs=placed, out_specs=P(mem, "gx", "gy"), check_vma=False)
```

```python
import functools

import jax
import jax.numpy as jnp
import numpy as np
from jax import lax
from jax.experimental import pallas as pl
from jax.experimental.pallas import tpu as pltpu
from jax.sharding import Mesh, PartitionSpec as P

F32, BF16 = jnp.float32, jnp.bfloat16
HALO = 16
VMEM = pl.BlockSpec(memory_space=pltpu.VMEM)


def line_terms(size):
    offsets = np.arange(-4, 5)
    taps = np.exp(-offsets * offsets / 18.0)
    taps = taps / np.sqrt(np.sum(taps * taps))

    def banded(count):
        return sum(t * np.eye(count, k=o) for t, o in zip(taps, offsets))

    pairs = np.repeat(np.eye(size // 2), 2, axis=1) * np.sqrt(0.5)
    coarse = np.sqrt(0.5) * banded(size // 2) @ pairs
    return banded(size), np.repeat(coarse, 2, axis=0), coarse


def split(values):
    high = values.astype(BF16)
    return high, (values - high.astype(values.dtype)).astype(BF16)


def left_table(size, parts):
    fine, pair, coarse = line_terms(size)
    rows = size // parts
    tables = []
    for part in range(parts):
        terms = []
        for term in (fine @ fine, fine @ pair, coarse @ fine, coarse @ pair):
            count = term.shape[0] // parts
            wide = np.zeros((count, rows + 2 * HALO))
            for e in range(rows + 2 * HALO):
                source = part * rows - HALO + e
                if 0 <= source < size:
                    wide[:, e] = term[part * count : (part + 1) * count, source]
            segments = wide.reshape(count, 4, 1, HALO)
            terms.append(np.broadcast_to(segments, (count, 4, 4, HALO)).reshape(count, 256))
        tables.append(np.concatenate(terms))
    return np.stack(tables)


def right_tables(size, parts):
    fine, pair, _ = line_terms(size)
    columns = size // parts
    owns, sides = [], []
    for part in range(parts):
        own = slice(part * columns, (part + 1) * columns)
        edge = slice(columns, columns + HALO) if part == 0 else slice(columns - HALO, columns)
        near = slice(columns - HALO, columns) if part == 0 else slice(columns, columns + HALO)
        terms = (fine @ fine, pair @ fine, fine @ pair, pair @ pair)
        owns.append(np.concatenate([term[own, own] for term in terms]))
        sides.append(np.concatenate([np.tile(term[edge, near], (1, 8)) for term in terms]))
    return np.stack(owns), np.stack(sides)


def halves(table):
    high = table.astype(np.float32).astype(BF16)
    low = (table - high.astype(np.float64)).astype(np.float32).astype(BF16)
    return np.stack([high, low], axis=1)


def dot3(left, right):
    (lh, ll), (rh, rl) = left, right
    dot = lambda a, b: jnp.dot(a, b, preferred_element_type=F32)
    return dot(lh, rh) + (dot(lh, rl) + dot(ll, rh))


def block_of(where, k):
    return lax.rem(where[3] + (2, 1, 3, 0)[k], 4)


def edge_kernel(where, p_hbm, c_hbm, p_ref, c_ref, edge_ref, sems):
    gy = where[2]
    copies = []
    for k in range(4):
        for h in range(2):
            source, at = pl.ds(8 * block_of(where, k) + 4 * h, 4), pl.ds(8 * k + 4 * h, 4)
            copies.append(pltpu.make_async_copy(p_hbm.at[0, source], p_ref.at[at], sems.at[0, 2 * k + h]))
            copies.append(pltpu.make_async_copy(c_hbm.at[source], c_ref.at[at], sems.at[1, 2 * k + h]))
    for copy in copies:
        copy.start()
    lane = lax.broadcasted_iota(jnp.int32, (1, 1, 128), 2)
    edges = jnp.zeros((4, 32, 128), F32)
    for g in range(8):
        copies[2 * g].wait()
        copies[2 * g + 1].wait()
        at = slice(4 * g, 4 * g + 4)
        last = (p_ref[at, :, 128:] * c_ref[at, :, 128:]).reshape(128, 128)
        first = (p_ref[at, :, :128] * c_ref[at, :, :128]).reshape(128, 128)
        v = jnp.where(gy == 0, pltpu.roll(last, 16, 1), first)
        if g:
            v = pltpu.roll(v, 16 * g, 1)
        edges = jnp.where(lane // 16 == g, v.reshape(4, 32, 128), edges)
    for f in range(4):
        edge_ref[f // 2, :, 128 * (f % 2) : 128 * (f % 2) + 128] = edges[f]


def product_kernel(where, p_ref, c_ref, *out_refs):
    for g in range(8):
        v = p_ref[4 * g : 4 * g + 4] * c_ref[4 * g : 4 * g + 4]
        top_ref, bottom_ref = out_refs[:2] if g < 4 else out_refs[2:]
        at = slice(4 * (g % 4), 4 * (g % 4) + 4)
        top_ref[at] = v[:, :HALO]
        bottom_ref[at] = v[:, HALO:]


def table_kernel(
    where, left_ref, edge_ref, right_hbm, xh_ref, xl_ref, eh_ref, el_ref, right_ref, sems
):
    gx, gy = where[1], where[2]
    copies = []
    for h in range(2):
        for k in range(4):
            at = pl.ds(256 * k, 256)
            copies.append(pltpu.make_async_copy(right_hbm.at[gy, h, at], right_ref.at[h, at], sems.at[h, k]))
    for copy in copies:
        copy.start()
    lane = lax.broadcasted_iota(jnp.int32, (1, 256), 1)
    narrow = lax.broadcasted_iota(jnp.int32, (1, 128), 1)
    for h, x_ref, e_ref in ((0, xh_ref, eh_ref), (1, xl_ref, el_ref)):
        row, start = 0, 0
        for count in (32, 32, 16, 16):
            rows = left_ref[gx, h, start : start + count].astype(F32)
            for f in range(4):
                mine = (lane // 16) % 4 == f
                x_ref[row : row + count] = jnp.where(mine, rows, jnp.zeros_like(rows)).astype(BF16)
                row += count
            start += count
        for t in range(4):
            rows = edge_ref[gy, h, 16 * t : 16 * t + 16].astype(F32)
            for g in range(8):
                at = 128 * t + 16 * g
                e_ref[at : at + 16] = jnp.where(narrow // 16 == g, rows, jnp.zeros_like(rows)).astype(BF16)
    for copy in copies:
        copy.wait()


def filter_kernel(
    part, where, p_ref, above_ref, top_ref, bottom_ref, below_ref, xh_ref, xl_ref, right_ref, *refs
):
    core, gy, z = where[0], where[2], where[4]
    dot_rows = lambda parts: dot3((xh_ref[...], xl_ref[...]), split(jnp.concatenate(parts)))
    narrow = lax.broadcasted_iota(jnp.int32, (1, 128), 1)
    if part == 0:
        side_ref, eh_ref, el_ref, keep_ref, send_ref, near_ref, *scratch = refs
        lanes = (slice(0, 128), slice(128, 256))
        sides = (above_ref[16:], side_ref[:, :HALO], side_ref[:, HALO:], below_ref[16:])
        side = dot_rows([s[f // 2, :, lanes[f % 2]] for s in sides for f in range(4)])
        fine = split(jnp.concatenate([side[:128], side[128:256]], axis=1))
        pair = split(jnp.concatenate([side[256:320], side[320:]], axis=1))
        near = dot3(fine, (eh_ref[:256], el_ref[:256]))
        near_pairs = dot3(pair, (eh_ref[256:], el_ref[256:]))
        near_ref[pl.ds(0, 64, stride=2), :] = near_pairs
        near_ref[pl.ds(1, 64, stride=2), :] = near_pairs
        near = near + near_ref[...]
        near = jnp.where(gy == 0, pltpu.roll(near, 112, 1), near)
        near_ref[...] = near
    else:
        near_ref, keep_ref, send_ref, *scratch = refs
        near = near_ref[...]
    fh_ref, fl_ref, ch_ref, cl_ref, alpha_ref, pairs_ref = scratch
    on_left = (narrow < HALO) & (gy == 1)
    on_right = (narrow >= 128 - HALO) & (gy == 0)

    for g in range(4):
        u = dot_rows([r[4 * g : 4 * g + 4].reshape(64, 256) for r in (above_ref, top_ref, bottom_ref, below_ref)])
        for t in range(2):
            at, lanes = slice(128 * g, 128 * g + 128), slice(256 * t, 256 * t + 256)
            fh_ref[at, lanes], fl_ref[at, lanes] = split(u[128 * t : 128 * t + 128])
            at = slice(64 * g, 64 * g + 64)
            ch_ref[at, lanes], cl_ref[at, lanes] = split(u[256 + 64 * t : 320 + 64 * t])

    alpha_ref[...] = dot3((fh_ref[...], fl_ref[...]), (right_ref[0, :512], right_ref[1, :512]))
    pairs = dot3((ch_ref[...], cl_ref[...]), (right_ref[0, 512:], right_ref[1, 512:]))
    for h in range(2):
        for s in range(2):
            pairs_ref[h, pl.ds(s, 256, stride=2), :] = pairs[:, 128 * h : 128 * h + 128]

    for g in range(4):
        at = slice(128 * g, 128 * g + 128)
        shift = (128 - 16 * (4 * part + g)) % 128
        moved = pltpu.roll(near, shift, 1) if shift else near
        zero = jnp.zeros_like(moved)
        low = pairs_ref[0, at] + jnp.where(on_left, moved, zero)
        high = pairs_ref[1, at] + jnp.where(on_right, moved, zero)
        alpha = alpha_ref[at] + jnp.concatenate([low, high], axis=1)
        first = 16 * part + 4 * g
        q = p_ref[first : first + 4] * alpha.reshape(4, 32, 256)
        for j in range(2):
            to = 4 * (g // 2) + lax.rem(2 * (g % 2) + j + 4 - z, 4)
            keep_ref[to] = jnp.where(core == 0, q[2 * j], q[2 * j + 1])
            send_ref[to] = jnp.where(core == 0, q[2 * j + 1], q[2 * j])


def call(kernel, outs, *args, hbm=(), scratch=(), cost=0, grant=16):
    args = [pltpu.with_memory_space_constraint(a, pltpu.HBM) if i in hbm else a for i, a in enumerate(args)]
    specs = [pl.BlockSpec(memory_space=pltpu.SMEM)] + [
        pl.BlockSpec(memory_space=pltpu.HBM) if i in hbm else VMEM for i in range(1, len(args))
    ]
    return pl.pallas_call(
        kernel,
        out_shape=[o if isinstance(o, jax.ShapeDtypeStruct) else jax.ShapeDtypeStruct(o, F32) for o in outs],
        in_specs=specs,
        out_specs=[VMEM] * len(outs),
        scratch_shapes=scratch,
        cost_estimate=pl.CostEstimate(flops=cost, bytes_accessed=1 << 20, transcendentals=0),
        compiler_params=pltpu.CompilerParams(vmem_limit_bytes=grant << 20),
    )(*args)


def body(perturbations, control):
    x, z, core, gx, gy = (lax.axis_index(a) for a in ("x", "z", "core", "gx", "gy"))
    where = jnp.stack([core, gx, gy, x, z]).astype(jnp.int32)
    left = jnp.asarray(halves(left_table(128, 4)))
    right, edge = (jnp.asarray(halves(t)) for t in right_tables(512, 2))
    vmem, sems = pltpu.VMEM, pltpu.SemaphoreType.DMA

    ring = lambda d: [(i, (i + d) % 4) for i in range(4)]
    swap = [(0, 1), (1, 0)]
    near_p, near_c, edges = call(
        edge_kernel, [(32, 32, 256)] * 2 + [(2, 32, 256)], where, perturbations, control, hbm=(1, 2),
        scratch=[sems((2, 8))],
    )
    side = lax.ppermute(edges, "gy", swap)
    tops, bottoms = [None] * 2, [None] * 2
    tops[0], bottoms[0], tops[1], bottoms[1] = call(
        product_kernel, [(18, 16, 256)] * 2 + [(16, 16, 256)] * 2, where, near_p, near_c
    )
    tops[0] = tops[0].at[16:].set(side[:, :HALO])
    bottoms[0] = bottoms[0].at[16:].set(side[:, HALO:])
    aboves, belows = [None] * 2, [None] * 2
    for part in range(2):
        aboves[part] = lax.ppermute(bottoms[part], "gx", ring(1))
        belows[part] = lax.ppermute(tops[part], "gx", ring(3))
    xh, xl, eh, el, right = call(
        table_kernel,
        [jax.ShapeDtypeStruct(s, BF16) for s in [(384, 256)] * 2 + [(512, 128)] * 2 + [(2, 1024, 256)]],
        where, left, edge, right, hbm=(3,), scratch=[sems((2, 4))],
    )
    piece = {}
    for part in range(2):
        extra = (side, eh, el) if part == 0 else (near,)
        keep, give, *rest = call(
            functools.partial(filter_kernel, part), [(8, 32, 256)] * 2 + [(128, 128)] * (part == 0),
            where, near_p, aboves[part], tops[part], bottoms[part], belows[part], xh, xl, right, *extra,
            scratch=[vmem((512, 512), BF16)] * 2 + [vmem((256, 512), BF16)] * 2
            + [vmem((512, 256), F32), vmem((2, 512, 128), F32)],
            cost=2 * 10**9,
        )
        near = rest[0] if rest else None
        got = lax.ppermute(give, "core", swap)
        for i in range(2):
            piece[((2, 1), (3, 0))[part][i]] = keep[4 * i : 4 * i + 4] + got[4 * i : 4 * i + 4]
        if part == 0:
            x2, x1 = (lax.ppermute(piece[d], "x", ring(d)) for d in (2, 1))
    x3 = lax.ppermute(piece[3], "x", ring(3))
    cell = [(piece[0][e : e + 1] + x2[e : e + 1]) + (x1[e : e + 1] + x3[e : e + 1]) for e in range(4)]
    z2, z1, z3 = (lax.ppermute(cell[e], "z", ring(e)) for e in (2, 1, 3))
    return ((cell[0] + z2) + (z1 + z3)) * (1.0 / 31.0)


def solution(mesh):
    grid = Mesh(mesh.devices.reshape(4, 4, 2, 4, 2), ("x", "z", "core", "gx", "gy"))
    mem = ("x", "z", "core")
    placed = (P(mem, None, "gx", "gy"), P(None, "gx", "gy"))
    return jax.shard_map(body, mesh=grid, in_specs=placed, out_specs=P(mem, "gx", "gy"), check_vma=False)
```

```python
import functools

import jax
import jax.numpy as jnp
import numpy as np
from jax import lax
from jax.experimental import pallas as pl
from jax.experimental.pallas import tpu as pltpu
from jax.sharding import Mesh, PartitionSpec as P

F32, BF16 = jnp.float32, jnp.bfloat16
HALO = 16
VMEM = pl.BlockSpec(memory_space=pltpu.VMEM)


def line_terms(size):
    offsets = np.arange(-4, 5)
    taps = np.exp(-offsets * offsets / 18.0)
    taps = taps / np.sqrt(np.sum(taps * taps))

    def banded(count):
        return sum(t * np.eye(count, k=o) for t, o in zip(taps, offsets))

    pairs = np.repeat(np.eye(size // 2), 2, axis=1) * np.sqrt(0.5)
    coarse = np.sqrt(0.5) * banded(size // 2) @ pairs
    return banded(size), np.repeat(coarse, 2, axis=0), coarse


def split(values):
    high = values.astype(BF16)
    return high, (values - high.astype(values.dtype)).astype(BF16)


def left_table(size, parts):
    fine, pair, coarse = line_terms(size)
    rows = size // parts
    tables = []
    for part in range(parts):
        terms = []
        for term in (fine @ fine, fine @ pair, coarse @ fine, coarse @ pair):
            count = term.shape[0] // parts
            wide = np.zeros((count, rows + 2 * HALO))
            for e in range(rows + 2 * HALO):
                source = part * rows - HALO + e
                if 0 <= source < size:
                    wide[:, e] = term[part * count : (part + 1) * count, source]
            segments = wide.reshape(count, 4, 1, HALO)
            terms.append(np.broadcast_to(segments, (count, 4, 4, HALO)).reshape(count, 256))
        tables.append(np.concatenate(terms))
    return np.stack(tables)


def right_tables(size, parts):
    fine, pair, _ = line_terms(size)
    columns = size // parts
    owns, sides = [], []
    for part in range(parts):
        own = slice(part * columns, (part + 1) * columns)
        edge = slice(columns, columns + HALO) if part == 0 else slice(columns - HALO, columns)
        near = slice(columns - HALO, columns) if part == 0 else slice(columns, columns + HALO)
        terms = (fine @ fine, pair @ fine, fine @ pair, pair @ pair)
        owns.append(np.concatenate([term[own, own] for term in terms]))
        sides.append(np.concatenate([np.tile(term[edge, near], (1, 8)) for term in terms]))
    return np.stack(owns), np.stack(sides)


def halves(table):
    high = table.astype(np.float32).astype(BF16)
    low = (table - high.astype(np.float64)).astype(np.float32).astype(BF16)
    return np.stack([high, low], axis=1)


def dot3(left, right):
    (lh, ll), (rh, rl) = left, right
    dot = lambda a, b: jnp.dot(a, b, preferred_element_type=F32)
    return dot(lh, rh) + (dot(lh, rl) + dot(ll, rh))


def block_of(where, k):
    return lax.rem(where[3] + (2, 1, 3, 0)[k], 4)


def product_kernel(where, p_hbm, c_hbm, p_ref, top_ref, bottom_ref, c_ref, sems):
    copies = []
    for k in range(4):
        for h in range(2):
            source, at = pl.ds(8 * block_of(where, k) + 4 * h, 4), pl.ds(8 * k + 4 * h, 4)
            copies.append(pltpu.make_async_copy(p_hbm.at[0, source], p_ref.at[at], sems.at[0, 2 * k + h]))
            copies.append(pltpu.make_async_copy(c_hbm.at[source], c_ref.at[at], sems.at[1, 2 * k + h]))
    for copy in copies:
        copy.start()
    for g in range(8):
        copies[2 * g].wait()
        copies[2 * g + 1].wait()
        at = slice(4 * g, 4 * g + 4)
        v = p_ref[at] * c_ref[at]
        top_ref[at] = v[:, :HALO]
        bottom_ref[at] = v[:, HALO:]


def edge_kernel(where, top_ref, bottom_ref, edge_ref):
    gy = where[2]
    lane = lax.broadcasted_iota(jnp.int32, (1, 1, 128), 2)
    for r_ref, rows in ((top_ref, slice(0, HALO)), (bottom_ref, slice(HALO, 2 * HALO))):
        edges = jnp.zeros((4, HALO, 128), F32)
        for g in range(8):
            at = slice(4 * g, 4 * g + 4)
            last = r_ref[at, :, 128:].reshape(64, 128)
            first = r_ref[at, :, :128].reshape(64, 128)
            v = jnp.where(gy == 0, pltpu.roll(last, 16, 1), first)
            if g:
                v = pltpu.roll(v, 16 * g, 1)
            edges = jnp.where(lane // 16 == g, v.reshape(4, HALO, 128), edges)
        for f in range(4):
            edge_ref[f // 2, rows, 128 * (f % 2) : 128 * (f % 2) + 128] = edges[f]


def table_kernel(
    where, left_ref, edge_ref, right_hbm, xh_ref, xl_ref, eh_ref, el_ref, right_ref, sems
):
    gx, gy = where[1], where[2]
    copies = []
    for h in range(2):
        for k in range(4):
            at = pl.ds(256 * k, 256)
            copies.append(pltpu.make_async_copy(right_hbm.at[gy, h, at], right_ref.at[h, at], sems.at[h, k]))
    for copy in copies:
        copy.start()
    lane = lax.broadcasted_iota(jnp.int32, (1, 256), 1)
    narrow = lax.broadcasted_iota(jnp.int32, (1, 128), 1)
    for h, x_ref, e_ref in ((0, xh_ref, eh_ref), (1, xl_ref, el_ref)):
        row, start = 0, 0
        for count in (32, 32, 16, 16):
            rows = left_ref[gx, h, start : start + count].astype(F32)
            for f in range(4):
                mine = (lane // 16) % 4 == f
                x_ref[row : row + count] = jnp.where(mine, rows, jnp.zeros_like(rows)).astype(BF16)
                row += count
            start += count
        for t in range(4):
            rows = edge_ref[gy, h, 16 * t : 16 * t + 16].astype(F32)
            for g in range(8):
                at = 128 * t + 16 * g
                e_ref[at : at + 16] = jnp.where(narrow // 16 == g, rows, jnp.zeros_like(rows)).astype(BF16)
    for copy in copies:
        copy.wait()


def filter_kernel(
    part, where, p_ref, above_ref, top_ref, bottom_ref, below_ref, xh_ref, xl_ref, right_ref, *refs
):
    core, gy, z = where[0], where[2], where[4]
    dot_rows = lambda parts: dot3((xh_ref[...], xl_ref[...]), split(jnp.concatenate(parts)))
    narrow = lax.broadcasted_iota(jnp.int32, (1, 128), 1)
    if part == 0:
        side_above_ref, side_ref, side_below_ref, eh_ref, el_ref, keep_ref, send_ref, near_ref, *scratch = refs
        lanes = (slice(0, 128), slice(128, 256))
        sides = (side_above_ref, side_ref.at[:, :HALO], side_ref.at[:, HALO:], side_below_ref)
        side = dot_rows([s[f // 2, :, lanes[f % 2]] for s in sides for f in range(4)])
        fine = split(jnp.concatenate([side[:128], side[128:256]], axis=1))
        pair = split(jnp.concatenate([side[256:320], side[320:]], axis=1))
        near = dot3(fine, (eh_ref[:256], el_ref[:256]))
        near_pairs = dot3(pair, (eh_ref[256:], el_ref[256:]))
        near_ref[pl.ds(0, 64, stride=2), :] = near_pairs
        near_ref[pl.ds(1, 64, stride=2), :] = near_pairs
        near = near + near_ref[...]
        near = jnp.where(gy == 0, pltpu.roll(near, 112, 1), near)
        near_ref[...] = near
    else:
        near_ref, keep_ref, send_ref, *scratch = refs
        near = near_ref[...]
    fh_ref, fl_ref, ch_ref, cl_ref, alpha_ref, pairs_ref = scratch
    on_left = (narrow < HALO) & (gy == 1)
    on_right = (narrow >= 128 - HALO) & (gy == 0)

    for g in range(4):
        fields = slice(16 * part + 4 * g, 16 * part + 4 * g + 4)
        u = dot_rows([r[fields].reshape(64, 256) for r in (above_ref, top_ref, bottom_ref, below_ref)])
        for t in range(2):
            at, lanes = slice(128 * g, 128 * g + 128), slice(256 * t, 256 * t + 256)
            fh_ref[at, lanes], fl_ref[at, lanes] = split(u[128 * t : 128 * t + 128])
            at = slice(64 * g, 64 * g + 64)
            ch_ref[at, lanes], cl_ref[at, lanes] = split(u[256 + 64 * t : 320 + 64 * t])

    alpha_ref[...] = dot3((fh_ref[...], fl_ref[...]), (right_ref[0, :512], right_ref[1, :512]))
    pairs = dot3((ch_ref[...], cl_ref[...]), (right_ref[0, 512:], right_ref[1, 512:]))
    for h in range(2):
        for s in range(2):
            pairs_ref[h, pl.ds(s, 256, stride=2), :] = pairs[:, 128 * h : 128 * h + 128]

    for g in range(4):
        at = slice(128 * g, 128 * g + 128)
        shift = (128 - 16 * (4 * part + g)) % 128
        moved = pltpu.roll(near, shift, 1) if shift else near
        zero = jnp.zeros_like(moved)
        low = pairs_ref[0, at] + jnp.where(on_left, moved, zero)
        high = pairs_ref[1, at] + jnp.where(on_right, moved, zero)
        alpha = alpha_ref[at] + jnp.concatenate([low, high], axis=1)
        first = 16 * part + 4 * g
        q = p_ref[first : first + 4] * alpha.reshape(4, 32, 256)
        for j in range(2):
            to = 4 * (g // 2) + lax.rem(2 * (g % 2) + j + 4 - z, 4)
            keep_ref[to] = jnp.where(core == 0, q[2 * j], q[2 * j + 1])
            send_ref[to] = jnp.where(core == 0, q[2 * j + 1], q[2 * j])


def call(kernel, outs, *args, hbm=(), scratch=(), cost=0, grant=16):
    args = [pltpu.with_memory_space_constraint(a, pltpu.HBM) if i in hbm else a for i, a in enumerate(args)]
    specs = [pl.BlockSpec(memory_space=pltpu.SMEM)] + [
        pl.BlockSpec(memory_space=pltpu.HBM) if i in hbm else VMEM for i in range(1, len(args))
    ]
    return pl.pallas_call(
        kernel,
        out_shape=[o if isinstance(o, jax.ShapeDtypeStruct) else jax.ShapeDtypeStruct(o, F32) for o in outs],
        in_specs=specs,
        out_specs=[VMEM] * len(outs),
        scratch_shapes=scratch,
        cost_estimate=pl.CostEstimate(flops=cost, bytes_accessed=1 << 20, transcendentals=0),
        compiler_params=pltpu.CompilerParams(vmem_limit_bytes=grant << 20),
    )(*args)


def body(perturbations, control):
    x, z, core, gx, gy = (lax.axis_index(a) for a in ("x", "z", "core", "gx", "gy"))
    where = jnp.stack([core, gx, gy, x, z]).astype(jnp.int32)
    left = jnp.asarray(halves(left_table(128, 4)))
    right, edge = (jnp.asarray(halves(t)) for t in right_tables(512, 2))
    vmem, sems = pltpu.VMEM, pltpu.SemaphoreType.DMA

    ring = lambda d: [(i, (i + d) % 4) for i in range(4)]
    swap = [(0, 1), (1, 0)]
    near_p, top, bottom = call(
        product_kernel, [(32, 32, 256)] + [(32, 16, 256)] * 2, where, perturbations, control, hbm=(1, 2),
        scratch=[vmem((32, 32, 256), F32), sems((2, 8))],
    )
    above = lax.ppermute(bottom, "gx", ring(1))
    below = lax.ppermute(top, "gx", ring(3))
    edges = call(edge_kernel, [(2, 32, 256)], where, top, bottom)[0]
    side = lax.ppermute(edges, "gy", swap)
    side_above = lax.ppermute(side[:, HALO:], "gx", ring(1))
    side_below = lax.ppermute(side[:, :HALO], "gx", ring(3))
    xh, xl, eh, el, right = call(
        table_kernel,
        [jax.ShapeDtypeStruct(s, BF16) for s in [(384, 256)] * 2 + [(512, 128)] * 2 + [(2, 1024, 256)]],
        where, left, edge, right, hbm=(3,), scratch=[sems((2, 4))],
    )
    piece = {}
    for part in range(2):
        extra = (side_above, side, side_below, eh, el) if part == 0 else (near,)
        keep, give, *rest = call(
            functools.partial(filter_kernel, part), [(8, 32, 256)] * 2 + [(128, 128)] * (part == 0),
            where, near_p, above, top, bottom, below, xh, xl, right, *extra,
            scratch=[vmem((512, 512), BF16)] * 2 + [vmem((256, 512), BF16)] * 2
            + [vmem((512, 256), F32), vmem((2, 512, 128), F32)],
            cost=2 * 10**9,
        )
        near = rest[0] if rest else None
        got = lax.ppermute(give, "core", swap)
        for i in range(2):
            piece[((2, 1), (3, 0))[part][i]] = keep[4 * i : 4 * i + 4] + got[4 * i : 4 * i + 4]
    x2, x1, x3 = (lax.ppermute(piece[d], "x", ring(d)) for d in (2, 1, 3))
    cell = [(piece[0][e : e + 1] + x2[e : e + 1]) + (x1[e : e + 1] + x3[e : e + 1]) for e in range(4)]
    z2, z1, z3 = (lax.ppermute(cell[e], "z", ring(e)) for e in (2, 1, 3))
    return ((cell[0] + z2) + (z1 + z3)) * (1.0 / 31.0)


def solution(mesh):
    grid = Mesh(mesh.devices.reshape(4, 4, 2, 4, 2), ("x", "z", "core", "gx", "gy"))
    mem = ("x", "z", "core")
    placed = (P(mem, None, "gx", "gy"), P(None, "gx", "gy"))
    return jax.shard_map(body, mesh=grid, in_specs=placed, out_specs=P(mem, "gx", "gy"), check_vma=False)
```

```python
import functools

import jax
import jax.numpy as jnp
import numpy as np
from jax import lax
from jax.experimental import pallas as pl
from jax.experimental.pallas import tpu as pltpu
from jax.sharding import Mesh, PartitionSpec as P


F32, BF16 = jnp.float32, jnp.bfloat16
HALO = 16
VMEM = pl.BlockSpec(memory_space=pltpu.VMEM)


def line_terms(size):
    offsets = np.arange(-4, 5)
    taps = np.exp(-offsets * offsets / 18.0)
    taps = taps / np.sqrt(np.sum(taps * taps))

    def banded(count):
        return sum(t * np.eye(count, k=o) for t, o in zip(taps, offsets))

    pairs = np.repeat(np.eye(size // 2), 2, axis=1) * np.sqrt(0.5)
    coarse = np.sqrt(0.5) * banded(size // 2) @ pairs
    return banded(size), np.repeat(coarse, 2, axis=0), coarse


def split(values):
    high = values.astype(BF16)
    return high, (values - high.astype(values.dtype)).astype(BF16)


def left_table(size, parts):
    fine, pair, coarse = line_terms(size)
    rows = size // parts
    tables = []
    for part in range(parts):
        terms = []
        for term in (fine @ fine, fine @ pair, coarse @ fine, coarse @ pair):
            count = term.shape[0] // parts
            wide = np.zeros((count, rows + 2 * HALO))
            for e in range(rows + 2 * HALO):
                source = part * rows - HALO + e
                if 0 <= source < size:
                    wide[:, e] = term[part * count : (part + 1) * count, source]
            segments = wide.reshape(count, 4, 1, HALO)
            terms.append(np.broadcast_to(segments, (count, 4, 4, HALO)).reshape(count, 256))
        tables.append(np.concatenate(terms))
    return np.stack(tables)


def right_tables(size, parts):
    fine, pair, _ = line_terms(size)
    columns = size // parts
    owns, sides = [], []
    for part in range(parts):
        own = slice(part * columns, (part + 1) * columns)
        edge = slice(columns, columns + HALO) if part == 0 else slice(columns - HALO, columns)
        near = slice(columns - HALO, columns) if part == 0 else slice(columns, columns + HALO)
        terms = (fine @ fine, pair @ fine, fine @ pair, pair @ pair)
        owns.append(np.concatenate([term[own, own] for term in terms]))
        sides.append(np.concatenate([np.tile(term[edge, near], (1, 8)) for term in terms]))
    return np.stack(owns), np.stack(sides)


def halves(table):
    high = table.astype(np.float32).astype(BF16)
    low = (table - high.astype(np.float64)).astype(np.float32).astype(BF16)
    return np.stack([high, low], axis=1)


def dot3(left, right):
    (lh, ll), (rh, rl) = left, right
    dot = lambda a, b: jnp.dot(a, b, preferred_element_type=F32)
    return dot(lh, rh) + (dot(lh, rl) + dot(ll, rh))


def block_of(where, k):
    return lax.rem(where[3] + (2, 1, 3, 0)[k], 4)


def product_kernel(where, p_hbm, c_hbm, p_ref, top_ref, bottom_ref, c_ref, sems):
    copies = []
    for k in range(4):
        for h in range(2):
            source, at = pl.ds(8 * block_of(where, k) + 4 * h, 4), pl.ds(8 * k + 4 * h, 4)
            copies.append(pltpu.make_async_copy(p_hbm.at[0, source], p_ref.at[at], sems.at[0, 2 * k + h]))
            copies.append(pltpu.make_async_copy(c_hbm.at[source], c_ref.at[at], sems.at[1, 2 * k + h]))
    for copy in copies:
        copy.start()
    for g in range(8):
        copies[2 * g].wait()
        copies[2 * g + 1].wait()
        at = slice(4 * g, 4 * g + 4)
        v = p_ref[at] * c_ref[at]
        top_ref[at] = v[:, :HALO]
        bottom_ref[at] = v[:, HALO:]


def edge_kernel(where, top_ref, bottom_ref, edge_ref):
    gy = where[2]
    lane = lax.broadcasted_iota(jnp.int32, (1, 1, 128), 2)
    for r_ref, rows in ((top_ref, slice(0, HALO)), (bottom_ref, slice(HALO, 2 * HALO))):
        edges = jnp.zeros((4, HALO, 128), F32)
        for g in range(8):
            at = slice(4 * g, 4 * g + 4)
            last = r_ref[at, :, 128:].reshape(64, 128)
            first = r_ref[at, :, :128].reshape(64, 128)
            v = jnp.where(gy == 0, pltpu.roll(last, 16, 1), first)
            if g:
                v = pltpu.roll(v, 16 * g, 1)
            edges = jnp.where(lane // 16 == g, v.reshape(4, HALO, 128), edges)
        for f in range(4):
            edge_ref[f // 2, rows, 128 * (f % 2) : 128 * (f % 2) + 128] = edges[f]


def table_kernel(
    where, left_ref, edge_ref, patch_ref, right_hbm, xh_ref, xl_ref, eh_ref, el_ref, right_ref, sems
):
    gx, gy = where[1], where[2]
    copies = []
    for h in range(2):
        for k in range(4):
            at = pl.ds(256 * k, 256)
            copies.append(pltpu.make_async_copy(right_hbm.at[h, at], right_ref.at[h, at], sems.at[h, k]))
    for copy in copies:
        copy.start()
    lane = lax.broadcasted_iota(jnp.int32, (1, 256), 1)
    narrow = lax.broadcasted_iota(jnp.int32, (1, 128), 1)
    for h, x_ref, e_ref in ((0, xh_ref, eh_ref), (1, xl_ref, el_ref)):
        row, start = 0, 0
        for count in (32, 32, 16, 16):
            rows = left_ref[gx, h, start : start + count].astype(F32)
            for f in range(4):
                mine = (lane // 16) % 4 == f
                x_ref[row : row + count] = jnp.where(mine, rows, jnp.zeros_like(rows)).astype(BF16)
                row += count
            start += count
        for t in range(4):
            rows = edge_ref[gy, h, 16 * t : 16 * t + 16].astype(F32)
            for g in range(8):
                at = 128 * t + 16 * g
                e_ref[at : at + 16] = jnp.where(narrow // 16 == g, rows, jnp.zeros_like(rows)).astype(BF16)
    for copy in copies:
        copy.wait()

    @pl.when(gy == 1)
    def _():
        for h in range(2):
            for t in range(4):
                right_ref[h, 256 * t : 256 * t + 32, :128] = patch_ref[h, 0, t]
                right_ref[h, 256 * t + 224 : 256 * t + 256, 128:] = patch_ref[h, 1, t]


def filter_kernel(
    part, where, p_ref, above_ref, top_ref, bottom_ref, below_ref, xh_ref, xl_ref, right_ref, *refs
):
    core, gy, z = where[0], where[2], where[4]
    dot_rows = lambda parts: dot3((xh_ref[...], xl_ref[...]), split(jnp.concatenate(parts)))
    narrow = lax.broadcasted_iota(jnp.int32, (1, 128), 1)
    if part == 0:
        side_above_ref, side_ref, side_below_ref, eh_ref, el_ref, keep_ref, send_ref, near_ref, *scratch = refs
        lanes = (slice(0, 128), slice(128, 256))
        sides = (side_above_ref, side_ref.at[:, :HALO], side_ref.at[:, HALO:], side_below_ref)
        side = dot_rows([s[f // 2, :, lanes[f % 2]] for s in sides for f in range(4)])
        fine = split(jnp.concatenate([side[:128], side[128:256]], axis=1))
        pair = split(jnp.concatenate([side[256:320], side[320:]], axis=1))
        near = dot3(fine, (eh_ref[:256], el_ref[:256]))
        near_pairs = dot3(pair, (eh_ref[256:], el_ref[256:]))
        near_ref[pl.ds(0, 64, stride=2), :] = near_pairs
        near_ref[pl.ds(1, 64, stride=2), :] = near_pairs
        near = near + near_ref[...]
        near = jnp.where(gy == 0, pltpu.roll(near, 112, 1), near)
        near_ref[...] = near
    else:
        near_ref, keep_ref, send_ref, *scratch = refs
        near = near_ref[...]
    fh_ref, fl_ref, ch_ref, cl_ref, alpha_ref, pairs_ref = scratch
    on_left = (narrow < HALO) & (gy == 1)
    on_right = (narrow >= 128 - HALO) & (gy == 0)

    for g in range(4):
        fields = slice(16 * part + 4 * g, 16 * part + 4 * g + 4)
        u = dot_rows([r[fields].reshape(64, 256) for r in (above_ref, top_ref, bottom_ref, below_ref)])
        for t in range(2):
            at, lanes = slice(128 * g, 128 * g + 128), slice(256 * t, 256 * t + 256)
            fh_ref[at, lanes], fl_ref[at, lanes] = split(u[128 * t : 128 * t + 128])
            at = slice(64 * g, 64 * g + 64)
            ch_ref[at, lanes], cl_ref[at, lanes] = split(u[256 + 64 * t : 320 + 64 * t])

    alpha_ref[...] = dot3((fh_ref[...], fl_ref[...]), (right_ref[0, :512], right_ref[1, :512]))
    pairs = dot3((ch_ref[...], cl_ref[...]), (right_ref[0, 512:], right_ref[1, 512:]))
    for h in range(2):
        for s in range(2):
            pairs_ref[h, pl.ds(s, 256, stride=2), :] = pairs[:, 128 * h : 128 * h + 128]

    for g in range(4):
        at = slice(128 * g, 128 * g + 128)
        shift = (128 - 16 * (4 * part + g)) % 128
        moved = pltpu.roll(near, shift, 1) if shift else near
        zero = jnp.zeros_like(moved)
        low = pairs_ref[0, at] + jnp.where(on_left, moved, zero)
        high = pairs_ref[1, at] + jnp.where(on_right, moved, zero)
        alpha = alpha_ref[at] + jnp.concatenate([low, high], axis=1)
        first = 16 * part + 4 * g
        q = p_ref[first : first + 4] * alpha.reshape(4, 32, 256)
        for j in range(2):
            to = 4 * (g // 2) + lax.rem(6 + z - (2 * (g % 2) + j), 4)
            keep_ref[to] = jnp.where(core == 0, q[2 * j], q[2 * j + 1])
            send_ref[to] = jnp.where(core == 0, q[2 * j + 1], q[2 * j])


def call(kernel, outs, *args, hbm=(), scratch=(), cost=0, grant=16):
    args = [pltpu.with_memory_space_constraint(a, pltpu.HBM) if i in hbm else a for i, a in enumerate(args)]
    specs = [pl.BlockSpec(memory_space=pltpu.SMEM)] + [
        pl.BlockSpec(memory_space=pltpu.HBM) if i in hbm else VMEM for i in range(1, len(args))
    ]
    return pl.pallas_call(
        kernel,
        out_shape=[o if isinstance(o, jax.ShapeDtypeStruct) else jax.ShapeDtypeStruct(o, F32) for o in outs],
        in_specs=specs,
        out_specs=[VMEM] * len(outs),
        scratch_shapes=scratch,
        cost_estimate=pl.CostEstimate(flops=cost, bytes_accessed=1 << 20, transcendentals=0),
        compiler_params=pltpu.CompilerParams(vmem_limit_bytes=grant << 20),
    )(*args)


def body(perturbations, control):
    x, z, core, gx, gy = (lax.axis_index(a) for a in ("x", "z", "core", "gx", "gy"))
    where = jnp.stack([core, gx, gy, x, z]).astype(jnp.int32)
    left = jnp.asarray(halves(left_table(128, 4)))
    right, edge = (halves(t) for t in right_tables(512, 2))
    blocks = right[1].reshape(2, 4, 256, 256)
    patch = jnp.asarray(np.stack([blocks[:, :, :32, :128], blocks[:, :, 224:, 128:]], axis=1))
    right, edge = jnp.asarray(right[0]), jnp.asarray(edge)
    vmem, sems = pltpu.VMEM, pltpu.SemaphoreType.DMA

    ring = lambda d: [(i, (i + d) % 4) for i in range(4)]
    swap = [(0, 1), (1, 0)]
    near_p, top, bottom = call(
        product_kernel, [(32, 32, 256)] + [(32, 16, 256)] * 2, where, perturbations, control, hbm=(1, 2),
        scratch=[vmem((32, 32, 256), F32), sems((2, 8))],
    )
    above = lax.ppermute(bottom, "gx", ring(1))
    below = lax.ppermute(top, "gx", ring(3))
    edges = call(edge_kernel, [(2, 32, 256)], where, top, bottom)[0]
    side = lax.ppermute(edges, "gy", swap)
    side_above = lax.ppermute(side[:, HALO:], "gx", ring(1))
    side_below = lax.ppermute(side[:, :HALO], "gx", ring(3))
    xh, xl, eh, el, right = call(
        table_kernel,
        [jax.ShapeDtypeStruct(s, BF16) for s in [(384, 256)] * 2 + [(512, 128)] * 2 + [(2, 1024, 256)]],
        where, left, edge, patch, right, hbm=(4,), scratch=[sems((2, 4))],
    )
    piece = {}
    for part in range(2):
        extra = (side_above, side, side_below, eh, el) if part == 0 else (near,)
        keep, give, *rest = call(
            functools.partial(filter_kernel, part), [(8, 32, 256)] * 2 + [(128, 128)] * (part == 0),
            where, near_p, above, top, bottom, below, xh, xl, right, *extra,
            scratch=[vmem((512, 512), BF16)] * 2 + [vmem((256, 512), BF16)] * 2
            + [vmem((512, 256), F32), vmem((2, 512, 128), F32)],
            cost=2 * 10**9,
        )
        near = rest[0] if rest else None
        got = lax.ppermute(give, "core", swap)
        for i in range(2):
            for wave in range(2):
                at = slice(4 * i + 2 * wave, 4 * i + 2 * wave + 2)
                piece[((2, 1), (3, 0))[part][i], wave] = keep[at] + got[at]
    waves = []
    for wave in range(2):
        x2, x1, x3 = (lax.ppermute(piece[d, wave], "x", ring(d)) for d in (2, 1, 3))
        waves.append([(piece[0, wave][i : i + 1] + x2[i : i + 1]) + (x1[i : i + 1] + x3[i : i + 1]) for i in range(2)])
    (far, next_), (own, last) = waves
    z2, z1, z3 = (lax.ppermute(cell, "z", ring(e)) for e, cell in ((2, far), (1, next_), (3, last)))
    return ((own + z2) + (z1 + z3)) * (1.0 / 31.0)


def solution(mesh):
    grid = Mesh(mesh.devices.reshape(4, 4, 2, 4, 2), ("x", "z", "core", "gx", "gy"))
    mem = ("x", "z", "core")
    placed = (P(mem, None, "gx", "gy"), P(None, "gx", "gy"))
    return jax.shard_map(body, mesh=grid, in_specs=placed, out_specs=P(mem, "gx", "gy"), check_vma=False)
```

```python
import functools

import jax
import jax.numpy as jnp
import numpy as np
from jax import lax
from jax.experimental import pallas as pl
from jax.experimental.pallas import tpu as pltpu
from jax.sharding import Mesh, PartitionSpec as P


F32, BF16 = jnp.float32, jnp.bfloat16
HALO = 16
VMEM = pl.BlockSpec(memory_space=pltpu.VMEM)


def line_terms(size):
    offsets = np.arange(-4, 5)
    taps = np.exp(-offsets * offsets / 18.0)
    taps = taps / np.sqrt(np.sum(taps * taps))

    def banded(count):
        return sum(t * np.eye(count, k=o) for t, o in zip(taps, offsets))

    pairs = np.repeat(np.eye(size // 2), 2, axis=1) * np.sqrt(0.5)
    coarse = np.sqrt(0.5) * banded(size // 2) @ pairs
    return banded(size), np.repeat(coarse, 2, axis=0), coarse


def split(values):
    high = values.astype(BF16)
    return high, (values - high.astype(values.dtype)).astype(BF16)


def left_table(size, parts):
    fine, pair, coarse = line_terms(size)
    rows = size // parts
    tables = []
    for part in range(parts):
        terms = []
        for term in (fine @ fine, fine @ pair, coarse @ fine, coarse @ pair):
            count = term.shape[0] // parts
            wide = np.zeros((count, rows + 2 * HALO))
            for e in range(rows + 2 * HALO):
                source = part * rows - HALO + e
                if 0 <= source < size:
                    wide[:, e] = term[part * count : (part + 1) * count, source]
            segments = wide.reshape(count, 4, 1, HALO)
            terms.append(np.broadcast_to(segments, (count, 4, 4, HALO)).reshape(count, 256))
        tables.append(np.concatenate(terms))
    return np.stack(tables)


def right_tables(size, parts):
    fine, pair, _ = line_terms(size)
    columns = size // parts
    owns, sides = [], []
    for part in range(parts):
        own = slice(part * columns, (part + 1) * columns)
        edge = slice(columns, columns + HALO) if part == 0 else slice(columns - HALO, columns)
        near = slice(columns - HALO, columns) if part == 0 else slice(columns, columns + HALO)
        terms = (fine @ fine, pair @ fine, fine @ pair, pair @ pair)
        owns.append(np.concatenate([term[own, own] for term in terms]))
        sides.append(np.concatenate([np.tile(term[edge, near], (1, 8)) for term in terms]))
    return np.stack(owns), np.stack(sides)


def halves(table):
    high = table.astype(np.float32).astype(BF16)
    low = (table - high.astype(np.float64)).astype(np.float32).astype(BF16)
    return np.stack([high, low], axis=1)


def dot3(left, right):
    (lh, ll), (rh, rl) = left, right
    dot = lambda a, b: jnp.dot(a, b, preferred_element_type=F32)
    return dot(lh, rh) + (dot(lh, rl) + dot(ll, rh))


def block_of(where, k):
    return lax.rem(where[3] + (2, 1, 3, 0)[k], 4)


def product_kernel(part, where, p_hbm, c_hbm, p_ref, top_ref, bottom_ref, c_ref, sems):
    copies = []
    for k in range(2):
        for h in range(2):
            source, at = pl.ds(8 * block_of(where, 2 * part + k) + 4 * h, 4), pl.ds(8 * k + 4 * h, 4)
            copies.append(pltpu.make_async_copy(p_hbm.at[0, source], p_ref.at[at], sems.at[0, 2 * k + h]))
            copies.append(pltpu.make_async_copy(c_hbm.at[source], c_ref.at[at], sems.at[1, 2 * k + h]))
    for copy in copies:
        copy.start()
    for g in range(4):
        copies[2 * g].wait()
        copies[2 * g + 1].wait()
        at = slice(4 * g, 4 * g + 4)
        v = p_ref[at] * c_ref[at]
        top_ref[at] = v[:, :HALO]
        bottom_ref[at] = v[:, HALO:]


def edge_kernel(where, top0_ref, bottom0_ref, top1_ref, bottom1_ref, edge_ref):
    gy = where[2]
    lane = lax.broadcasted_iota(jnp.int32, (1, 128), 1)
    near = pl.ds(pl.multiple_of(128 * (1 - gy), 128), 128)
    for refs, rows in (((top0_ref, top1_ref), slice(0, HALO)), ((bottom0_ref, bottom1_ref), slice(HALO, 2 * HALO))):
        edges = jnp.zeros((64, 128), F32)
        for g in range(8):
            at = slice(4 * (g % 4), 4 * (g % 4) + 4)
            v = refs[g // 4][at, :, near].reshape(64, 128)
            if g:
                v = pltpu.roll(v, 16 * g, 1)
            edges = jnp.where(lane // 16 == lax.rem(g + 7 * (1 - gy), 8), v, edges)
        for f in range(4):
            edge_ref[f // 2, rows, 128 * (f % 2) : 128 * (f % 2) + 128] = edges[16 * f : 16 * f + 16]


def table_kernel(
    where, left_ref, edge_ref, patch_ref, right_hbm, xh_ref, xl_ref, eh_ref, el_ref, right_ref, sems
):
    gx, gy = where[1], where[2]
    copies = []
    for h in range(2):
        for k in range(4):
            at = pl.ds(256 * k, 256)
            copies.append(pltpu.make_async_copy(right_hbm.at[h, at], right_ref.at[h, at], sems.at[h, k]))
    for copy in copies:
        copy.start()
    lane = lax.broadcasted_iota(jnp.int32, (1, 256), 1)
    narrow = lax.broadcasted_iota(jnp.int32, (1, 128), 1)
    for h, x_ref, e_ref in ((0, xh_ref, eh_ref), (1, xl_ref, el_ref)):
        row, start = 0, 0
        for count in (32, 32, 16, 16):
            rows = left_ref[gx, h, start : start + count].astype(F32)
            for f in range(4):
                mine = (lane // 16) % 4 == f
                x_ref[row : row + count] = jnp.where(mine, rows, jnp.zeros_like(rows)).astype(BF16)
                row += count
            start += count
        for t in range(4):
            rows = edge_ref[gy, h, 16 * t : 16 * t + 16].astype(F32)
            for g in range(8):
                at = 128 * t + 16 * g
                e_ref[at : at + 16] = jnp.where(narrow // 16 == g, rows, jnp.zeros_like(rows)).astype(BF16)
    for copy in copies:
        copy.wait()

    @pl.when(gy == 1)
    def _():
        for h in range(2):
            for t in range(4):
                right_ref[h, 256 * t : 256 * t + 32, :128] = patch_ref[h, 0, t]
                right_ref[h, 256 * t + 224 : 256 * t + 256, 128:] = patch_ref[h, 1, t]


def filter_kernel(
    part, where, p_ref, above_ref, top_ref, bottom_ref, below_ref, xh_ref, xl_ref, right_ref, *refs
):
    core, gy, z = where[0], where[2], where[4]
    dot_rows = lambda parts: dot3((xh_ref[...], xl_ref[...]), split(jnp.concatenate(parts)))
    narrow = lax.broadcasted_iota(jnp.int32, (1, 128), 1)
    if part == 0:
        side_above_ref, side_ref, side_below_ref, eh_ref, el_ref, keep_ref, send_ref, near_ref, *scratch = refs
        lanes = (slice(0, 128), slice(128, 256))
        sides = (side_above_ref, side_ref.at[:, :HALO], side_ref.at[:, HALO:], side_below_ref)
        side = dot_rows([s[f // 2, :, lanes[f % 2]] for s in sides for f in range(4)])
        fine = split(jnp.concatenate([side[:128], side[128:256]], axis=1))
        pair = split(jnp.concatenate([side[256:320], side[320:]], axis=1))
        near = dot3(fine, (eh_ref[:256], el_ref[:256]))
        near_pairs = dot3(pair, (eh_ref[256:], el_ref[256:]))
        near_ref[pl.ds(0, 64, stride=2), :] = near_pairs
        near_ref[pl.ds(1, 64, stride=2), :] = near_pairs
        near = near + near_ref[...]
        near = jnp.where(gy == 0, pltpu.roll(near, 112, 1), pltpu.roll(near, 16, 1))
        near_ref[...] = near
    else:
        near_ref, keep_ref, send_ref, *scratch = refs
        near = near_ref[...]
    fh_ref, fl_ref, ch_ref, cl_ref, alpha_ref, pairs_ref = scratch
    on_left = (narrow < HALO) & (gy == 1)
    on_right = (narrow >= 128 - HALO) & (gy == 0)

    for g in range(4):
        fields = slice(4 * g, 4 * g + 4)
        u = dot_rows([r[fields].reshape(64, 256) for r in (above_ref, top_ref, bottom_ref, below_ref)])
        for t in range(2):
            at, lanes = slice(128 * g, 128 * g + 128), slice(256 * t, 256 * t + 256)
            fh_ref[at, lanes], fl_ref[at, lanes] = split(u[128 * t : 128 * t + 128])
            at = slice(64 * g, 64 * g + 64)
            ch_ref[at, lanes], cl_ref[at, lanes] = split(u[256 + 64 * t : 320 + 64 * t])

    alpha_ref[...] = dot3((fh_ref[...], fl_ref[...]), (right_ref[0, :512], right_ref[1, :512]))
    pairs = dot3((ch_ref[...], cl_ref[...]), (right_ref[0, 512:], right_ref[1, 512:]))
    for h in range(2):
        for s in range(2):
            pairs_ref[h, pl.ds(s, 256, stride=2), :] = pairs[:, 128 * h : 128 * h + 128]

    for g in range(4):
        at = slice(128 * g, 128 * g + 128)
        shift = (128 - 16 * (4 * part + g)) % 128
        moved = pltpu.roll(near, shift, 1) if shift else near
        zero = jnp.zeros_like(moved)
        low = pairs_ref[0, at] + jnp.where(on_left, moved, zero)
        high = pairs_ref[1, at] + jnp.where(on_right, moved, zero)
        alpha = alpha_ref[at] + jnp.concatenate([low, high], axis=1)
        q = p_ref[4 * g : 4 * g + 4] * alpha.reshape(4, 32, 256)
        for j in range(2):
            to = 4 * (g // 2) + lax.rem(6 + z - (2 * (g % 2) + j), 4)
            keep_ref[to] = jnp.where(core == 0, q[2 * j], q[2 * j + 1])
            send_ref[to] = jnp.where(core == 0, q[2 * j + 1], q[2 * j])


def call(kernel, outs, *args, hbm=(), scratch=(), cost=0, grant=16):
    args = [pltpu.with_memory_space_constraint(a, pltpu.HBM) if i in hbm else a for i, a in enumerate(args)]
    specs = [pl.BlockSpec(memory_space=pltpu.SMEM)] + [
        pl.BlockSpec(memory_space=pltpu.HBM) if i in hbm else VMEM for i in range(1, len(args))
    ]
    return pl.pallas_call(
        kernel,
        out_shape=[o if isinstance(o, jax.ShapeDtypeStruct) else jax.ShapeDtypeStruct(o, F32) for o in outs],
        in_specs=specs,
        out_specs=[VMEM] * len(outs),
        scratch_shapes=scratch,
        cost_estimate=pl.CostEstimate(flops=cost, bytes_accessed=1 << 20, transcendentals=0),
        compiler_params=pltpu.CompilerParams(vmem_limit_bytes=grant << 20),
    )(*args)


def body(perturbations, control):
    x, z, core, gx, gy = (lax.axis_index(a) for a in ("x", "z", "core", "gx", "gy"))
    where = jnp.stack([core, gx, gy, x, z]).astype(jnp.int32)
    left = jnp.asarray(halves(left_table(128, 4)))
    right, edge = (halves(t) for t in right_tables(512, 2))
    blocks = right[1].reshape(2, 4, 256, 256)
    patch = jnp.asarray(np.stack([blocks[:, :, :32, :128], blocks[:, :, 224:, 128:]], axis=1))
    right, edge = jnp.asarray(right[0]), jnp.asarray(edge)
    vmem, sems = pltpu.VMEM, pltpu.SemaphoreType.DMA

    ring = lambda d: [(i, (i + d) % 4) for i in range(4)]
    swap = [(0, 1), (1, 0)]
    ps, tops, bottoms, aboves, belows = [], [], [], [], []
    for part in range(2):
        p, top, bottom = call(
            functools.partial(product_kernel, part), [(16, 32, 256)] + [(16, 16, 256)] * 2,
            where, perturbations, control, hbm=(1, 2), scratch=[vmem((16, 32, 256), F32), sems((2, 4))],
        )
        ps.append(p)
        tops.append(top)
        bottoms.append(bottom)
        aboves.append(lax.ppermute(bottom, "gx", ring(1)))
        belows.append(lax.ppermute(top, "gx", ring(3)))
    edges = call(edge_kernel, [(2, 32, 256)], where, tops[0], bottoms[0], tops[1], bottoms[1])[0]
    side = lax.ppermute(edges, "gy", swap)
    side_above = lax.ppermute(side[:, HALO:], "gx", ring(1))
    side_below = lax.ppermute(side[:, :HALO], "gx", ring(3))
    xh, xl, eh, el, right = call(
        table_kernel,
        [jax.ShapeDtypeStruct(s, BF16) for s in [(384, 256)] * 2 + [(512, 128)] * 2 + [(2, 1024, 256)]],
        where, left, edge, patch, right, hbm=(4,), scratch=[sems((2, 4))],
    )
    piece = {}
    for part in range(2):
        extra = (side_above, side, side_below, eh, el) if part == 0 else (near,)
        keep, give, *rest = call(
            functools.partial(filter_kernel, part), [(8, 32, 256)] * 2 + [(128, 128)] * (part == 0),
            where, ps[part], aboves[part], tops[part], bottoms[part], belows[part], xh, xl, right, *extra,
            scratch=[vmem((512, 512), BF16)] * 2 + [vmem((256, 512), BF16)] * 2
            + [vmem((512, 256), F32), vmem((2, 512, 128), F32)],
            cost=2 * 10**9,
        )
        near = rest[0] if rest else None
        got = lax.ppermute(give, "core", swap)
        for i in range(2):
            for wave in range(2):
                at = slice(4 * i + 2 * wave, 4 * i + 2 * wave + 2)
                piece[((2, 1), (3, 0))[part][i], wave] = keep[at] + got[at]
    waves = []
    for wave in range(2):
        x2, x1, x3 = (lax.ppermute(piece[d, wave], "x", ring(d)) for d in (2, 1, 3))
        waves.append([(piece[0, wave][i : i + 1] + x2[i : i + 1]) + (x1[i : i + 1] + x3[i : i + 1]) for i in range(2)])
    (far, next_), (own, last) = waves
    z2, z1, z3 = (lax.ppermute(cell, "z", ring(e)) for e, cell in ((2, far), (1, next_), (3, last)))
    return ((own + z2) + (z1 + z3)) * (1.0 / 31.0)


def solution(mesh):
    grid = Mesh(mesh.devices.reshape(4, 4, 2, 4, 2), ("x", "z", "core", "gx", "gy"))
    mem = ("x", "z", "core")
    placed = (P(mem, None, "gx", "gy"), P(None, "gx", "gy"))
    return jax.shard_map(body, mesh=grid, in_specs=placed, out_specs=P(mem, "gx", "gy"), check_vma=False)
```

```python
import functools

import jax
import jax.numpy as jnp
import numpy as np
from jax import lax
from jax.experimental import pallas as pl
from jax.experimental.pallas import tpu as pltpu
from jax.sharding import Mesh, PartitionSpec as P


F32, BF16 = jnp.float32, jnp.bfloat16
HALO = 16
VMEM = pl.BlockSpec(memory_space=pltpu.VMEM)


def line_terms(size):
    offsets = np.arange(-4, 5)
    taps = np.exp(-offsets * offsets / 18.0)
    taps = taps / np.sqrt(np.sum(taps * taps))

    def banded(count):
        return sum(t * np.eye(count, k=o) for t, o in zip(taps, offsets))

    pairs = np.repeat(np.eye(size // 2), 2, axis=1) * np.sqrt(0.5)
    coarse = np.sqrt(0.5) * banded(size // 2) @ pairs
    return banded(size), np.repeat(coarse, 2, axis=0), coarse


def split(values):
    high = values.astype(BF16)
    return high, (values - high.astype(values.dtype)).astype(BF16)


def left_table(size, parts):
    fine, pair, coarse = line_terms(size)
    rows = size // parts
    tables = []
    for part in range(parts):
        terms = []
        for term in (fine @ fine, fine @ pair, coarse @ fine, coarse @ pair):
            count = term.shape[0] // parts
            wide = np.zeros((count, rows + 2 * HALO))
            for e in range(rows + 2 * HALO):
                source = part * rows - HALO + e
                if 0 <= source < size:
                    wide[:, e] = term[part * count : (part + 1) * count, source]
            terms.append(wide)
        tables.append(np.concatenate(terms))
    return np.stack(tables)


def right_tables(size, parts):
    fine, pair, _ = line_terms(size)
    columns = size // parts
    owns, sides = [], []
    for part in range(parts):
        own = slice(part * columns, (part + 1) * columns)
        edge = slice(columns, columns + HALO) if part == 0 else slice(columns - HALO, columns)
        near = slice(columns - HALO, columns) if part == 0 else slice(columns, columns + HALO)
        terms = (fine @ fine, pair @ fine, fine @ pair, pair @ pair)
        owns.append(np.concatenate([term[own, own] for term in terms]))
        sides.append(np.concatenate([np.tile(term[edge, near], (1, 8)) for term in terms]))
    return np.stack(owns), np.stack(sides)


def halves(table):
    high = table.astype(np.float32).astype(BF16)
    low = (table - high.astype(np.float64)).astype(np.float32).astype(BF16)
    return np.stack([high, low], axis=1)


def dot3(left, right):
    (lh, ll), (rh, rl) = left, right
    dot = lambda a, b: jnp.dot(a, b, preferred_element_type=F32)
    return dot(lh, rh) + (dot(lh, rl) + dot(ll, rh))


def block_of(where, k):
    return lax.rem(where[3] + (2, 1, 3, 0)[k], 4)


def product_kernel(where, p_hbm, c_hbm, p_ref, top_ref, bottom_ref, c_ref, sems):
    copies = []
    for k in range(4):
        for h in range(2):
            source, at = pl.ds(8 * block_of(where, k) + 4 * h, 4), pl.ds(8 * k + 4 * h, 4)
            copies.append(pltpu.make_async_copy(p_hbm.at[0, source], p_ref.at[at], sems.at[0, 2 * k + h]))
            copies.append(pltpu.make_async_copy(c_hbm.at[source], c_ref.at[at], sems.at[1, 2 * k + h]))
    for copy in copies:
        copy.start()
    for g in range(8):
        copies[2 * g].wait()
        copies[2 * g + 1].wait()
        at = slice(4 * g, 4 * g + 4)
        v = p_ref[at] * c_ref[at]
        top_ref[at] = v[:, :HALO]
        bottom_ref[at] = v[:, HALO:]


def edge_kernel(where, top_ref, bottom_ref, edge_ref):
    gy = where[2]
    lane = lax.broadcasted_iota(jnp.int32, (1, 128), 1)
    near = pl.ds(pl.multiple_of(128 * (1 - gy), 128), 128)
    for r_ref, rows in ((top_ref, slice(0, HALO)), (bottom_ref, slice(HALO, 2 * HALO))):
        edges = jnp.zeros((64, 128), F32)
        for g in range(8):
            v = r_ref[4 * g : 4 * g + 4, :, near].reshape(64, 128)
            if g:
                v = pltpu.roll(v, 16 * g, 1)
            edges = jnp.where(lane // 16 == lax.rem(g + 7 * (1 - gy), 8), v, edges)
        for f in range(4):
            edge_ref[f // 2, rows, 128 * (f % 2) : 128 * (f % 2) + 128] = edges[16 * f : 16 * f + 16]


def table_kernel(
    where, edge_ref, patch_ref, right_hbm, eh_ref, el_ref, right_ref, sems
):
    gy = where[2]
    copies = []
    for h in range(2):
        for k in range(4):
            at = pl.ds(256 * k, 256)
            copies.append(pltpu.make_async_copy(right_hbm.at[h, at], right_ref.at[h, at], sems.at[h, k]))
    for copy in copies:
        copy.start()
    narrow = lax.broadcasted_iota(jnp.int32, (1, 128), 1)
    for h, e_ref in ((0, eh_ref), (1, el_ref)):
        for t in range(4):
            rows = edge_ref[gy, h, 16 * t : 16 * t + 16].astype(F32)
            for g in range(8):
                at = 128 * t + 16 * g
                e_ref[at : at + 16] = jnp.where(narrow // 16 == g, rows, jnp.zeros_like(rows)).astype(BF16)
    for copy in copies:
        copy.wait()

    @pl.when(gy == 1)
    def _():
        for h in range(2):
            for t in range(4):
                right_ref[h, 256 * t : 256 * t + 32, :128] = patch_ref[h, 0, t]
                right_ref[h, 256 * t + 224 : 256 * t + 256, 128:] = patch_ref[h, 1, t]


def filter_kernel(
    part, where, p_ref, above_ref, top_ref, bottom_ref, below_ref, left_ref, right_ref, *refs
):
    core, gy, z = where[0], where[2], where[4]
    left = left_ref[where[1]]

    def dot_rows(parts):
        high, low = split(jnp.concatenate(parts))
        return jnp.dot(left, jnp.concatenate([high, high, low]), preferred_element_type=F32)

    narrow = lax.broadcasted_iota(jnp.int32, (1, 128), 1)
    if part == 0:
        side_above_ref, side_ref, side_below_ref, eh_ref, el_ref, keep_ref, send_ref, near_ref, *scratch = refs
        lanes = (slice(0, 128), slice(128, 256))
        sides = (side_above_ref, side_ref.at[:, :HALO], side_ref.at[:, HALO:], side_below_ref)
        side = [dot_rows([s[f // 2, :, lanes[f % 2]] for s in sides]) for f in range(4)]
        fine = split(jnp.concatenate([jnp.concatenate([u[:32], u[32:64]], axis=1) for u in side]))
        pair = split(jnp.concatenate([jnp.concatenate([u[64:80], u[80:]], axis=1) for u in side]))
        near = dot3(fine, (eh_ref[:256], el_ref[:256]))
        near_pairs = dot3(pair, (eh_ref[256:], el_ref[256:]))
        near_ref[pl.ds(0, 64, stride=2), :] = near_pairs
        near_ref[pl.ds(1, 64, stride=2), :] = near_pairs
        near = near + near_ref[...]
        near = jnp.where(gy == 0, pltpu.roll(near, 112, 1), pltpu.roll(near, 16, 1))
        near_ref[...] = near
    else:
        near_ref, keep_ref, send_ref, *scratch = refs
        near = near_ref[...]
    fh_ref, fl_ref, ch_ref, cl_ref, alpha_ref, pairs_ref = scratch
    on_left = (narrow < HALO) & (gy == 1)
    on_right = (narrow >= 128 - HALO) & (gy == 0)

    for f in range(16):
        u = dot_rows([r[16 * part + f] for r in (above_ref, top_ref, bottom_ref, below_ref)])
        for t in range(2):
            at, lanes = slice(32 * f, 32 * f + 32), slice(256 * t, 256 * t + 256)
            fh_ref[at, lanes], fl_ref[at, lanes] = split(u[32 * t : 32 * t + 32])
            at = slice(16 * f, 16 * f + 16)
            ch_ref[at, lanes], cl_ref[at, lanes] = split(u[64 + 16 * t : 80 + 16 * t])

    alpha_ref[...] = dot3((fh_ref[...], fl_ref[...]), (right_ref[0, :512], right_ref[1, :512]))
    pairs = dot3((ch_ref[...], cl_ref[...]), (right_ref[0, 512:], right_ref[1, 512:]))
    for h in range(2):
        for s in range(2):
            pairs_ref[h, pl.ds(s, 256, stride=2), :] = pairs[:, 128 * h : 128 * h + 128]

    for g in range(4):
        at = slice(128 * g, 128 * g + 128)
        shift = (128 - 16 * (4 * part + g)) % 128
        moved = pltpu.roll(near, shift, 1) if shift else near
        zero = jnp.zeros_like(moved)
        low = pairs_ref[0, at] + jnp.where(on_left, moved, zero)
        high = pairs_ref[1, at] + jnp.where(on_right, moved, zero)
        alpha = alpha_ref[at] + jnp.concatenate([low, high], axis=1)
        first = 16 * part + 4 * g
        q = p_ref[first : first + 4] * alpha.reshape(4, 32, 256)
        for j in range(2):
            to = 4 * (g // 2) + lax.rem(6 + z - (2 * (g % 2) + j), 4)
            keep_ref[to] = jnp.where(core == 0, q[2 * j], q[2 * j + 1])
            send_ref[to] = jnp.where(core == 0, q[2 * j + 1], q[2 * j])


def call(kernel, outs, *args, hbm=(), scratch=(), cost=0, grant=16):
    args = [pltpu.with_memory_space_constraint(a, pltpu.HBM) if i in hbm else a for i, a in enumerate(args)]
    specs = [pl.BlockSpec(memory_space=pltpu.SMEM)] + [
        pl.BlockSpec(memory_space=pltpu.HBM) if i in hbm else VMEM for i in range(1, len(args))
    ]
    return pl.pallas_call(
        kernel,
        out_shape=[o if isinstance(o, jax.ShapeDtypeStruct) else jax.ShapeDtypeStruct(o, F32) for o in outs],
        in_specs=specs,
        out_specs=[VMEM] * len(outs),
        scratch_shapes=scratch,
        cost_estimate=pl.CostEstimate(flops=cost, bytes_accessed=1 << 20, transcendentals=0),
        compiler_params=pltpu.CompilerParams(vmem_limit_bytes=grant << 20),
    )(*args)


def body(perturbations, control):
    x, z, core, gx, gy = (lax.axis_index(a) for a in ("x", "z", "core", "gx", "gy"))
    where = jnp.stack([core, gx, gy, x, z]).astype(jnp.int32)
    high, low = np.moveaxis(halves(left_table(128, 4)), 1, 0)
    left = jnp.asarray(np.concatenate([high, low, high], axis=2))
    right, edge = (halves(t) for t in right_tables(512, 2))
    blocks = right[1].reshape(2, 4, 256, 256)
    patch = jnp.asarray(np.stack([blocks[:, :, :32, :128], blocks[:, :, 224:, 128:]], axis=1))
    right, edge = jnp.asarray(right[0]), jnp.asarray(edge)
    vmem, sems = pltpu.VMEM, pltpu.SemaphoreType.DMA

    ring = lambda d: [(i, (i + d) % 4) for i in range(4)]
    swap = [(0, 1), (1, 0)]
    near_p, top, bottom = call(
        product_kernel, [(32, 32, 256)] + [(32, 16, 256)] * 2, where, perturbations, control, hbm=(1, 2),
        scratch=[vmem((32, 32, 256), F32), sems((2, 8))],
    )
    above = lax.ppermute(bottom, "gx", ring(1))
    below = lax.ppermute(top, "gx", ring(3))
    edges = call(edge_kernel, [(2, 32, 256)], where, top, bottom)[0]
    side = lax.ppermute(edges, "gy", swap)
    side_above = lax.ppermute(side[:, HALO:], "gx", ring(1))
    side_below = lax.ppermute(side[:, :HALO], "gx", ring(3))
    eh, el, right = call(
        table_kernel, [jax.ShapeDtypeStruct(s, BF16) for s in [(512, 128)] * 2 + [(2, 1024, 256)]],
        where, edge, patch, right, hbm=(3,), scratch=[sems((2, 4))],
    )
    piece = {}
    for part in range(2):
        extra = (side_above, side, side_below, eh, el) if part == 0 else (near,)
        keep, give, *rest = call(
            functools.partial(filter_kernel, part), [(8, 32, 256)] * 2 + [(128, 128)] * (part == 0),
            where, near_p, above, top, bottom, below, left, right, *extra,
            scratch=[vmem((512, 512), BF16)] * 2 + [vmem((256, 512), BF16)] * 2
            + [vmem((512, 256), F32), vmem((2, 512, 128), F32)],
            cost=2 * 10**9,
        )
        near = rest[0] if rest else None
        got = lax.ppermute(give, "core", swap)
        for i in range(2):
            for wave in range(2):
                at = slice(4 * i + 2 * wave, 4 * i + 2 * wave + 2)
                piece[((2, 1), (3, 0))[part][i], wave] = keep[at] + got[at]
    waves = []
    for wave in range(2):
        x2, x1, x3 = (lax.ppermute(piece[d, wave], "x", ring(d)) for d in (2, 1, 3))
        waves.append([(piece[0, wave][i : i + 1] + x2[i : i + 1]) + (x1[i : i + 1] + x3[i : i + 1]) for i in range(2)])
    (far, next_), (own, last) = waves
    z2, z1, z3 = (lax.ppermute(cell, "z", ring(e)) for e, cell in ((2, far), (1, next_), (3, last)))
    return ((own + z2) + (z1 + z3)) * (1.0 / 31.0)


def solution(mesh):
    grid = Mesh(mesh.devices.reshape(4, 4, 2, 4, 2), ("x", "z", "core", "gx", "gy"))
    mem = ("x", "z", "core")
    placed = (P(mem, None, "gx", "gy"), P(None, "gx", "gy"))
    return jax.shard_map(body, mesh=grid, in_specs=placed, out_specs=P(mem, "gx", "gy"), check_vma=False)
```

```python
import functools

import jax
import jax.numpy as jnp
import numpy as np
from jax import lax
from jax.experimental import pallas as pl
from jax.experimental.pallas import tpu as pltpu
from jax.sharding import Mesh, PartitionSpec as P


F32, BF16 = jnp.float32, jnp.bfloat16
HALO = 16
VMEM = pl.BlockSpec(memory_space=pltpu.VMEM)


def line_terms(size):
    offsets = np.arange(-4, 5)
    taps = np.exp(-offsets * offsets / 18.0)
    taps = taps / np.sqrt(np.sum(taps * taps))

    def banded(count):
        return sum(t * np.eye(count, k=o) for t, o in zip(taps, offsets))

    pairs = np.repeat(np.eye(size // 2), 2, axis=1) * np.sqrt(0.5)
    coarse = np.sqrt(0.5) * banded(size // 2) @ pairs
    return banded(size), np.repeat(coarse, 2, axis=0), coarse


def split(values):
    high = values.astype(BF16)
    return high, (values - high.astype(values.dtype)).astype(BF16)


def left_table(size, parts):
    fine, pair, coarse = line_terms(size)
    rows = size // parts
    tables = []
    for part in range(parts):
        terms = []
        for term in (fine @ fine, fine @ pair, coarse @ fine, coarse @ pair):
            count = term.shape[0] // parts
            wide = np.zeros((count, rows + 2 * HALO))
            for e in range(rows + 2 * HALO):
                source = part * rows - HALO + e
                if 0 <= source < size:
                    wide[:, e] = term[part * count : (part + 1) * count, source]
            terms.append(wide)
        tables.append(np.concatenate(terms))
    return np.stack(tables)


def right_tables(size, parts):
    fine, pair, _ = line_terms(size)
    columns = size // parts
    owns, sides = [], []
    for part in range(parts):
        own = slice(part * columns, (part + 1) * columns)
        edge = slice(columns, columns + HALO) if part == 0 else slice(columns - HALO, columns)
        near = slice(columns - HALO, columns) if part == 0 else slice(columns, columns + HALO)
        terms = (fine @ fine, pair @ fine, fine @ pair, pair @ pair)
        owns.append(np.concatenate([term[own, own] for term in terms]))
        sides.append(np.concatenate([np.tile(term[edge, near], (1, 8)) for term in terms]))
    return np.stack(owns), np.stack(sides)


def halves(table):
    high = table.astype(np.float32).astype(BF16)
    low = (table - high.astype(np.float64)).astype(np.float32).astype(BF16)
    return np.stack([high, low], axis=1)


def dot3(left, right):
    (lh, ll), (rh, rl) = left, right
    dot = lambda a, b: jnp.dot(a, b, preferred_element_type=F32)
    return dot(lh, rh) + (dot(lh, rl) + dot(ll, rh))


def block_of(where, k):
    return lax.rem(where[3] + (2, 1, 3, 0)[k], 4)


def product_kernel(where, p_hbm, c_hbm, p_ref, top_ref, bottom_ref, c_ref, sems):
    copies = []
    for k in range(4):
        for h in range(2):
            source, at = pl.ds(8 * block_of(where, k) + 4 * h, 4), pl.ds(8 * k + 4 * h, 4)
            copies.append(pltpu.make_async_copy(p_hbm.at[0, source], p_ref.at[at], sems.at[0, 2 * k + h]))
            copies.append(pltpu.make_async_copy(c_hbm.at[source], c_ref.at[at], sems.at[1, 2 * k + h]))
    for copy in copies:
        copy.start()
    for g in range(8):
        copies[2 * g].wait()
        copies[2 * g + 1].wait()
        at = slice(4 * g, 4 * g + 4)
        v = p_ref[at] * c_ref[at]
        top_ref[at] = v[:, :HALO]
        bottom_ref[at] = v[:, HALO:]


def edge_kernel(where, top_ref, bottom_ref, edge_ref):
    gy = where[2]
    lane = lax.broadcasted_iota(jnp.int32, (1, 128), 1)
    near = pl.ds(pl.multiple_of(128 * (1 - gy), 128), 128)
    for r_ref, rows in ((top_ref, slice(0, HALO)), (bottom_ref, slice(HALO, 2 * HALO))):
        edges = jnp.zeros((64, 128), F32)
        for g in range(8):
            v = r_ref[4 * g : 4 * g + 4, :, near].reshape(64, 128)
            if g:
                v = pltpu.roll(v, 16 * g, 1)
            edges = jnp.where(lane // 16 == lax.rem(g + 7 * (1 - gy), 8), v, edges)
        for f in range(4):
            edge_ref[f // 2, rows, 128 * (f % 2) : 128 * (f % 2) + 128] = edges[16 * f : 16 * f + 16]


def table_kernel(
    where, edge_ref, patch_ref, right_hbm, eh_ref, el_ref, right_ref, sems
):
    gy = where[2]
    copies = []
    for h in range(2):
        for k in range(4):
            at = pl.ds(256 * k, 256)
            copies.append(pltpu.make_async_copy(right_hbm.at[h, at], right_ref.at[h, at], sems.at[h, k]))
    for copy in copies:
        copy.start()
    narrow = lax.broadcasted_iota(jnp.int32, (1, 128), 1)
    for h, e_ref in ((0, eh_ref), (1, el_ref)):
        for t in range(4):
            rows = edge_ref[gy, h, 16 * t : 16 * t + 16].astype(F32)
            for g in range(8):
                at = 128 * t + 16 * g
                e_ref[at : at + 16] = jnp.where(narrow // 16 == g, rows, jnp.zeros_like(rows)).astype(BF16)
    for copy in copies:
        copy.wait()

    @pl.when(gy == 1)
    def _():
        for h in range(2):
            for t in range(4):
                right_ref[h, 256 * t : 256 * t + 32, :128] = patch_ref[h, 0, t]
                right_ref[h, 256 * t + 224 : 256 * t + 256, 128:] = patch_ref[h, 1, t]


def filter_kernel(
    part, where, p_ref, above_ref, top_ref, bottom_ref, below_ref, left_ref, right_ref, *refs
):
    core, gy, z = where[0], where[2], where[4]
    left = left_ref[where[1]]

    def dot_rows(parts):
        high, low = split(jnp.concatenate(parts))
        return jnp.dot(left, jnp.concatenate([high, high, low]), preferred_element_type=F32)

    narrow = lax.broadcasted_iota(jnp.int32, (1, 128), 1)
    if part == 0:
        side_above_ref, side_ref, side_below_ref, eh_ref, el_ref, keep_ref, send_ref, near_ref, *scratch = refs
        lanes = (slice(0, 128), slice(128, 256))
        sides = (side_above_ref, side_ref.at[:, :HALO], side_ref.at[:, HALO:], side_below_ref)
        side = [dot_rows([s[f // 2, :, lanes[f % 2]] for s in sides]) for f in range(4)]
        fine = split(jnp.concatenate([jnp.concatenate([u[:32], u[32:64]], axis=1) for u in side]))
        pair = split(jnp.concatenate([jnp.concatenate([u[64:80], u[80:]], axis=1) for u in side]))
        near = dot3(fine, (eh_ref[:256], el_ref[:256]))
        near_pairs = dot3(pair, (eh_ref[256:], el_ref[256:]))
        near_ref[pl.ds(0, 64, stride=2), :] = near_pairs
        near_ref[pl.ds(1, 64, stride=2), :] = near_pairs
        near = near + near_ref[...]
        near = jnp.where(gy == 0, pltpu.roll(near, 112, 1), pltpu.roll(near, 16, 1))
        near_ref[...] = near
    else:
        near_ref, keep_ref, send_ref, *scratch = refs
        near = near_ref[...]
    fh_ref, fl_ref, ch_ref, cl_ref, alpha_ref, pairs_ref = scratch
    on_left = (narrow < HALO) & (gy == 1)
    on_right = (narrow >= 128 - HALO) & (gy == 0)

    for f in range(16):
        u = dot_rows([r[16 * part + f] for r in (above_ref, top_ref, bottom_ref, below_ref)])
        for t in range(2):
            at, lanes = slice(32 * f, 32 * f + 32), slice(256 * t, 256 * t + 256)
            fh_ref[at, lanes], fl_ref[at, lanes] = split(u[32 * t : 32 * t + 32])
            at = slice(16 * f, 16 * f + 16)
            ch_ref[at, lanes], cl_ref[at, lanes] = split(u[64 + 16 * t : 80 + 16 * t])

    alpha_ref[...] = dot3((fh_ref[...], fl_ref[...]), (right_ref[0, :512], right_ref[1, :512]))
    pairs = dot3((ch_ref[...], cl_ref[...]), (right_ref[0, 512:], right_ref[1, 512:]))
    for h in range(2):
        for s in range(2):
            pairs_ref[h, pl.ds(s, 256, stride=2), :] = pairs[:, 128 * h : 128 * h + 128]

    for g in range(4):
        at = slice(128 * g, 128 * g + 128)
        shift = (128 - 16 * (4 * part + g)) % 128
        moved = pltpu.roll(near, shift, 1) if shift else near
        zero = jnp.zeros_like(moved)
        low = pairs_ref[0, at] + jnp.where(on_left, moved, zero)
        high = pairs_ref[1, at] + jnp.where(on_right, moved, zero)
        alpha = alpha_ref[at] + jnp.concatenate([low, high], axis=1)
        first = 16 * part + 4 * g
        q = p_ref[first : first + 4] * alpha.reshape(4, 32, 256)
        for j in range(2):
            e = lax.rem(2 * (g % 2) + j + 4 - z, 4)
            odd, half = lax.rem(e, 2), lax.div(e, 2)
            to = 4 * (g // 2) + odd * half + (1 - odd) * (3 - half)
            keep_ref[to] = jnp.where(core == 0, q[2 * j], q[2 * j + 1])
            send_ref[to] = jnp.where(core == 0, q[2 * j + 1], q[2 * j])


def call(kernel, outs, *args, hbm=(), scratch=(), cost=0, grant=16):
    args = [pltpu.with_memory_space_constraint(a, pltpu.HBM) if i in hbm else a for i, a in enumerate(args)]
    specs = [pl.BlockSpec(memory_space=pltpu.SMEM)] + [
        pl.BlockSpec(memory_space=pltpu.HBM) if i in hbm else VMEM for i in range(1, len(args))
    ]
    return pl.pallas_call(
        kernel,
        out_shape=[o if isinstance(o, jax.ShapeDtypeStruct) else jax.ShapeDtypeStruct(o, F32) for o in outs],
        in_specs=specs,
        out_specs=[VMEM] * len(outs),
        scratch_shapes=scratch,
        cost_estimate=pl.CostEstimate(flops=cost, bytes_accessed=1 << 20, transcendentals=0),
        compiler_params=pltpu.CompilerParams(vmem_limit_bytes=grant << 20),
    )(*args)


def body(perturbations, control):
    x, z, core, gx, gy = (lax.axis_index(a) for a in ("x", "z", "core", "gx", "gy"))
    where = jnp.stack([core, gx, gy, x, z]).astype(jnp.int32)
    high, low = np.moveaxis(halves(left_table(128, 4)), 1, 0)
    left = jnp.asarray(np.concatenate([high, low, high], axis=2))
    right, edge = (halves(t) for t in right_tables(512, 2))
    blocks = right[1].reshape(2, 4, 256, 256)
    patch = jnp.asarray(np.stack([blocks[:, :, :32, :128], blocks[:, :, 224:, 128:]], axis=1))
    right, edge = jnp.asarray(right[0]), jnp.asarray(edge)
    vmem, sems = pltpu.VMEM, pltpu.SemaphoreType.DMA

    ring = lambda d: [(i, (i + d) % 4) for i in range(4)]
    swap = [(0, 1), (1, 0)]
    near_p, top, bottom = call(
        product_kernel, [(32, 32, 256)] + [(32, 16, 256)] * 2, where, perturbations, control, hbm=(1, 2),
        scratch=[vmem((32, 32, 256), F32), sems((2, 8))],
    )
    above = lax.ppermute(bottom, "gx", ring(1))
    below = lax.ppermute(top, "gx", ring(3))
    edges = call(edge_kernel, [(2, 32, 256)], where, top, bottom)[0]
    side = lax.ppermute(edges, "gy", swap)
    side_above = lax.ppermute(side[:, HALO:], "gx", ring(1))
    side_below = lax.ppermute(side[:, :HALO], "gx", ring(3))
    eh, el, right = call(
        table_kernel, [jax.ShapeDtypeStruct(s, BF16) for s in [(512, 128)] * 2 + [(2, 1024, 256)]],
        where, edge, patch, right, hbm=(3,), scratch=[sems((2, 4))],
    )
    piece = {}
    for part in range(2):
        extra = (side_above, side, side_below, eh, el) if part == 0 else (near,)
        keep, give, *rest = call(
            functools.partial(filter_kernel, part), [(8, 32, 256)] * 2 + [(128, 128)] * (part == 0),
            where, near_p, above, top, bottom, below, left, right, *extra,
            scratch=[vmem((512, 512), BF16)] * 2 + [vmem((256, 512), BF16)] * 2
            + [vmem((512, 256), F32), vmem((2, 512, 128), F32)],
            cost=2 * 10**9,
        )
        near = rest[0] if rest else None
        got = lax.ppermute(give, "core", swap)
        for i, d in enumerate(((2, 1), (3, 0))[part]):
            for wave, at in enumerate((slice(0, 4),) if d == 2 else (slice(0, 2), slice(2, 4))):
                piece[d, wave] = keep[4 * i : 4 * i + 4][at] + got[4 * i : 4 * i + 4][at]
    x2 = lax.ppermute(piece[2, 0], "x", ring(2))
    waves = []
    for wave in range(2):
        x1, x3 = (lax.ppermute(piece[d, wave], "x", ring(d)) for d in (1, 3))
        waves.append([
            (piece[0, wave][i : i + 1] + x2[2 * wave + i : 2 * wave + i + 1]) + (x1[i : i + 1] + x3[i : i + 1])
            for i in range(2)
        ])
        x2, waves[wave] = lax.optimization_barrier((x2, waves[wave]))
    (next_, last), (far, own) = waves
    z1, z3, z2 = (lax.ppermute(cell, "z", ring(e)) for e, cell in ((1, next_), (3, last), (2, far)))
    return ((own + z2) + (z1 + z3)) * (1.0 / 31.0)


def solution(mesh):
    grid = Mesh(mesh.devices.reshape(4, 4, 2, 4, 2), ("x", "z", "core", "gx", "gy"))
    mem = ("x", "z", "core")
    placed = (P(mem, None, "gx", "gy"), P(None, "gx", "gy"))
    return jax.shard_map(body, mesh=grid, in_specs=placed, out_specs=P(mem, "gx", "gy"), check_vma=False)
```

```python
import functools

import jax
import jax.numpy as jnp
import numpy as np
from jax import lax
from jax.experimental import pallas as pl
from jax.experimental.pallas import tpu as pltpu
from jax.sharding import Mesh, PartitionSpec as P


F32, BF16 = jnp.float32, jnp.bfloat16
HALO = 16
VMEM = pl.BlockSpec(memory_space=pltpu.VMEM)


def line_terms(size):
    offsets = np.arange(-4, 5)
    taps = np.exp(-offsets * offsets / 18.0)
    taps = taps / np.sqrt(np.sum(taps * taps))

    def banded(count):
        return sum(t * np.eye(count, k=o) for t, o in zip(taps, offsets))

    pairs = np.repeat(np.eye(size // 2), 2, axis=1) * np.sqrt(0.5)
    coarse = np.sqrt(0.5) * banded(size // 2) @ pairs
    return banded(size), np.repeat(coarse, 2, axis=0), coarse


def split(values):
    high = values.astype(BF16)
    return high, (values - high.astype(values.dtype)).astype(BF16)


def left_table(size, parts):
    fine, pair, coarse = line_terms(size)
    rows = size // parts
    tables = []
    for part in range(parts):
        terms = []
        for term in (fine @ fine, fine @ pair, coarse @ fine, coarse @ pair):
            count = term.shape[0] // parts
            wide = np.zeros((count, rows + 2 * HALO))
            for e in range(rows + 2 * HALO):
                source = part * rows - HALO + e
                if 0 <= source < size:
                    wide[:, e] = term[part * count : (part + 1) * count, source]
            terms.append(wide)
        tables.append(np.concatenate(terms))
    return np.stack(tables)


def right_tables(size, parts):
    fine, pair, _ = line_terms(size)
    columns = size // parts
    owns, sides = [], []
    for part in range(parts):
        own = slice(part * columns, (part + 1) * columns)
        edge = slice(columns, columns + HALO) if part == 0 else slice(columns - HALO, columns)
        near = slice(columns - HALO, columns) if part == 0 else slice(columns, columns + HALO)
        terms = (fine @ fine, pair @ fine, fine @ pair, pair @ pair)
        owns.append(np.concatenate([term[own, own] for term in terms]))
        sides.append(np.concatenate([np.tile(term[edge, near], (1, 8)) for term in terms]))
    return np.stack(owns), np.stack(sides)


def halves(table):
    high = table.astype(np.float32).astype(BF16)
    low = (table - high.astype(np.float64)).astype(np.float32).astype(BF16)
    return np.stack([high, low], axis=1)


def dot3(left, right):
    (lh, ll), (rh, rl) = left, right
    dot = lambda a, b: jnp.dot(a, b, preferred_element_type=F32)
    return dot(lh, rh) + (dot(lh, rl) + dot(ll, rh))


def block_of(where, k):
    return lax.rem(where[3] + (2, 1, 3, 0)[k], 4)


def product_kernel(where, p_hbm, c_hbm, p_ref, top_ref, bottom_ref, c_ref, sems):
    copies = []
    for k in range(4):
        for h in range(2):
            source, at = pl.ds(8 * block_of(where, k) + 4 * h, 4), pl.ds(8 * k + 4 * h, 4)
            copies.append(pltpu.make_async_copy(p_hbm.at[0, source], p_ref.at[at], sems.at[0, 2 * k + h]))
            copies.append(pltpu.make_async_copy(c_hbm.at[source], c_ref.at[at], sems.at[1, 2 * k + h]))
    for copy in copies:
        copy.start()
    for g in range(8):
        copies[2 * g].wait()
        copies[2 * g + 1].wait()
        at = slice(4 * g, 4 * g + 4)
        v = p_ref[at] * c_ref[at]
        top_ref[at] = v[:, :HALO]
        bottom_ref[at] = v[:, HALO:]


def edge_kernel(where, top_ref, bottom_ref, edge_ref, edge_top_ref, edge_bottom_ref):
    gy = where[2]
    lane = lax.broadcasted_iota(jnp.int32, (1, 128), 1)
    near = pl.ds(pl.multiple_of(128 * (1 - gy), 128), 128)
    for r_ref, rows, half_ref in (
        (top_ref, slice(0, HALO), edge_top_ref), (bottom_ref, slice(HALO, 2 * HALO), edge_bottom_ref)
    ):
        edges = jnp.zeros((64, 128), F32)
        for g in range(8):
            v = r_ref[4 * g : 4 * g + 4, :, near].reshape(64, 128)
            if g:
                v = pltpu.roll(v, 16 * g, 1)
            edges = jnp.where(lane // 16 == lax.rem(g + 7 * (1 - gy), 8), v, edges)
        for f in range(4):
            lanes = slice(128 * (f % 2), 128 * (f % 2) + 128)
            edge_ref[f // 2, rows, lanes] = edges[16 * f : 16 * f + 16]
            half_ref[f // 2, :, lanes] = edges[16 * f : 16 * f + 16]


def table_kernel(
    where, edge_ref, patch_ref, right_hbm, eh_ref, el_ref, right_ref, sems
):
    gy = where[2]
    copies = []
    for h in range(2):
        for k in range(4):
            at = pl.ds(256 * k, 256)
            copies.append(pltpu.make_async_copy(right_hbm.at[h, at], right_ref.at[h, at], sems.at[h, k]))
    for copy in copies:
        copy.start()
    narrow = lax.broadcasted_iota(jnp.int32, (1, 128), 1)
    for h, e_ref in ((0, eh_ref), (1, el_ref)):
        for t in range(4):
            rows = edge_ref[gy, h, 16 * t : 16 * t + 16].astype(F32)
            for g in range(8):
                at = 128 * t + 16 * g
                e_ref[at : at + 16] = jnp.where(narrow // 16 == g, rows, jnp.zeros_like(rows)).astype(BF16)
    for copy in copies:
        copy.wait()

    @pl.when(gy == 1)
    def _():
        for h in range(2):
            for t in range(4):
                right_ref[h, 256 * t : 256 * t + 32, :128] = patch_ref[h, 0, t]
                right_ref[h, 256 * t + 224 : 256 * t + 256, 128:] = patch_ref[h, 1, t]


def filter_kernel(
    part, where, p_ref, above_ref, top_ref, bottom_ref, below_ref, left_ref, right_ref, *refs
):
    core, gy, z = where[0], where[2], where[4]
    left = left_ref[where[1]]

    def dot_rows(parts):
        high, low = split(jnp.concatenate(parts))
        return jnp.dot(left, jnp.concatenate([high, high, low]), preferred_element_type=F32)

    narrow = lax.broadcasted_iota(jnp.int32, (1, 128), 1)
    if part == 0:
        side_above_ref, side_ref, side_below_ref, eh_ref, el_ref, keep_ref, send_ref, near_ref, *scratch = refs
        lanes = (slice(0, 128), slice(128, 256))
        sides = (side_above_ref, side_ref.at[:, :HALO], side_ref.at[:, HALO:], side_below_ref)
        side = [dot_rows([s[f // 2, :, lanes[f % 2]] for s in sides]) for f in range(4)]
        fine = split(jnp.concatenate([jnp.concatenate([u[:32], u[32:64]], axis=1) for u in side]))
        pair = split(jnp.concatenate([jnp.concatenate([u[64:80], u[80:]], axis=1) for u in side]))
        near = dot3(fine, (eh_ref[:256], el_ref[:256]))
        near_pairs = dot3(pair, (eh_ref[256:], el_ref[256:]))
        near_ref[pl.ds(0, 64, stride=2), :] = near_pairs
        near_ref[pl.ds(1, 64, stride=2), :] = near_pairs
        near = near + near_ref[...]
        near = jnp.where(gy == 0, pltpu.roll(near, 112, 1), pltpu.roll(near, 16, 1))
        near_ref[...] = near
    else:
        near_ref, keep_ref, send_ref, *scratch = refs
        near = near_ref[...]
    fh_ref, fl_ref, ch_ref, cl_ref, alpha_ref, pairs_ref = scratch
    on_left = (narrow < HALO) & (gy == 1)
    on_right = (narrow >= 128 - HALO) & (gy == 0)

    for f in range(16):
        u = dot_rows([r[16 * part + f] for r in (above_ref, top_ref, bottom_ref, below_ref)])
        for t in range(2):
            at, lanes = slice(32 * f, 32 * f + 32), slice(256 * t, 256 * t + 256)
            fh_ref[at, lanes], fl_ref[at, lanes] = split(u[32 * t : 32 * t + 32])
            at = slice(16 * f, 16 * f + 16)
            ch_ref[at, lanes], cl_ref[at, lanes] = split(u[64 + 16 * t : 80 + 16 * t])

    alpha_ref[...] = dot3((fh_ref[...], fl_ref[...]), (right_ref[0, :512], right_ref[1, :512]))
    pairs = dot3((ch_ref[...], cl_ref[...]), (right_ref[0, 512:], right_ref[1, 512:]))
    for h in range(2):
        for s in range(2):
            pairs_ref[h, pl.ds(s, 256, stride=2), :] = pairs[:, 128 * h : 128 * h + 128]

    for g in range(4):
        at = slice(128 * g, 128 * g + 128)
        shift = (128 - 16 * (4 * part + g)) % 128
        moved = pltpu.roll(near, shift, 1) if shift else near
        zero = jnp.zeros_like(moved)
        low = pairs_ref[0, at] + jnp.where(on_left, moved, zero)
        high = pairs_ref[1, at] + jnp.where(on_right, moved, zero)
        alpha = alpha_ref[at] + jnp.concatenate([low, high], axis=1)
        first = 16 * part + 4 * g
        q = p_ref[first : first + 4] * alpha.reshape(4, 32, 256)
        for j in range(2):
            to = 4 * (g // 2) + lax.rem(6 + z - (2 * (g % 2) + j), 4)
            keep_ref[to] = jnp.where(core == 0, q[2 * j], q[2 * j + 1])
            send_ref[to] = jnp.where(core == 0, q[2 * j + 1], q[2 * j])


def call(kernel, outs, *args, hbm=(), scratch=(), cost=0, grant=16):
    args = [pltpu.with_memory_space_constraint(a, pltpu.HBM) if i in hbm else a for i, a in enumerate(args)]
    specs = [pl.BlockSpec(memory_space=pltpu.SMEM)] + [
        pl.BlockSpec(memory_space=pltpu.HBM) if i in hbm else VMEM for i in range(1, len(args))
    ]
    return pl.pallas_call(
        kernel,
        out_shape=[o if isinstance(o, jax.ShapeDtypeStruct) else jax.ShapeDtypeStruct(o, F32) for o in outs],
        in_specs=specs,
        out_specs=[VMEM] * len(outs),
        scratch_shapes=scratch,
        cost_estimate=pl.CostEstimate(flops=cost, bytes_accessed=1 << 20, transcendentals=0),
        compiler_params=pltpu.CompilerParams(vmem_limit_bytes=grant << 20),
    )(*args)


def body(perturbations, control):
    x, z, core, gx, gy = (lax.axis_index(a) for a in ("x", "z", "core", "gx", "gy"))
    where = jnp.stack([core, gx, gy, x, z]).astype(jnp.int32)
    high, low = np.moveaxis(halves(left_table(128, 4)), 1, 0)
    left = jnp.asarray(np.concatenate([high, low, high], axis=2))
    right, edge = (halves(t) for t in right_tables(512, 2))
    blocks = right[1].reshape(2, 4, 256, 256)
    patch = jnp.asarray(np.stack([blocks[:, :, :32, :128], blocks[:, :, 224:, 128:]], axis=1))
    right, edge = jnp.asarray(right[0]), jnp.asarray(edge)
    vmem, sems = pltpu.VMEM, pltpu.SemaphoreType.DMA

    ring = lambda d: [(i, (i + d) % 4) for i in range(4)]
    swap = [(0, 1), (1, 0)]
    near_p, top, bottom = call(
        product_kernel, [(32, 32, 256)] + [(32, 16, 256)] * 2, where, perturbations, control, hbm=(1, 2),
        scratch=[vmem((32, 32, 256), F32), sems((2, 8))],
    )
    above = lax.ppermute(bottom, "gx", ring(1))
    below = lax.ppermute(top, "gx", ring(3))
    edges, edge_top, edge_bottom = call(
        edge_kernel, [(2, 32, 256)] + [(2, 16, 256)] * 2, where, top, bottom
    )
    diagonal = lambda d: [(2 * a + b, 2 * ((a + d) % 4) + 1 - b) for a in range(4) for b in range(2)]
    side_above = lax.ppermute(edge_bottom, ("gx", "gy"), diagonal(1))
    side_below = lax.ppermute(edge_top, ("gx", "gy"), diagonal(3))
    side = lax.ppermute(edges, "gy", swap)
    eh, el, right = call(
        table_kernel, [jax.ShapeDtypeStruct(s, BF16) for s in [(512, 128)] * 2 + [(2, 1024, 256)]],
        where, edge, patch, right, hbm=(3,), scratch=[sems((2, 4))],
    )
    piece = {}
    for part in range(2):
        extra = (side_above, side, side_below, eh, el) if part == 0 else (near,)
        keep, give, *rest = call(
            functools.partial(filter_kernel, part), [(8, 32, 256)] * 2 + [(128, 128)] * (part == 0),
            where, near_p, above, top, bottom, below, left, right, *extra,
            scratch=[vmem((512, 512), BF16)] * 2 + [vmem((256, 512), BF16)] * 2
            + [vmem((512, 256), F32), vmem((2, 512, 128), F32)],
            cost=2 * 10**9,
        )
        near = rest[0] if rest else None
        got = lax.ppermute(give, "core", swap)
        for i in range(2):
            for wave in range(2):
                at = slice(4 * i + 2 * wave, 4 * i + 2 * wave + 2)
                piece[((2, 1), (3, 0))[part][i], wave] = keep[at] + got[at]
    waves = []
    for wave in range(2):
        x2, x1, x3 = (lax.ppermute(piece[d, wave], "x", ring(d)) for d in (2, 1, 3))
        waves.append([(piece[0, wave][i : i + 1] + x2[i : i + 1]) + (x1[i : i + 1] + x3[i : i + 1]) for i in range(2)])
    (far, next_), (own, last) = waves
    z2, z1, z3 = (lax.ppermute(cell, "z", ring(e)) for e, cell in ((2, far), (1, next_), (3, last)))
    return ((own + z2) + (z1 + z3)) * (1.0 / 31.0)


def solution(mesh):
    grid = Mesh(mesh.devices.reshape(4, 4, 2, 4, 2), ("x", "z", "core", "gx", "gy"))
    mem = ("x", "z", "core")
    placed = (P(mem, None, "gx", "gy"), P(None, "gx", "gy"))
    return jax.shard_map(body, mesh=grid, in_specs=placed, out_specs=P(mem, "gx", "gy"), check_vma=False)
```

```python
import functools

import jax
import jax.numpy as jnp
import numpy as np
from jax import lax
from jax.experimental import pallas as pl
from jax.experimental.pallas import tpu as pltpu
from jax.sharding import Mesh, PartitionSpec as P


PARTS = ((2,), (1,), (3, 0))

F32, BF16 = jnp.float32, jnp.bfloat16
HALO = 16
VMEM = pl.BlockSpec(memory_space=pltpu.VMEM)


def line_terms(size):
    offsets = np.arange(-4, 5)
    taps = np.exp(-offsets * offsets / 18.0)
    taps = taps / np.sqrt(np.sum(taps * taps))

    def banded(count):
        return sum(t * np.eye(count, k=o) for t, o in zip(taps, offsets))

    pairs = np.repeat(np.eye(size // 2), 2, axis=1) * np.sqrt(0.5)
    coarse = np.sqrt(0.5) * banded(size // 2) @ pairs
    return banded(size), np.repeat(coarse, 2, axis=0), coarse


def split(values):
    high = values.astype(BF16)
    return high, (values - high.astype(values.dtype)).astype(BF16)


def left_table(size, parts):
    fine, pair, coarse = line_terms(size)
    rows = size // parts
    tables = []
    for part in range(parts):
        terms = []
        for term in (fine @ fine, fine @ pair, coarse @ fine, coarse @ pair):
            count = term.shape[0] // parts
            wide = np.zeros((count, rows + 2 * HALO))
            for e in range(rows + 2 * HALO):
                source = part * rows - HALO + e
                if 0 <= source < size:
                    wide[:, e] = term[part * count : (part + 1) * count, source]
            terms.append(wide)
        tables.append(np.concatenate(terms))
    return np.stack(tables)


def right_tables(size, parts):
    fine, pair, _ = line_terms(size)
    columns = size // parts
    owns, sides = [], []
    for part in range(parts):
        own = slice(part * columns, (part + 1) * columns)
        edge = slice(columns, columns + HALO) if part == 0 else slice(columns - HALO, columns)
        near = slice(columns - HALO, columns) if part == 0 else slice(columns, columns + HALO)
        terms = (fine @ fine, pair @ fine, fine @ pair, pair @ pair)
        owns.append(np.concatenate([term[own, own] for term in terms]))
        sides.append(np.concatenate([np.tile(term[edge, near], (1, 8)) for term in terms]))
    return np.stack(owns), np.stack(sides)


def halves(table):
    high = table.astype(np.float32).astype(BF16)
    low = (table - high.astype(np.float64)).astype(np.float32).astype(BF16)
    return np.stack([high, low], axis=1)


def dot3(left, right):
    (lh, ll), (rh, rl) = left, right
    dot = lambda a, b: jnp.dot(a, b, preferred_element_type=F32)
    return dot(lh, rh) + (dot(lh, rl) + dot(ll, rh))


def block_of(where, k):
    return lax.rem(where[3] + (2, 1, 3, 0)[k], 4)


def product_kernel(where, p_hbm, c_hbm, p_ref, top_ref, bottom_ref, c_ref, sems):
    copies = []
    for k in range(4):
        for h in range(2):
            source, at = pl.ds(8 * block_of(where, k) + 4 * h, 4), pl.ds(8 * k + 4 * h, 4)
            copies.append(pltpu.make_async_copy(p_hbm.at[0, source], p_ref.at[at], sems.at[0, 2 * k + h]))
            copies.append(pltpu.make_async_copy(c_hbm.at[source], c_ref.at[at], sems.at[1, 2 * k + h]))
    for copy in copies:
        copy.start()
    for g in range(8):
        copies[2 * g].wait()
        copies[2 * g + 1].wait()
        at = slice(4 * g, 4 * g + 4)
        v = p_ref[at] * c_ref[at]
        top_ref[at] = v[:, :HALO]
        bottom_ref[at] = v[:, HALO:]


def edge_kernel(where, top_ref, bottom_ref, edge_ref, edge_top_ref, edge_bottom_ref):
    gy = where[2]
    lane = lax.broadcasted_iota(jnp.int32, (1, 128), 1)
    near = pl.ds(pl.multiple_of(128 * (1 - gy), 128), 128)
    for r_ref, rows, half_ref in (
        (top_ref, slice(0, HALO), edge_top_ref), (bottom_ref, slice(HALO, 2 * HALO), edge_bottom_ref)
    ):
        edges = jnp.zeros((64, 128), F32)
        for g in range(8):
            v = r_ref[4 * g : 4 * g + 4, :, near].reshape(64, 128)
            if g:
                v = pltpu.roll(v, 16 * g, 1)
            edges = jnp.where(lane // 16 == lax.rem(g + 7 * (1 - gy), 8), v, edges)
        for f in range(4):
            lanes = slice(128 * (f % 2), 128 * (f % 2) + 128)
            edge_ref[f // 2, rows, lanes] = edges[16 * f : 16 * f + 16]
            half_ref[f // 2, :, lanes] = edges[16 * f : 16 * f + 16]


def table_kernel(
    where, edge_ref, patch_ref, right_hbm, eh_ref, el_ref, right_ref, sems
):
    gy = where[2]
    copies = []
    for h in range(2):
        for k in range(4):
            at = pl.ds(256 * k, 256)
            copies.append(pltpu.make_async_copy(right_hbm.at[h, at], right_ref.at[h, at], sems.at[h, k]))
    for copy in copies:
        copy.start()
    narrow = lax.broadcasted_iota(jnp.int32, (1, 128), 1)
    for h, e_ref in ((0, eh_ref), (1, el_ref)):
        for t in range(4):
            rows = edge_ref[gy, h, 16 * t : 16 * t + 16].astype(F32)
            for g in range(8):
                at = 128 * t + 16 * g
                e_ref[at : at + 16] = jnp.where(narrow // 16 == g, rows, jnp.zeros_like(rows)).astype(BF16)
    for copy in copies:
        copy.wait()

    @pl.when(gy == 1)
    def _():
        for h in range(2):
            for t in range(4):
                right_ref[h, 256 * t : 256 * t + 32, :128] = patch_ref[h, 0, t]
                right_ref[h, 256 * t + 224 : 256 * t + 256, 128:] = patch_ref[h, 1, t]


def filter_kernel(
    block, count, where, p_ref, above_ref, top_ref, bottom_ref, below_ref, left_ref, right_ref, *refs
):
    core, gy, z = where[0], where[2], where[4]
    left = left_ref[where[1]]

    def dot_rows(parts):
        high, low = split(jnp.concatenate(parts))
        return jnp.dot(left, jnp.concatenate([high, high, low]), preferred_element_type=F32)

    narrow = lax.broadcasted_iota(jnp.int32, (1, 128), 1)
    if block == 0:
        side_above_ref, side_ref, side_below_ref, eh_ref, el_ref, keep_ref, send_ref, near_ref, *scratch = refs
        lanes = (slice(0, 128), slice(128, 256))
        sides = (side_above_ref, side_ref.at[:, :HALO], side_ref.at[:, HALO:], side_below_ref)
        side = [dot_rows([s[f // 2, :, lanes[f % 2]] for s in sides]) for f in range(4)]
        fine = split(jnp.concatenate([jnp.concatenate([u[:32], u[32:64]], axis=1) for u in side]))
        pair = split(jnp.concatenate([jnp.concatenate([u[64:80], u[80:]], axis=1) for u in side]))
        near = dot3(fine, (eh_ref[:256], el_ref[:256]))
        near_pairs = dot3(pair, (eh_ref[256:], el_ref[256:]))
        near_ref[pl.ds(0, 64, stride=2), :] = near_pairs
        near_ref[pl.ds(1, 64, stride=2), :] = near_pairs
        near = near + near_ref[...]
        near = jnp.where(gy == 0, pltpu.roll(near, 112, 1), pltpu.roll(near, 16, 1))
        near_ref[...] = near
    else:
        near_ref, keep_ref, send_ref, *scratch = refs
        near = near_ref[...]
    fh_ref, fl_ref, ch_ref, cl_ref, alpha_ref, pairs_ref = scratch
    on_left = (narrow < HALO) & (gy == 1)
    on_right = (narrow >= 128 - HALO) & (gy == 0)

    for f in range(8 * count):
        u = dot_rows([r[8 * block + f] for r in (above_ref, top_ref, bottom_ref, below_ref)])
        for t in range(2):
            at, lanes = slice(32 * f, 32 * f + 32), slice(256 * t, 256 * t + 256)
            fh_ref[at, lanes], fl_ref[at, lanes] = split(u[32 * t : 32 * t + 32])
            at = slice(16 * f, 16 * f + 16)
            ch_ref[at, lanes], cl_ref[at, lanes] = split(u[64 + 16 * t : 80 + 16 * t])

    alpha_ref[...] = dot3((fh_ref[...], fl_ref[...]), (right_ref[0, :512], right_ref[1, :512]))
    pairs = dot3((ch_ref[...], cl_ref[...]), (right_ref[0, 512:], right_ref[1, 512:]))
    for h in range(2):
        for s in range(2):
            pairs_ref[h, pl.ds(s, 128 * count, stride=2), :] = pairs[:, 128 * h : 128 * h + 128]

    for g in range(2 * count):
        at = slice(128 * g, 128 * g + 128)
        shift = (128 - 16 * (2 * block + g)) % 128
        moved = pltpu.roll(near, shift, 1) if shift else near
        zero = jnp.zeros_like(moved)
        low = pairs_ref[0, at] + jnp.where(on_left, moved, zero)
        high = pairs_ref[1, at] + jnp.where(on_right, moved, zero)
        alpha = alpha_ref[at] + jnp.concatenate([low, high], axis=1)
        first = 8 * block + 4 * g
        q = p_ref[first : first + 4] * alpha.reshape(4, 32, 256)
        for j in range(2):
            to = 4 * (g // 2) + lax.rem(6 + z - (2 * (g % 2) + j), 4)
            keep_ref[to] = jnp.where(core == 0, q[2 * j], q[2 * j + 1])
            send_ref[to] = jnp.where(core == 0, q[2 * j + 1], q[2 * j])


def call(kernel, outs, *args, hbm=(), scratch=(), cost=0, grant=16):
    args = [pltpu.with_memory_space_constraint(a, pltpu.HBM) if i in hbm else a for i, a in enumerate(args)]
    specs = [pl.BlockSpec(memory_space=pltpu.SMEM)] + [
        pl.BlockSpec(memory_space=pltpu.HBM) if i in hbm else VMEM for i in range(1, len(args))
    ]
    return pl.pallas_call(
        kernel,
        out_shape=[o if isinstance(o, jax.ShapeDtypeStruct) else jax.ShapeDtypeStruct(o, F32) for o in outs],
        in_specs=specs,
        out_specs=[VMEM] * len(outs),
        scratch_shapes=scratch,
        cost_estimate=pl.CostEstimate(flops=cost, bytes_accessed=1 << 20, transcendentals=0),
        compiler_params=pltpu.CompilerParams(vmem_limit_bytes=grant << 20),
    )(*args)


def body(perturbations, control):
    x, z, core, gx, gy = (lax.axis_index(a) for a in ("x", "z", "core", "gx", "gy"))
    where = jnp.stack([core, gx, gy, x, z]).astype(jnp.int32)
    high, low = np.moveaxis(halves(left_table(128, 4)), 1, 0)
    left = jnp.asarray(np.concatenate([high, low, high], axis=2))
    right, edge = (halves(t) for t in right_tables(512, 2))
    blocks = right[1].reshape(2, 4, 256, 256)
    patch = jnp.asarray(np.stack([blocks[:, :, :32, :128], blocks[:, :, 224:, 128:]], axis=1))
    right, edge = jnp.asarray(right[0]), jnp.asarray(edge)
    vmem, sems = pltpu.VMEM, pltpu.SemaphoreType.DMA

    ring = lambda d: [(i, (i + d) % 4) for i in range(4)]
    swap = [(0, 1), (1, 0)]
    near = None
    near_p, top, bottom = call(
        product_kernel, [(32, 32, 256)] + [(32, 16, 256)] * 2, where, perturbations, control, hbm=(1, 2),
        scratch=[vmem((32, 32, 256), F32), sems((2, 8))],
    )
    above = lax.ppermute(bottom, "gx", ring(1))
    below = lax.ppermute(top, "gx", ring(3))
    edges, edge_top, edge_bottom = call(
        edge_kernel, [(2, 32, 256)] + [(2, 16, 256)] * 2, where, top, bottom
    )
    diagonal = lambda d: [(2 * a + b, 2 * ((a + d) % 4) + 1 - b) for a in range(4) for b in range(2)]
    side_above = lax.ppermute(edge_bottom, ("gx", "gy"), diagonal(1))
    side_below = lax.ppermute(edge_top, ("gx", "gy"), diagonal(3))
    side = lax.ppermute(edges, "gy", swap)
    eh, el, right = call(
        table_kernel, [jax.ShapeDtypeStruct(s, BF16) for s in [(512, 128)] * 2 + [(2, 1024, 256)]],
        where, edge, patch, right, hbm=(3,), scratch=[sems((2, 4))],
    )
    piece, block = {}, 0
    for part, distances in enumerate(PARTS):
        count = len(distances)
        extra = (side_above, side, side_below, eh, el) if part == 0 else (near,)
        keep, give, *rest = call(
            functools.partial(filter_kernel, block, count),
            [(4 * count, 32, 256)] * 2 + [(128, 128)] * (part == 0),
            where, near_p, above, top, bottom, below, left, right, *extra,
            scratch=[vmem((256 * count, 512), BF16)] * 2 + [vmem((128 * count, 512), BF16)] * 2
            + [vmem((256 * count, 256), F32), vmem((2, 256 * count, 128), F32)],
            cost=10**9 * count,
        )
        near = rest[0] if rest else near
        got = lax.ppermute(give, "core", swap)
        for i, d in enumerate(distances):
            for wave, at in enumerate((slice(0, 4),) if d in (2, 1) else (slice(0, 2), slice(2, 4))):
                piece[d, wave] = keep[4 * i : 4 * i + 4][at] + got[4 * i : 4 * i + 4][at]
        block += count
    x2, x1 = (lax.ppermute(piece[d, 0], "x", ring(d)) for d in (2, 1))
    waves = []
    for wave in range(2):
        x3 = lax.ppermute(piece[3, wave], "x", ring(3))
        cells = [
            (piece[0, wave][i : i + 1] + x2[j : j + 1]) + (x1[j : j + 1] + x3[i : i + 1])
            for i, j in ((0, 2 * wave), (1, 2 * wave + 1))
        ]
        x2, x1, cells = lax.optimization_barrier((x2, x1, cells))
        waves.append(cells)
    (far, next_), (own, last) = waves
    z2, z1, z3 = (lax.ppermute(cell, "z", ring(e)) for e, cell in ((2, far), (1, next_), (3, last)))
    return ((own + z2) + (z1 + z3)) * (1.0 / 31.0)


def solution(mesh):
    grid = Mesh(mesh.devices.reshape(4, 4, 2, 4, 2), ("x", "z", "core", "gx", "gy"))
    mem = ("x", "z", "core")
    placed = (P(mem, None, "gx", "gy"), P(None, "gx", "gy"))
    return jax.shard_map(body, mesh=grid, in_specs=placed, out_specs=P(mem, "gx", "gy"), check_vma=False)
```

```python
import functools

import jax
import jax.numpy as jnp
import numpy as np
from jax import lax
from jax.experimental import pallas as pl
from jax.experimental.pallas import tpu as pltpu
from jax.sharding import Mesh, PartitionSpec as P


F32, BF16 = jnp.float32, jnp.bfloat16
HALO = 16
VMEM = pl.BlockSpec(memory_space=pltpu.VMEM)


def line_terms(size):
    offsets = np.arange(-4, 5)
    taps = np.exp(-offsets * offsets / 18.0)
    taps = taps / np.sqrt(np.sum(taps * taps))

    def banded(count):
        return sum(t * np.eye(count, k=o) for t, o in zip(taps, offsets))

    pairs = np.repeat(np.eye(size // 2), 2, axis=1) * np.sqrt(0.5)
    coarse = np.sqrt(0.5) * banded(size // 2) @ pairs
    return banded(size), np.repeat(coarse, 2, axis=0), coarse


def split(values):
    high = values.astype(BF16)
    return high, (values - high.astype(values.dtype)).astype(BF16)


def left_table(size, parts):
    fine, pair, coarse = line_terms(size)
    rows = size // parts
    tables = []
    for part in range(parts):
        terms = []
        for term in (fine @ fine, fine @ pair, coarse @ fine, coarse @ pair):
            count = term.shape[0] // parts
            wide = np.zeros((count, rows + 2 * HALO))
            for e in range(rows + 2 * HALO):
                source = part * rows - HALO + e
                if 0 <= source < size:
                    wide[:, e] = term[part * count : (part + 1) * count, source]
            terms.append(wide)
        tables.append(np.concatenate(terms))
    return np.stack(tables)


def right_tables(size, parts):
    fine, pair, _ = line_terms(size)
    columns = size // parts
    owns, sides = [], []
    for part in range(parts):
        own = slice(part * columns, (part + 1) * columns)
        edge = slice(columns, columns + HALO) if part == 0 else slice(columns - HALO, columns)
        near = slice(columns - HALO, columns) if part == 0 else slice(columns, columns + HALO)
        terms = (fine @ fine, pair @ fine, fine @ pair, pair @ pair)
        owns.append(np.concatenate([term[own, own] for term in terms]))
        sides.append(np.concatenate([np.tile(term[edge, near], (1, 8)) for term in terms]))
    return np.stack(owns), np.stack(sides)


def halves(table):
    high = table.astype(np.float32).astype(BF16)
    low = (table - high.astype(np.float64)).astype(np.float32).astype(BF16)
    return np.stack([high, low], axis=1)


def dot3(left, right):
    (lh, ll), (rh, rl) = left, right
    dot = lambda a, b: jnp.dot(a, b, preferred_element_type=F32)
    return dot(lh, rh) + (dot(lh, rl) + dot(ll, rh))


def block_of(where, k):
    return lax.rem(where[3] + (2, 1, 3, 0)[k], 4)


def product_kernel(where, p_hbm, c_hbm, p_ref, top_ref, bottom_ref, c_ref, sems):
    copies = []
    for k in range(4):
        for h in range(2):
            source, at = pl.ds(8 * block_of(where, k) + 4 * h, 4), pl.ds(8 * k + 4 * h, 4)
            copies.append(pltpu.make_async_copy(p_hbm.at[0, source], p_ref.at[at], sems.at[0, 2 * k + h]))
            copies.append(pltpu.make_async_copy(c_hbm.at[source], c_ref.at[at], sems.at[1, 2 * k + h]))
    for copy in copies:
        copy.start()
    for g in range(8):
        copies[2 * g].wait()
        copies[2 * g + 1].wait()
        at = slice(4 * g, 4 * g + 4)
        v = p_ref[at] * c_ref[at]
        top_ref[at] = v[:, :HALO]
        bottom_ref[at] = v[:, HALO:]


def edge_kernel(where, top_ref, bottom_ref, edge_ref, edge_top_ref, edge_bottom_ref):
    gy = where[2]
    lane = lax.broadcasted_iota(jnp.int32, (1, 128), 1)
    near = pl.ds(pl.multiple_of(128 * (1 - gy), 128), 128)
    for r_ref, rows, half_ref in (
        (top_ref, slice(0, HALO), edge_top_ref), (bottom_ref, slice(HALO, 2 * HALO), edge_bottom_ref)
    ):
        edges = jnp.zeros((64, 128), F32)
        for g in range(8):
            v = r_ref[4 * g : 4 * g + 4, :, near].reshape(64, 128)
            if g:
                v = pltpu.roll(v, 16 * g, 1)
            edges = jnp.where(lane // 16 == lax.rem(g + 7 * (1 - gy), 8), v, edges)
        for f in range(4):
            lanes = slice(128 * (f % 2), 128 * (f % 2) + 128)
            edge_ref[f // 2, rows, lanes] = edges[16 * f : 16 * f + 16]
            half_ref[f // 2, :, lanes] = edges[16 * f : 16 * f + 16]


def table_kernel(
    where, edge_ref, patch_ref, right_hbm, eh_ref, el_ref, right_ref, sems
):
    gy = where[2]
    copies = []
    for h in range(2):
        for k in range(4):
            at = pl.ds(256 * k, 256)
            copies.append(pltpu.make_async_copy(right_hbm.at[h, at], right_ref.at[h, at], sems.at[h, k]))
    for copy in copies:
        copy.start()
    narrow = lax.broadcasted_iota(jnp.int32, (1, 128), 1)
    for h, e_ref in ((0, eh_ref), (1, el_ref)):
        for t in range(4):
            rows = edge_ref[gy, h, 16 * t : 16 * t + 16].astype(F32)
            for g in range(8):
                at = 128 * t + 16 * g
                e_ref[at : at + 16] = jnp.where(narrow // 16 == g, rows, jnp.zeros_like(rows)).astype(BF16)
    for copy in copies:
        copy.wait()

    @pl.when(gy == 1)
    def _():
        for h in range(2):
            for t in range(4):
                right_ref[h, 256 * t : 256 * t + 32, :128] = patch_ref[h, 0, t]
                right_ref[h, 256 * t + 224 : 256 * t + 256, 128:] = patch_ref[h, 1, t]


def stack3(parts):
    high, low = split(jnp.concatenate(parts))
    return jnp.concatenate([high, high, low])


def early_kernel(
    where, top_ref, bottom_ref, side_above_ref, side_ref, side_below_ref, left_ref, inner_ref, eh_ref, el_ref, right_ref,
    near_ref, own_ref, uh_ref, ul_ref, pairs_ref,
):
    gy = where[2]
    left, inner = left_ref[where[1]], inner_ref[where[1]]
    lanes = (slice(0, 128), slice(128, 256))
    sides = (side_above_ref, side_ref.at[:, :HALO], side_ref.at[:, HALO:], side_below_ref)
    side = [
        jnp.dot(left, stack3([s[f // 2, :, lanes[f % 2]] for s in sides]), preferred_element_type=F32) for f in range(4)
    ]
    fine = split(jnp.concatenate([jnp.concatenate([u[:32], u[32:64]], axis=1) for u in side]))
    pair = split(jnp.concatenate([jnp.concatenate([u[64:80], u[80:]], axis=1) for u in side]))
    near = dot3(fine, (eh_ref[:256], el_ref[:256]))
    near_pairs = dot3(pair, (eh_ref[256:], el_ref[256:]))
    pairs_ref[pl.ds(0, 64, stride=2), :] = near_pairs
    pairs_ref[pl.ds(1, 64, stride=2), :] = near_pairs
    near = near + pairs_ref[...]
    near_ref[...] = jnp.where(gy == 0, pltpu.roll(near, 112, 1), pltpu.roll(near, 16, 1))
    for f in range(32):
        at = slice(16 * f, 16 * f + 16)
        u = jnp.dot(inner, stack3([top_ref[f], bottom_ref[f]]), preferred_element_type=F32)
        uh_ref[at], ul_ref[at] = split(u)
    own_ref[...] = dot3((uh_ref[...], ul_ref[...]), (right_ref[0, :256], right_ref[1, :256]))


def filter_kernel(
    part, where, p_ref, above_ref, top_ref, bottom_ref, below_ref, left_ref, right_ref, near_ref, own_ref,
    keep_ref, send_ref, fh_ref, fl_ref, mh_ref, ml_ref, ch_ref, cl_ref, outer_ref, middle_ref, pairs_ref,
):
    core, gy, z = where[0], where[2], where[4]
    left = left_ref[where[1]]
    narrow = lax.broadcasted_iota(jnp.int32, (1, 128), 1)
    near = near_ref[...]
    on_left = (narrow < HALO) & (gy == 1)
    on_right = (narrow >= 128 - HALO) & (gy == 0)

    for f in range(16):
        v = stack3([r[16 * part + f] for r in (above_ref, top_ref, bottom_ref, below_ref)])
        u = jnp.dot(left, v, preferred_element_type=F32)
        at = slice(16 * f, 16 * f + 16)
        fh_ref[at, :256], fl_ref[at, :256] = split(u[:16])
        fh_ref[at, 256:], fl_ref[at, 256:] = split(u[16:32])
        mh_ref[at], ml_ref[at] = split(u[32:48])
        ch_ref[at, :256], cl_ref[at, :256] = split(u[48:64])
        ch_ref[at, 256:], cl_ref[at, 256:] = split(u[64:])

    outer_ref[...] = dot3((fh_ref[...], fl_ref[...]), (right_ref[0, :512], right_ref[1, :512]))
    middle_ref[...] = dot3((mh_ref[...], ml_ref[...]), (right_ref[0, 256:512], right_ref[1, 256:512]))
    pairs = dot3((ch_ref[...], cl_ref[...]), (right_ref[0, 512:], right_ref[1, 512:]))
    for h in range(2):
        for s in range(2):
            pairs_ref[h, pl.ds(s, 256, stride=2), :] = pairs[:, 128 * h : 128 * h + 128]

    for g in range(4):
        at = slice(128 * g, 128 * g + 128)
        shift = (128 - 16 * (4 * part + g)) % 128
        moved = pltpu.roll(near, shift, 1) if shift else near
        zero = jnp.zeros_like(moved)
        low = pairs_ref[0, at] + jnp.where(on_left, moved, zero)
        high = pairs_ref[1, at] + jnp.where(on_right, moved, zero)
        rows = []
        for f in range(4 * g, 4 * g + 4):
            own = own_ref[16 * (16 * part + f) : 16 * (16 * part + f) + 16]
            rows += [outer_ref[16 * f : 16 * f + 8], middle_ref[16 * f : 16 * f + 16] + own]
            rows += [outer_ref[16 * f + 8 : 16 * f + 16]]
        alpha = jnp.concatenate(rows) + jnp.concatenate([low, high], axis=1)
        first = 16 * part + 4 * g
        q = p_ref[first : first + 4] * alpha.reshape(4, 32, 256)
        for j in range(2):
            to = 4 * (g // 2) + lax.rem(6 + z - (2 * (g % 2) + j), 4)
            keep_ref[to] = jnp.where(core == 0, q[2 * j], q[2 * j + 1])
            send_ref[to] = jnp.where(core == 0, q[2 * j + 1], q[2 * j])


def call(kernel, outs, *args, hbm=(), scratch=(), cost=0, grant=16):
    args = [pltpu.with_memory_space_constraint(a, pltpu.HBM) if i in hbm else a for i, a in enumerate(args)]
    specs = [pl.BlockSpec(memory_space=pltpu.SMEM)] + [
        pl.BlockSpec(memory_space=pltpu.HBM) if i in hbm else VMEM for i in range(1, len(args))
    ]
    return pl.pallas_call(
        kernel,
        out_shape=[o if isinstance(o, jax.ShapeDtypeStruct) else jax.ShapeDtypeStruct(o, F32) for o in outs],
        in_specs=specs,
        out_specs=[VMEM] * len(outs),
        scratch_shapes=scratch,
        cost_estimate=pl.CostEstimate(flops=cost, bytes_accessed=1 << 20, transcendentals=0),
        compiler_params=pltpu.CompilerParams(vmem_limit_bytes=grant << 20),
    )(*args)


def body(perturbations, control):
    x, z, core, gx, gy = (lax.axis_index(a) for a in ("x", "z", "core", "gx", "gy"))
    where = jnp.stack([core, gx, gy, x, z]).astype(jnp.int32)
    high, low = np.moveaxis(halves(left_table(128, 4)), 1, 0)
    three = lambda rows, cells: jnp.asarray(
        np.concatenate([t[:, rows, cells] for t in (high, low, high)], axis=2)
    )
    whole = slice(0, 64)
    left = three(slice(0, 96), whole)
    inner = three(slice(8, 24), slice(HALO, 48))
    rows = np.r_[0:8, 24:32, 32:40, 56:64, 40:56, 64:96]
    left_rest = three(rows, whole)
    right, edge = (halves(t) for t in right_tables(512, 2))
    blocks = right[1].reshape(2, 4, 256, 256)
    patch = jnp.asarray(np.stack([blocks[:, :, :32, :128], blocks[:, :, 224:, 128:]], axis=1))
    right, edge = jnp.asarray(right[0]), jnp.asarray(edge)
    vmem, sems = pltpu.VMEM, pltpu.SemaphoreType.DMA

    ring = lambda d: [(i, (i + d) % 4) for i in range(4)]
    swap = [(0, 1), (1, 0)]
    near_p, top, bottom = call(
        product_kernel, [(32, 32, 256)] + [(32, 16, 256)] * 2, where, perturbations, control, hbm=(1, 2),
        scratch=[vmem((32, 32, 256), F32), sems((2, 8))],
    )
    above = lax.ppermute(bottom, "gx", ring(1))
    below = lax.ppermute(top, "gx", ring(3))
    edges, edge_top, edge_bottom = call(
        edge_kernel, [(2, 32, 256)] + [(2, 16, 256)] * 2, where, top, bottom
    )
    diagonal = lambda d: [(2 * a + b, 2 * ((a + d) % 4) + 1 - b) for a in range(4) for b in range(2)]
    side_above = lax.ppermute(edge_bottom, ("gx", "gy"), diagonal(1))
    side_below = lax.ppermute(edge_top, ("gx", "gy"), diagonal(3))
    side = lax.ppermute(edges, "gy", swap)
    eh, el, right = call(
        table_kernel, [jax.ShapeDtypeStruct(s, BF16) for s in [(512, 128)] * 2 + [(2, 1024, 256)]],
        where, edge, patch, right, hbm=(3,), scratch=[sems((2, 4))],
    )
    near, own = call(
        early_kernel, [(128, 128), (512, 256)], where, top, bottom, side_above, side, side_below,
        left, inner, eh, el, right, scratch=[vmem((512, 256), BF16)] * 2 + [vmem((128, 128), F32)],
        cost=10**9,
    )
    piece = {}
    for part in range(2):
        keep, give = call(
            functools.partial(filter_kernel, part), [(8, 32, 256)] * 2,
            where, near_p, above, top, bottom, below, left_rest, right, near, own,
            scratch=[vmem((256, 512), BF16)] * 2 + [vmem((256, 256), BF16)] * 2 + [vmem((256, 512), BF16)] * 2
            + [vmem((256, 256), F32)] * 2 + [vmem((2, 512, 128), F32)],
            cost=2 * 10**9,
        )
        got = lax.ppermute(give, "core", swap)
        for i in range(2):
            for wave in range(2):
                at = slice(4 * i + 2 * wave, 4 * i + 2 * wave + 2)
                piece[((2, 1), (3, 0))[part][i], wave] = keep[at] + got[at]
    waves = []
    for wave in range(2):
        x2, x1, x3 = (lax.ppermute(piece[d, wave], "x", ring(d)) for d in (2, 1, 3))
        waves.append([(piece[0, wave][i : i + 1] + x2[i : i + 1]) + (x1[i : i + 1] + x3[i : i + 1]) for i in range(2)])
    (far, next_), (stay, last) = waves
    z2, z1, z3 = (lax.ppermute(cell, "z", ring(e)) for e, cell in ((2, far), (1, next_), (3, last)))
    return ((stay + z2) + (z1 + z3)) * (1.0 / 31.0)


def solution(mesh):
    grid = Mesh(mesh.devices.reshape(4, 4, 2, 4, 2), ("x", "z", "core", "gx", "gy"))
    mem = ("x", "z", "core")
    placed = (P(mem, None, "gx", "gy"), P(None, "gx", "gy"))
    return jax.shard_map(body, mesh=grid, in_specs=placed, out_specs=P(mem, "gx", "gy"), check_vma=False)
```

```python
import functools

import jax
import jax.numpy as jnp
import numpy as np
from jax import lax
from jax.experimental import pallas as pl
from jax.experimental.pallas import tpu as pltpu
from jax.sharding import Mesh, PartitionSpec as P


F32, BF16 = jnp.float32, jnp.bfloat16
HALO = 16
VMEM = pl.BlockSpec(memory_space=pltpu.VMEM)


def line_terms(size):
    offsets = np.arange(-4, 5)
    taps = np.exp(-offsets * offsets / 18.0)
    taps = taps / np.sqrt(np.sum(taps * taps))

    def banded(count):
        return sum(t * np.eye(count, k=o) for t, o in zip(taps, offsets))

    pairs = np.repeat(np.eye(size // 2), 2, axis=1) * np.sqrt(0.5)
    coarse = np.sqrt(0.5) * banded(size // 2) @ pairs
    return banded(size), np.repeat(coarse, 2, axis=0), coarse


def split(values):
    high = values.astype(BF16)
    return high, (values - high.astype(values.dtype)).astype(BF16)


def left_table(size, parts):
    fine, pair, coarse = line_terms(size)
    rows = size // parts
    tables = []
    for part in range(parts):
        terms = []
        for term in (fine @ fine, fine @ pair, coarse @ fine, coarse @ pair):
            count = term.shape[0] // parts
            wide = np.zeros((count, rows + 2 * HALO))
            for e in range(rows + 2 * HALO):
                source = part * rows - HALO + e
                if 0 <= source < size:
                    wide[:, e] = term[part * count : (part + 1) * count, source]
            terms.append(wide)
        tables.append(np.concatenate(terms))
    return np.stack(tables)


def right_tables(size, parts):
    fine, pair, _ = line_terms(size)
    columns = size // parts
    owns, sides = [], []
    for part in range(parts):
        own = slice(part * columns, (part + 1) * columns)
        edge = slice(columns, columns + HALO) if part == 0 else slice(columns - HALO, columns)
        near = slice(columns - HALO, columns) if part == 0 else slice(columns, columns + HALO)
        terms = (fine @ fine, pair @ fine, fine @ pair, pair @ pair)
        owns.append(np.concatenate([term[own, own] for term in terms]))
        sides.append(np.concatenate([np.tile(term[edge, near], (1, 8)) for term in terms]))
    return np.stack(owns), np.stack(sides)


def halves(table):
    high = table.astype(np.float32).astype(BF16)
    low = (table - high.astype(np.float64)).astype(np.float32).astype(BF16)
    return np.stack([high, low], axis=1)


def dot3(left, right):
    (lh, ll), (rh, rl) = left, right
    dot = lambda a, b: jnp.dot(a, b, preferred_element_type=F32)
    return dot(lh, rh) + (dot(lh, rl) + dot(ll, rh))


def block_of(where, k):
    return lax.rem(where[3] + (2, 1, 3, 0)[k], 4)


def product_kernel(where, p_hbm, c_hbm, p_ref, top_ref, bottom_ref, c_ref, sems):
    copies = []
    for k in range(4):
        source, at = pl.ds(8 * block_of(where, k), 8), pl.ds(8 * k, 8)
        copies.append(pltpu.make_async_copy(p_hbm.at[0, source], p_ref.at[at], sems.at[0, k]))
        copies.append(pltpu.make_async_copy(c_hbm.at[source], c_ref.at[at], sems.at[1, k]))
    for copy in copies:
        copy.start()
    for k in range(4):
        copies[2 * k].wait()
        copies[2 * k + 1].wait()
        for g in range(2 * k, 2 * k + 2):
            at = slice(4 * g, 4 * g + 4)
            v = p_ref[at] * c_ref[at]
            top_ref[at] = v[:, :HALO]
            bottom_ref[at] = v[:, HALO:]


def edge_kernel(where, top_ref, bottom_ref, edge_ref, edge_top_ref, edge_bottom_ref):
    gy = where[2]
    lane = lax.broadcasted_iota(jnp.int32, (1, 128), 1)
    near = pl.ds(pl.multiple_of(128 * (1 - gy), 128), 128)
    for r_ref, rows, half_ref in (
        (top_ref, slice(0, HALO), edge_top_ref), (bottom_ref, slice(HALO, 2 * HALO), edge_bottom_ref)
    ):
        edges = jnp.zeros((64, 128), F32)
        for g in range(8):
            v = r_ref[4 * g : 4 * g + 4, :, near].reshape(64, 128)
            if g:
                v = pltpu.roll(v, 16 * g, 1)
            edges = jnp.where(lane // 16 == lax.rem(g + 7 * (1 - gy), 8), v, edges)
        for f in range(4):
            lanes = slice(128 * (f % 2), 128 * (f % 2) + 128)
            edge_ref[f // 2, rows, lanes] = edges[16 * f : 16 * f + 16]
            half_ref[f // 2, :, lanes] = edges[16 * f : 16 * f + 16]


def table_kernel(
    where, edge_ref, patch_ref, right_hbm, eh_ref, el_ref, right_ref, sems
):
    gy = where[2]
    copies = []
    for h in range(2):
        for k in range(4):
            at = pl.ds(256 * k, 256)
            copies.append(pltpu.make_async_copy(right_hbm.at[h, at], right_ref.at[h, at], sems.at[h, k]))
    for copy in copies:
        copy.start()
    narrow = lax.broadcasted_iota(jnp.int32, (1, 128), 1)
    for h, e_ref in ((0, eh_ref), (1, el_ref)):
        for t in range(4):
            rows = edge_ref[gy, h, 16 * t : 16 * t + 16].astype(F32)
            for g in range(8):
                at = 128 * t + 16 * g
                e_ref[at : at + 16] = jnp.where(narrow // 16 == g, rows, jnp.zeros_like(rows)).astype(BF16)
    for copy in copies:
        copy.wait()

    @pl.when(gy == 1)
    def _():
        for h in range(2):
            for t in range(4):
                right_ref[h, 256 * t : 256 * t + 32, :128] = patch_ref[h, 0, t]
                right_ref[h, 256 * t + 224 : 256 * t + 256, 128:] = patch_ref[h, 1, t]


def stack3(parts):
    high, low = split(jnp.concatenate(parts))
    return jnp.concatenate([high, high, low])


def early_kernel(
    where, top_ref, bottom_ref, side_above_ref, side_ref, side_below_ref, left_ref, inner_ref, eh_ref, el_ref, right_ref,
    near_ref, own_ref, uh_ref, ul_ref, pairs_ref,
):
    gy = where[2]
    left, inner = left_ref[where[1]], inner_ref[where[1]]
    lanes = (slice(0, 128), slice(128, 256))
    sides = (side_above_ref, side_ref.at[:, :HALO], side_ref.at[:, HALO:], side_below_ref)
    side = [
        jnp.dot(left, stack3([s[f // 2, :, lanes[f % 2]] for s in sides]), preferred_element_type=F32) for f in range(4)
    ]
    fine = split(jnp.concatenate([jnp.concatenate([u[:32], u[32:64]], axis=1) for u in side]))
    pair = split(jnp.concatenate([jnp.concatenate([u[64:80], u[80:]], axis=1) for u in side]))
    near = dot3(fine, (eh_ref[:256], el_ref[:256]))
    near_pairs = dot3(pair, (eh_ref[256:], el_ref[256:]))
    pairs_ref[pl.ds(0, 64, stride=2), :] = near_pairs
    pairs_ref[pl.ds(1, 64, stride=2), :] = near_pairs
    near = near + pairs_ref[...]
    near_ref[...] = jnp.where(gy == 0, pltpu.roll(near, 112, 1), pltpu.roll(near, 16, 1))
    for f in range(32):
        at = slice(16 * f, 16 * f + 16)
        u = jnp.dot(inner, stack3([top_ref[f], bottom_ref[f]]), preferred_element_type=F32)
        uh_ref[at], ul_ref[at] = split(u)
    own_ref[...] = dot3((uh_ref[...], ul_ref[...]), (right_ref[0, :256], right_ref[1, :256]))


def filter_kernel(
    part, where, p_ref, above_ref, top_ref, bottom_ref, below_ref, left_ref, right_ref, near_ref, own_ref,
    keep_ref, send_ref, fh_ref, fl_ref, mh_ref, ml_ref, ch_ref, cl_ref, outer_ref, middle_ref, pairs_ref,
):
    core, gy, z = where[0], where[2], where[4]
    left = left_ref[where[1]]
    narrow = lax.broadcasted_iota(jnp.int32, (1, 128), 1)
    near = near_ref[...]
    on_left = (narrow < HALO) & (gy == 1)
    on_right = (narrow >= 128 - HALO) & (gy == 0)

    for f in range(16):
        v = stack3([r[16 * part + f] for r in (above_ref, top_ref, bottom_ref, below_ref)])
        u = jnp.dot(left, v, preferred_element_type=F32)
        at = slice(16 * f, 16 * f + 16)
        fh_ref[at, :256], fl_ref[at, :256] = split(u[:16])
        fh_ref[at, 256:], fl_ref[at, 256:] = split(u[16:32])
        mh_ref[at], ml_ref[at] = split(u[32:48])
        ch_ref[at, :256], cl_ref[at, :256] = split(u[48:64])
        ch_ref[at, 256:], cl_ref[at, 256:] = split(u[64:])

    outer_ref[...] = dot3((fh_ref[...], fl_ref[...]), (right_ref[0, :512], right_ref[1, :512]))
    middle_ref[...] = dot3((mh_ref[...], ml_ref[...]), (right_ref[0, 256:512], right_ref[1, 256:512]))
    pairs = dot3((ch_ref[...], cl_ref[...]), (right_ref[0, 512:], right_ref[1, 512:]))
    for h in range(2):
        for s in range(2):
            pairs_ref[h, pl.ds(s, 256, stride=2), :] = pairs[:, 128 * h : 128 * h + 128]

    for g in range(4):
        at = slice(128 * g, 128 * g + 128)
        shift = (128 - 16 * (4 * part + g)) % 128
        moved = pltpu.roll(near, shift, 1) if shift else near
        zero = jnp.zeros_like(moved)
        low = pairs_ref[0, at] + jnp.where(on_left, moved, zero)
        high = pairs_ref[1, at] + jnp.where(on_right, moved, zero)
        rows = []
        for f in range(4 * g, 4 * g + 4):
            own = own_ref[16 * (16 * part + f) : 16 * (16 * part + f) + 16]
            rows += [outer_ref[16 * f : 16 * f + 8], middle_ref[16 * f : 16 * f + 16] + own]
            rows += [outer_ref[16 * f + 8 : 16 * f + 16]]
        alpha = jnp.concatenate(rows) + jnp.concatenate([low, high], axis=1)
        first = 16 * part + 4 * g
        q = p_ref[first : first + 4] * alpha.reshape(4, 32, 256)
        for j in range(2):
            to = 4 * (g // 2) + lax.rem(6 + z - (2 * (g % 2) + j), 4)
            keep_ref[to] = jnp.where(core == 0, q[2 * j], q[2 * j + 1])
            send_ref[to] = jnp.where(core == 0, q[2 * j + 1], q[2 * j])


def call(kernel, outs, *args, hbm=(), scratch=(), cost=0, grant=16):
    args = [pltpu.with_memory_space_constraint(a, pltpu.HBM) if i in hbm else a for i, a in enumerate(args)]
    specs = [pl.BlockSpec(memory_space=pltpu.SMEM)] + [
        pl.BlockSpec(memory_space=pltpu.HBM) if i in hbm else VMEM for i in range(1, len(args))
    ]
    return pl.pallas_call(
        kernel,
        out_shape=[o if isinstance(o, jax.ShapeDtypeStruct) else jax.ShapeDtypeStruct(o, F32) for o in outs],
        in_specs=specs,
        out_specs=[VMEM] * len(outs),
        scratch_shapes=scratch,
        cost_estimate=pl.CostEstimate(flops=cost, bytes_accessed=1 << 20, transcendentals=0),
        compiler_params=pltpu.CompilerParams(vmem_limit_bytes=grant << 20),
    )(*args)


def body(perturbations, control):
    x, z, core, gx, gy = (lax.axis_index(a) for a in ("x", "z", "core", "gx", "gy"))
    where = jnp.stack([core, gx, gy, x, z]).astype(jnp.int32)
    high, low = np.moveaxis(halves(left_table(128, 4)), 1, 0)
    three = lambda rows, cells: jnp.asarray(
        np.concatenate([t[:, rows, cells] for t in (high, low, high)], axis=2)
    )
    whole = slice(0, 64)
    left = three(slice(0, 96), whole)
    inner = three(slice(8, 24), slice(HALO, 48))
    rows = np.r_[0:8, 24:32, 32:40, 56:64, 40:56, 64:96]
    left_rest = three(rows, whole)
    right, edge = (halves(t) for t in right_tables(512, 2))
    blocks = right[1].reshape(2, 4, 256, 256)
    patch = jnp.asarray(np.stack([blocks[:, :, :32, :128], blocks[:, :, 224:, 128:]], axis=1))
    right, edge = jnp.asarray(right[0]), jnp.asarray(edge)
    vmem, sems = pltpu.VMEM, pltpu.SemaphoreType.DMA

    ring = lambda d: [(i, (i + d) % 4) for i in range(4)]
    swap = [(0, 1), (1, 0)]
    near_p, top, bottom = call(
        product_kernel, [(32, 32, 256)] + [(32, 16, 256)] * 2, where, perturbations, control, hbm=(1, 2),
        scratch=[vmem((32, 32, 256), F32), sems((2, 4))],
    )
    above = lax.ppermute(bottom, "gx", ring(1))
    below = lax.ppermute(top, "gx", ring(3))
    edges, edge_top, edge_bottom = call(
        edge_kernel, [(2, 32, 256)] + [(2, 16, 256)] * 2, where, top, bottom
    )
    diagonal = lambda d: [(2 * a + b, 2 * ((a + d) % 4) + 1 - b) for a in range(4) for b in range(2)]
    side_above = lax.ppermute(edge_bottom, ("gx", "gy"), diagonal(1))
    side_below = lax.ppermute(edge_top, ("gx", "gy"), diagonal(3))
    side = lax.ppermute(edges, "gy", swap)
    eh, el, right = call(
        table_kernel, [jax.ShapeDtypeStruct(s, BF16) for s in [(512, 128)] * 2 + [(2, 1024, 256)]],
        where, edge, patch, right, hbm=(3,), scratch=[sems((2, 4))],
    )
    near, own = call(
        early_kernel, [(128, 128), (512, 256)], where, top, bottom, side_above, side, side_below,
        left, inner, eh, el, right, scratch=[vmem((512, 256), BF16)] * 2 + [vmem((128, 128), F32)],
        cost=10**9,
    )
    piece = {}
    for part in range(2):
        keep, give = call(
            functools.partial(filter_kernel, part), [(8, 32, 256)] * 2,
            where, near_p, above, top, bottom, below, left_rest, right, near, own,
            scratch=[vmem((256, 512), BF16)] * 2 + [vmem((256, 256), BF16)] * 2 + [vmem((256, 512), BF16)] * 2
            + [vmem((256, 256), F32)] * 2 + [vmem((2, 512, 128), F32)],
            cost=2 * 10**9,
        )
        got = lax.ppermute(give, "core", swap)
        for i in range(2):
            for wave in range(2):
                at = slice(4 * i + 2 * wave, 4 * i + 2 * wave + 2)
                piece[((2, 1), (3, 0))[part][i], wave] = keep[at] + got[at]
    waves = []
    for wave in range(2):
        x2, x1, x3 = (lax.ppermute(piece[d, wave], "x", ring(d)) for d in (2, 1, 3))
        waves.append([(piece[0, wave][i : i + 1] + x2[i : i + 1]) + (x1[i : i + 1] + x3[i : i + 1]) for i in range(2)])
    (far, next_), (stay, last) = waves
    z2, z1, z3 = (lax.ppermute(cell, "z", ring(e)) for e, cell in ((2, far), (1, next_), (3, last)))
    return ((stay + z2) + (z1 + z3)) * (1.0 / 31.0)


def solution(mesh):
    grid = Mesh(mesh.devices.reshape(4, 4, 2, 4, 2), ("x", "z", "core", "gx", "gy"))
    mem = ("x", "z", "core")
    placed = (P(mem, None, "gx", "gy"), P(None, "gx", "gy"))
    return jax.shard_map(body, mesh=grid, in_specs=placed, out_specs=P(mem, "gx", "gy"), check_vma=False)
```

```python
import functools

import jax
import jax.numpy as jnp
import numpy as np
from jax import lax
from jax.experimental import pallas as pl
from jax.experimental.pallas import tpu as pltpu
from jax.sharding import Mesh, PartitionSpec as P


F32, BF16 = jnp.float32, jnp.bfloat16
HALO = 16
VMEM = pl.BlockSpec(memory_space=pltpu.VMEM)


def line_terms(size):
    offsets = np.arange(-4, 5)
    taps = np.exp(-offsets * offsets / 18.0)
    taps = taps / np.sqrt(np.sum(taps * taps))

    def banded(count):
        return sum(t * np.eye(count, k=o) for t, o in zip(taps, offsets))

    pairs = np.repeat(np.eye(size // 2), 2, axis=1) * np.sqrt(0.5)
    coarse = np.sqrt(0.5) * banded(size // 2) @ pairs
    return banded(size), np.repeat(coarse, 2, axis=0), coarse


def split(values):
    high = values.astype(BF16)
    return high, (values - high.astype(values.dtype)).astype(BF16)


def left_table(size, parts):
    fine, pair, coarse = line_terms(size)
    rows = size // parts
    tables = []
    for part in range(parts):
        terms = []
        for term in (fine @ fine, fine @ pair, coarse @ fine, coarse @ pair):
            count = term.shape[0] // parts
            wide = np.zeros((count, rows + 2 * HALO))
            for e in range(rows + 2 * HALO):
                source = part * rows - HALO + e
                if 0 <= source < size:
                    wide[:, e] = term[part * count : (part + 1) * count, source]
            terms.append(wide)
        tables.append(np.concatenate(terms))
    return np.stack(tables)


def right_tables(size, parts):
    fine, pair, _ = line_terms(size)
    columns = size // parts
    owns, sides = [], []
    for part in range(parts):
        own = slice(part * columns, (part + 1) * columns)
        edge = slice(columns, columns + HALO) if part == 0 else slice(columns - HALO, columns)
        near = slice(columns - HALO, columns) if part == 0 else slice(columns, columns + HALO)
        terms = (fine @ fine, pair @ fine, fine @ pair, pair @ pair)
        owns.append(np.concatenate([term[own, own] for term in terms]))
        sides.append(np.concatenate([np.tile(term[edge, near], (1, 8)) for term in terms]))
    return np.stack(owns), np.stack(sides)


def halves(table):
    high = table.astype(np.float32).astype(BF16)
    low = (table - high.astype(np.float64)).astype(np.float32).astype(BF16)
    return np.stack([high, low], axis=1)


def dot3(left, right):
    (lh, ll), (rh, rl) = left, right
    dot = lambda a, b: jnp.dot(a, b, preferred_element_type=F32)
    return dot(lh, rh) + (dot(lh, rl) + dot(ll, rh))


def block_of(where, k):
    return lax.rem(where[3] + (2, 1, 3, 0)[k], 4)


def product_kernel(where, p_hbm, c_hbm, p_ref, top_ref, bottom_ref, c_ref, sems):
    copies = []
    for k in range(4):
        source, at = pl.ds(8 * block_of(where, k), 8), pl.ds(8 * k, 8)
        copies.append(pltpu.make_async_copy(p_hbm.at[0, source], p_ref.at[at], sems.at[0, k]))
        copies.append(pltpu.make_async_copy(c_hbm.at[source], c_ref.at[at], sems.at[1, k]))
    for copy in copies:
        copy.start()
    for k in range(4):
        copies[2 * k].wait()
        copies[2 * k + 1].wait()
        for g in range(2 * k, 2 * k + 2):
            at = slice(4 * g, 4 * g + 4)
            v = p_ref[at] * c_ref[at]
            top_ref[at] = v[:, :HALO]
            bottom_ref[at] = v[:, HALO:]


def edge_kernel(where, top_ref, bottom_ref, edge_ref, edge_top_ref, edge_bottom_ref):
    gy = where[2]
    lane = lax.broadcasted_iota(jnp.int32, (1, 128), 1)
    near = pl.ds(pl.multiple_of(128 * (1 - gy), 128), 128)
    for r_ref, rows, half_ref in (
        (top_ref, slice(0, HALO), edge_top_ref), (bottom_ref, slice(HALO, 2 * HALO), edge_bottom_ref)
    ):
        edges = jnp.zeros((64, 128), F32)
        for g in range(8):
            v = r_ref[4 * g : 4 * g + 4, :, near].reshape(64, 128)
            if g:
                v = pltpu.roll(v, 16 * g, 1)
            edges = jnp.where(lane // 16 == lax.rem(g + 7 * (1 - gy), 8), v, edges)
        for f in range(4):
            lanes = slice(128 * (f % 2), 128 * (f % 2) + 128)
            edge_ref[f // 2, rows, lanes] = edges[16 * f : 16 * f + 16]
            half_ref[f // 2, :, lanes] = edges[16 * f : 16 * f + 16]


def table_kernel(
    where, edge_ref, patch_ref, right_hbm, eh_ref, el_ref, right_ref, sems
):
    gy = where[2]
    copies = []
    for h in range(2):
        for k in range(4):
            at = pl.ds(256 * k, 256)
            copies.append(pltpu.make_async_copy(right_hbm.at[h, at], right_ref.at[h, at], sems.at[h, k]))
    for copy in copies:
        copy.start()
    narrow = lax.broadcasted_iota(jnp.int32, (1, 128), 1)
    for h, e_ref in ((0, eh_ref), (1, el_ref)):
        for t in range(4):
            rows = edge_ref[gy, h, 16 * t : 16 * t + 16].astype(F32)
            for g in range(8):
                at = 128 * t + 16 * g
                e_ref[at : at + 16] = jnp.where(narrow // 16 == g, rows, jnp.zeros_like(rows)).astype(BF16)
    for copy in copies:
        copy.wait()

    @pl.when(gy == 1)
    def _():
        for h in range(2):
            for t in range(4):
                right_ref[h, 256 * t : 256 * t + 32, :128] = patch_ref[h, 0, t]
                right_ref[h, 256 * t + 224 : 256 * t + 256, 128:] = patch_ref[h, 1, t]


def stack3(parts):
    high, low = split(jnp.concatenate(parts))
    return jnp.concatenate([high, high, low])


def early_kernel(
    where, top_ref, bottom_ref, side_above_ref, side_ref, side_below_ref, left_ref, inner_ref, eh_ref, el_ref, right_ref,
    near_ref, own_ref, uh_ref, ul_ref, pairs_ref,
):
    gy = where[2]
    left, inner = left_ref[where[1]], inner_ref[where[1]]
    lanes = (slice(0, 128), slice(128, 256))
    sides = (side_above_ref, side_ref.at[:, :HALO], side_ref.at[:, HALO:], side_below_ref)
    side = [
        jnp.dot(left, stack3([s[f // 2, :, lanes[f % 2]] for s in sides]), preferred_element_type=F32) for f in range(4)
    ]
    fine = split(jnp.concatenate([jnp.concatenate([u[:32], u[32:64]], axis=1) for u in side]))
    pair = split(jnp.concatenate([jnp.concatenate([u[64:80], u[80:]], axis=1) for u in side]))
    near = dot3(fine, (eh_ref[:256], el_ref[:256]))
    near_pairs = dot3(pair, (eh_ref[256:], el_ref[256:]))
    pairs_ref[pl.ds(0, 64, stride=2), :] = near_pairs
    pairs_ref[pl.ds(1, 64, stride=2), :] = near_pairs
    near = near + pairs_ref[...]
    near_ref[...] = jnp.where(gy == 0, pltpu.roll(near, 112, 1), pltpu.roll(near, 16, 1))
    for f in range(32):
        at = slice(16 * f, 16 * f + 16)
        u = jnp.dot(inner, stack3([top_ref[f], bottom_ref[f]]), preferred_element_type=F32)
        uh_ref[at], ul_ref[at] = split(u)
    own_ref[...] = dot3((uh_ref[...], ul_ref[...]), (right_ref[0, :256], right_ref[1, :256]))


def filter_kernel(
    part, where, p_ref, above_ref, top_ref, bottom_ref, below_ref, left_ref, right_ref, near_ref, own_ref,
    keep_ref, send_ref, fh_ref, fl_ref, mh_ref, ml_ref, ch_ref, cl_ref, outer_ref, middle_ref, pairs_ref,
):
    core, gy, z = where[0], where[2], where[4]
    left = left_ref[where[1]]
    narrow = lax.broadcasted_iota(jnp.int32, (1, 128), 1)
    near = near_ref[...]
    on_left = (narrow < HALO) & (gy == 1)
    on_right = (narrow >= 128 - HALO) & (gy == 0)

    for f in range(16):
        v = stack3([r[16 * part + f] for r in (above_ref, top_ref, bottom_ref, below_ref)])
        u = jnp.dot(left, v, preferred_element_type=F32)
        at = slice(16 * f, 16 * f + 16)
        fh_ref[at], fl_ref[at] = split(u[:16])
        both = slice(32 * f, 32 * f + 32)
        mh_ref[both], ml_ref[both] = split(u[16:48])
        ch_ref[at, :256], cl_ref[at, :256] = split(u[48:64])
        ch_ref[at, 256:], cl_ref[at, 256:] = split(u[64:])

    outer_ref[...] = dot3((fh_ref[...], fl_ref[...]), (right_ref[0, :256], right_ref[1, :256]))
    middle_ref[...] = dot3((mh_ref[...], ml_ref[...]), (right_ref[0, 256:512], right_ref[1, 256:512]))
    pairs = dot3((ch_ref[...], cl_ref[...]), (right_ref[0, 512:], right_ref[1, 512:]))
    for h in range(2):
        for s in range(2):
            pairs_ref[h, pl.ds(s, 256, stride=2), :] = pairs[:, 128 * h : 128 * h + 128]

    for g in range(4):
        at = slice(128 * g, 128 * g + 128)
        shift = (128 - 16 * (4 * part + g)) % 128
        moved = pltpu.roll(near, shift, 1) if shift else near
        zero = jnp.zeros_like(moved)
        low = pairs_ref[0, at] + jnp.where(on_left, moved, zero)
        high = pairs_ref[1, at] + jnp.where(on_right, moved, zero)
        rows = []
        for f in range(4 * g, 4 * g + 4):
            own = own_ref[16 * (16 * part + f) : 16 * (16 * part + f) + 16]
            rows += [outer_ref[16 * f : 16 * f + 8], own, outer_ref[16 * f + 8 : 16 * f + 16]]
        alpha = (jnp.concatenate(rows) + middle_ref[at]) + jnp.concatenate([low, high], axis=1)
        first = 16 * part + 4 * g
        q = p_ref[first : first + 4] * alpha.reshape(4, 32, 256)
        for j in range(2):
            to = 4 * (g // 2) + lax.rem(6 + z - (2 * (g % 2) + j), 4)
            keep_ref[to] = jnp.where(core == 0, q[2 * j], q[2 * j + 1])
            send_ref[to] = jnp.where(core == 0, q[2 * j + 1], q[2 * j])


def call(kernel, outs, *args, hbm=(), scratch=(), cost=0, grant=16):
    args = [pltpu.with_memory_space_constraint(a, pltpu.HBM) if i in hbm else a for i, a in enumerate(args)]
    specs = [pl.BlockSpec(memory_space=pltpu.SMEM)] + [
        pl.BlockSpec(memory_space=pltpu.HBM) if i in hbm else VMEM for i in range(1, len(args))
    ]
    return pl.pallas_call(
        kernel,
        out_shape=[o if isinstance(o, jax.ShapeDtypeStruct) else jax.ShapeDtypeStruct(o, F32) for o in outs],
        in_specs=specs,
        out_specs=[VMEM] * len(outs),
        scratch_shapes=scratch,
        cost_estimate=pl.CostEstimate(flops=cost, bytes_accessed=1 << 20, transcendentals=0),
        compiler_params=pltpu.CompilerParams(vmem_limit_bytes=grant << 20),
    )(*args)


def body(perturbations, control):
    x, z, core, gx, gy = (lax.axis_index(a) for a in ("x", "z", "core", "gx", "gy"))
    where = jnp.stack([core, gx, gy, x, z]).astype(jnp.int32)
    high, low = np.moveaxis(halves(left_table(128, 4)), 1, 0)
    three = lambda rows, cells: jnp.asarray(
        np.concatenate([t[:, rows, cells] for t in (high, low, high)], axis=2)
    )
    whole = slice(0, 64)
    left = three(slice(0, 96), whole)
    inner = three(slice(8, 24), slice(HALO, 48))
    rows = np.r_[0:8, 24:32, 32:96]
    left_rest = three(rows, whole)
    right, edge = (halves(t) for t in right_tables(512, 2))
    blocks = right[1].reshape(2, 4, 256, 256)
    patch = jnp.asarray(np.stack([blocks[:, :, :32, :128], blocks[:, :, 224:, 128:]], axis=1))
    right, edge = jnp.asarray(right[0]), jnp.asarray(edge)
    vmem, sems = pltpu.VMEM, pltpu.SemaphoreType.DMA

    ring = lambda d: [(i, (i + d) % 4) for i in range(4)]
    swap = [(0, 1), (1, 0)]
    near_p, top, bottom = call(
        product_kernel, [(32, 32, 256)] + [(32, 16, 256)] * 2, where, perturbations, control, hbm=(1, 2),
        scratch=[vmem((32, 32, 256), F32), sems((2, 4))],
    )
    above = lax.ppermute(bottom, "gx", ring(1))
    below = lax.ppermute(top, "gx", ring(3))
    edges, edge_top, edge_bottom = call(
        edge_kernel, [(2, 32, 256)] + [(2, 16, 256)] * 2, where, top, bottom
    )
    diagonal = lambda d: [(2 * a + b, 2 * ((a + d) % 4) + 1 - b) for a in range(4) for b in range(2)]
    side_above = lax.ppermute(edge_bottom, ("gx", "gy"), diagonal(1))
    side_below = lax.ppermute(edge_top, ("gx", "gy"), diagonal(3))
    side = lax.ppermute(edges, "gy", swap)
    eh, el, right = call(
        table_kernel, [jax.ShapeDtypeStruct(s, BF16) for s in [(512, 128)] * 2 + [(2, 1024, 256)]],
        where, edge, patch, right, hbm=(3,), scratch=[sems((2, 4))],
    )
    near, own = call(
        early_kernel, [(128, 128), (512, 256)], where, top, bottom, side_above, side, side_below,
        left, inner, eh, el, right, scratch=[vmem((512, 256), BF16)] * 2 + [vmem((128, 128), F32)],
        cost=10**9,
    )
    piece = {}
    for part in range(2):
        keep, give = call(
            functools.partial(filter_kernel, part), [(8, 32, 256)] * 2,
            where, near_p, above, top, bottom, below, left_rest, right, near, own,
            scratch=[vmem((256, 256), BF16)] * 2 + [vmem((512, 256), BF16)] * 2 + [vmem((256, 512), BF16)] * 2
            + [vmem((256, 256), F32), vmem((512, 256), F32), vmem((2, 512, 128), F32)],
            cost=2 * 10**9,
        )
        got = lax.ppermute(give, "core", swap)
        for i in range(2):
            for wave in range(2):
                at = slice(4 * i + 2 * wave, 4 * i + 2 * wave + 2)
                piece[((2, 1), (3, 0))[part][i], wave] = keep[at] + got[at]
    waves = []
    for wave in range(2):
        x2, x1, x3 = (lax.ppermute(piece[d, wave], "x", ring(d)) for d in (2, 1, 3))
        waves.append([(piece[0, wave][i : i + 1] + x2[i : i + 1]) + (x1[i : i + 1] + x3[i : i + 1]) for i in range(2)])
    (far, next_), (stay, last) = waves
    z2, z1, z3 = (lax.ppermute(cell, "z", ring(e)) for e, cell in ((2, far), (1, next_), (3, last)))
    return ((stay + z2) + (z1 + z3)) * (1.0 / 31.0)


def solution(mesh):
    grid = Mesh(mesh.devices.reshape(4, 4, 2, 4, 2), ("x", "z", "core", "gx", "gy"))
    mem = ("x", "z", "core")
    placed = (P(mem, None, "gx", "gy"), P(None, "gx", "gy"))
    return jax.shard_map(body, mesh=grid, in_specs=placed, out_specs=P(mem, "gx", "gy"), check_vma=False)
```
